32 devices in a mesh: dp: 16 (over z, y, x), tensor: 2 (over core).
Axes of the slice: x: 2, y: 2, z: 4, core: 2. Of those that a mesh axis runs over, the one named last changes fastest.
Arguments:
- inputs: bfloat16 [4096, 768], P(('dp', 'tensor')), may hold values from -6 to 6
- neighbours: bfloat16 [96, 128, 768], P(('dp', 'tensor')), may hold values from -6 to 6
- nbr_index: int32 [64, 2], P('dp'), may hold values from 0 to 5
- ln1_gain: float32 [768], P('dp'), may hold values from 0.25 to 1.75
- ln1_bias: float32 [768], P('dp'), may hold values from -1.5 to 1.5
- ln2_gain: float32 [768], P('dp'), may hold values from 0.25 to 1.75
- ln2_bias: float32 [768], P('dp'), may hold values from -1.5 to 1.5
- ln3_gain: float32 [768], P('dp'), may hold values from 0.25 to 1.75
- ln3_bias: float32 [768], P('dp'), may hold values from -1.5 to 1.5
- w_query: float32 [768, 768], P('dp', 'tensor'), may hold values from -0.21875 to 0.21875
- w_key: float32 [768, 768], P('dp', 'tensor'), may hold values from -0.21875 to 0.21875
- w_value: float32 [768, 768], P('dp', 'tensor'), may hold values from -0.21875 to 0.21875
- c_query: float32 [768, 768], P('dp', 'tensor'), may hold values from -0.21875 to 0.21875
- c_key: float32 [768, 768], P('dp', 'tensor'), may hold values from -0.21875 to 0.21875
- c_value: float32 [768, 768], P('dp', 'tensor'), may hold values from -0.21875 to 0.21875
- w_up: float32 [768, 3072], P('dp', 'tensor'), may hold values from -0.21875 to 0.21875
- w_out: float32 [768, 768], P('tensor', 'dp'), may hold values from -0.875 to 0.875
- c_out: float32 [768, 768], P('tensor', 'dp'), may hold values from -0.875 to 0.875
- w_down: float32 [3072, 768], P('tensor', 'dp'), may hold values from -0.109375 to 0.109375
- cotangent: bfloat16 [4096, 768], P(('dp', 'tensor')), may hold values from -6 to 6
Outputs:
- result: bfloat16 [4096, 768], P(('dp', 'tensor'))
- d_inputs: float32 [4096, 768], P(('dp', 'tensor'))
- d_neighbours: float32 [96, 128, 768], P(('dp', 'tensor'))
- d_ln1_gain: float32 [768], P('dp')
- d_ln1_bias: float32 [768], P('dp')
- d_ln2_gain: float32 [768], P('dp')
- d_ln2_bias: float32 [768], P('dp')
- d_ln3_gain: float32 [768], P('dp')
- d_ln3_bias: float32 [768], P('dp')
- d_w_query: float32 [768, 768], P('dp', 'tensor')
- d_w_key: float32 [768, 768], P('dp', 'tensor')
- d_w_value: float32 [768, 768], P('dp', 'tensor')
- d_c_query: float32 [768, 768], P('dp', 'tensor')
- d_c_key: float32 [768, 768], P('dp', 'tensor')
- d_c_value: float32 [768, 768], P('dp', 'tensor')
- d_w_up: float32 [768, 3072], P('dp', 'tensor')
- d_w_out: float32 [768, 768], P('tensor', 'dp')
- d_c_out: float32 [768, 768], P('tensor', 'dp')
- d_w_down: float32 [3072, 768], P('tensor', 'dp')
The draws below stay inside these ranges and needn't reach their ends.
Inputs may be any that keep to these rules, and one draw needn't show every extreme that they name: `nbr_index`: row s * 4 + c names two neighbours (they may coincide) of sequence s, counted from 0 within that sequence's 6.
All inputs are finite; a program needn't handle non-finite values.
Results may differ from the reference program's by a relative error of at most 0.03.
Values may be sent and summed in bfloat16 or wider, within the bound.
No kernel may reach another device: no remote copies, remote signals or barrier semaphores. Data moves between devices by JAX's collectives and lax.ppermute only.
A program may use at most 128 MiB of HBM per device.

```python
import jax
import jax.numpy as jnp
from jax import lax

D = 768
HEADS = 12
HEAD_DIM = 64
FF = 3072
SEQ_LEN = 256
GROUP = 64
NBR_LEN = 128
NBRS = 2
GROUPS = 4
POOL = 6
TOKENS = 4096
POOL_ALL = 96
N_DP = 16


def with_ends(entries, rng, low, largest):
    longest = entries.shape.index(max(entries.shape))
    spots = []
    for shift in (0, 1):
        where = [jax.random.randint(jax.random.fold_in(rng, axis), (), 0, length) for axis, length in enumerate(entries.shape)]
        where[longest] = (where[longest] + shift) % entries.shape[longest]
        spots.append(tuple(where))
    return entries.at[spots[0]].set(low).at[spots[1]].set(largest)


def block_scale(stream_key, extent, split, low, top_value):
    factor_of, own = 1.0, jax.random.fold_in(stream_key, 6)
    for position, parts in split:
        steps = jnp.exp(jax.random.uniform(jax.random.fold_in(own, position), (parts,), jnp.float32, low / len(split), top_value / len(split)))
        factor_of = factor_of * jnp.repeat(steps, extent[position] // parts).reshape([-1 if axis == position else 1 for axis in range(len(extent))])
    return factor_of


def scatter_about(rng, extent, deviation, bound, cuts=(), held_as=jnp.bfloat16):
    array = deviation * jax.random.normal(rng, extent, jnp.float32)
    if cuts:
        array = array * block_scale(rng, extent, cuts, -0.22, 0.18)
    return jnp.clip(array, -bound, bound).astype(held_as)


def setup_inputs(seed: int = 0) -> dict:
    key_of = jax.random.split(jax.random.key(seed), 21)
    inputs = scatter_about(key_of[0], (TOKENS, D), 1.0, 6.0, ((0, 32),))
    neighbours = scatter_about(key_of[1], (POOL_ALL, NBR_LEN, D), 1.0, 6.0, ((0, 32),))
    nbr_index = with_ends(jax.random.randint(key_of[2], (N_DP * GROUPS, NBRS), 0, POOL), jax.random.fold_in(key_of[2], 1), 0, POOL - 1).astype(jnp.int32)
    ln1_gain = jnp.clip(1.0 + 0.15 * jax.random.normal(key_of[3], (D,), jnp.float32), 0.25, 1.75)
    ln1_bias = scatter_about(key_of[4], (D,), 0.3, 1.5, ((0, 16),), jnp.float32)
    ln2_gain = jnp.clip(1.0 + 0.15 * jax.random.normal(key_of[5], (D,), jnp.float32), 0.25, 1.75)
    ln2_bias = scatter_about(key_of[6], (D,), 0.3, 1.5, ((0, 16),), jnp.float32)
    ln3_gain = jnp.clip(1.0 + 0.15 * jax.random.normal(key_of[7], (D,), jnp.float32), 0.25, 1.75)
    ln3_bias = scatter_about(key_of[8], (D,), 0.3, 1.5, ((0, 16),), jnp.float32)
    w_query = scatter_about(key_of[9], (D, D), D ** -0.5, 0.21875, ((0, 16), (1, 2)), jnp.float32)
    w_key = scatter_about(key_of[10], (D, D), D ** -0.5, 0.21875, ((0, 16), (1, 2)), jnp.float32)
    w_value = scatter_about(key_of[11], (D, D), D ** -0.5, 0.21875, ((0, 16), (1, 2)), jnp.float32)
    c_query = scatter_about(key_of[12], (D, D), D ** -0.5, 0.21875, ((0, 16), (1, 2)), jnp.float32)
    c_key = scatter_about(key_of[13], (D, D), D ** -0.5, 0.21875, ((0, 16), (1, 2)), jnp.float32)
    c_value = scatter_about(key_of[14], (D, D), D ** -0.5, 0.21875, ((0, 16), (1, 2)), jnp.float32)
    w_up = scatter_about(key_of[15], (D, FF), D ** -0.5, 0.21875, ((0, 16), (1, 2)), jnp.float32)
    w_out = scatter_about(key_of[16], (D, D), (D // 16) ** -0.5, 0.875, ((0, 2), (1, 16)), jnp.float32)
    c_out = scatter_about(key_of[17], (D, D), (D // 16) ** -0.5, 0.875, ((0, 2), (1, 16)), jnp.float32)
    w_down = scatter_about(key_of[18], (FF, D), FF ** -0.5, 0.109375, ((0, 2), (1, 16)), jnp.float32)
    cotangent = scatter_about(key_of[19], (TOKENS, D), 1.0, 6.0, ((0, 32),))
    return dict(inputs=inputs, neighbours=neighbours, nbr_index=nbr_index, ln1_gain=ln1_gain, ln1_bias=ln1_bias, ln2_gain=ln2_gain, ln2_bias=ln2_bias, ln3_gain=ln3_gain, ln3_bias=ln3_bias, w_query=w_query, w_key=w_key, w_value=w_value, c_query=c_query, c_key=c_key, c_value=c_value, w_up=w_up, w_out=w_out, c_out=c_out, w_down=w_down, cotangent=cotangent)


@jax.custom_vjp
def low(v):
    return lax.optimization_barrier(v.astype(jnp.bfloat16)).astype(jnp.float32)

@jax.custom_vjp
def low_back(v):
    return v

def low_keep(v):
    return (low(v), None)

def low_pass(kept, grad):
    return (grad,)

def back_keep(v):
    return (v, None)

def back_low(kept, grad):
    return (low(grad),)
low.defvjp(low_keep, low_pass)
low_back.defvjp(back_keep, back_low)
HIGHEST_MODE = lax.Precision.HIGHEST
NEG_FILL = -1e+30

def matmul(left, right):
    return jnp.dot(left, right, precision=HIGHEST_MODE, preferred_element_type=jnp.float32)

def layer_norm(stream, gain, shift):
    center = stream - lax.optimization_barrier(jnp.mean(stream, axis=-1, keepdims=True))
    spread = lax.optimization_barrier(jnp.mean(center * center, axis=-1, keepdims=True))
    return center * lax.rsqrt(spread + 1e-05) * gain + shift

def rotate(heads_in, direction):
    count_rows = heads_in.shape[0]
    halfway = heads_in.shape[-1] // 2
    frequency = jnp.power(10000.0, -jnp.arange(halfway, dtype=jnp.float32) / halfway)
    angles = jnp.arange(count_rows, dtype=jnp.float32)[:, None] * frequency[None, :]
    cosine = jnp.cos(angles)[:, None, :]
    sine_part = direction * jnp.sin(angles)[:, None, :]
    leading = heads_in[..., :halfway]
    trailing = heads_in[..., halfway:]
    return jnp.concatenate([leading * cosine - trailing * sine_part, trailing * cosine + leading * sine_part], axis=-1)

def gelu_tanh(pre_act):
    return 0.5 * pre_act * (1.0 + jnp.tanh(0.7978845608028654 * (pre_act + 0.044715 * pre_act * pre_act * pre_act)))

def sequence(stream, pool_rows, chosen, weights):
    gain_one, shift_one, gain_two, shift_two, gain_three, shift_three, query_w, key_w, value_w, cquery_w, ckey_w, cvalue_w, up_w, out_w, cout_w, down_w = weights
    count_rows = stream.shape[0]
    score_scale = HEAD_DIM ** (-0.5)
    normed_one = low(layer_norm(stream, gain_one, shift_one))
    queries = low(rotate(low_back(matmul(normed_one, query_w)).reshape(count_rows, HEADS, HEAD_DIM), 1.0))
    keys_all = low(rotate(low_back(matmul(normed_one, key_w)).reshape(count_rows, HEADS, HEAD_DIM), 1.0))
    values_all = low(low_back(matmul(normed_one, value_w))).reshape(count_rows, HEADS, HEAD_DIM)
    scores = low_back(jnp.einsum('qhd,khd->hqk', queries, keys_all, precision=HIGHEST_MODE) * score_scale)
    causal = jnp.arange(count_rows)[:, None] >= jnp.arange(count_rows)[None, :]
    scores = jnp.where(causal[None], scores, NEG_FILL)
    attend = low(jax.nn.softmax(scores, axis=-1))
    mixture = low(low_back(jnp.einsum('hqk,khd->qhd', attend, values_all, precision=HIGHEST_MODE))).reshape(count_rows, D)
    after_self = stream + low_back(matmul(mixture, out_w))
    normed_two = low(layer_norm(after_self, gain_two, shift_two))
    cqueries = low(low_back(matmul(normed_two, cquery_w))).reshape(GROUPS, GROUP, HEADS, HEAD_DIM)
    pool_flat = pool_rows.reshape(POOL * NBR_LEN, D)
    ckeys = low(low_back(matmul(pool_flat, ckey_w))).reshape(POOL, NBR_LEN, HEADS, HEAD_DIM)
    cvalues = low(low_back(matmul(pool_flat, cvalue_w))).reshape(POOL, NBR_LEN, HEADS, HEAD_DIM)
    chosen_keys = ckeys[chosen].reshape(GROUPS, NBRS * NBR_LEN, HEADS, HEAD_DIM)
    chosen_values = cvalues[chosen].reshape(GROUPS, NBRS * NBR_LEN, HEADS, HEAD_DIM)
    cscores = low_back(jnp.einsum('cqhd,ckhd->chqk', cqueries, chosen_keys, precision=HIGHEST_MODE) * score_scale)
    cattend = low(jax.nn.softmax(cscores, axis=-1))
    cmixture = low(low_back(jnp.einsum('chqk,ckhd->cqhd', cattend, chosen_values, precision=HIGHEST_MODE))).reshape(count_rows, D)
    after_cross = after_self + low_back(matmul(cmixture, cout_w))
    normed_three = low(layer_norm(after_cross, gain_three, shift_three))
    hidden = low(gelu_tanh(low_back(matmul(normed_three, up_w))))
    return after_cross + low_back(matmul(hidden, down_w))

def reference(inputs, neighbours, nbr_index, ln1_gain, ln1_bias, ln2_gain, ln2_bias, ln3_gain, ln3_bias, w_query, w_key, w_value, c_query, c_key, c_value, w_up, w_out, c_out, w_down, cotangent):
    states = inputs.astype(jnp.float32).reshape(N_DP, SEQ_LEN, D)
    pools = neighbours.astype(jnp.float32).reshape(N_DP, POOL, NBR_LEN, D)
    indices = nbr_index.reshape(N_DP, GROUPS, NBRS).astype(jnp.int32)
    masters = (ln1_gain, ln1_bias, ln2_gain, ln2_bias, ln3_gain, ln3_bias, w_query, w_key, w_value, c_query, c_key, c_value, w_up, w_out, c_out, w_down)

    def forward(states_in, pools_in, masters_in):
        lowered = tuple((low(master) for master in masters_in))
        checked = jax.checkpoint(sequence)

        def advance(carried, element):
            return (carried, checked(element[0], element[1], element[2], lowered))
        unused, outcome = lax.scan(advance, jnp.zeros((), jnp.float32), (states_in, pools_in, indices))
        return outcome
    outcome, pullback = jax.vjp(forward, states, pools, masters)
    grad_states, grad_pools, grad_masters = pullback(cotangent.astype(jnp.float32).reshape(N_DP, SEQ_LEN, D))
    return (outcome.reshape(TOKENS, D).astype(jnp.bfloat16), grad_states.reshape(TOKENS, D), grad_pools.reshape(POOL_ALL, NBR_LEN, D), grad_masters[0], grad_masters[1], grad_masters[2], grad_masters[3], grad_masters[4], grad_masters[5], grad_masters[6], grad_masters[7], grad_masters[8], grad_masters[9], grad_masters[10], grad_masters[11], grad_masters[12], grad_masters[13], grad_masters[14], grad_masters[15])
```

```python
import jax
import jax.numpy as jnp
from jax import lax
from jax.sharding import PartitionSpec as P

D = 768
HEAD_DIM = 64
GROUP = 64
NBR_LEN = 128
NBRS = 2
LANES = 128


HIGHEST_MODE = lax.Precision.HIGHEST
NEG_FILL = -1e30


def product(left, right):
    return jnp.dot(left, right, preferred_element_type=jnp.float32)


def outer_sum(left, right):
    return lax.dot_general(
        left, right, (((0,), (0,)), ((), ())), preferred_element_type=jnp.float32
    )


def back_product(left, right):
    return lax.dot_general(
        left, right, (((1,), (1,)), ((), ())), preferred_element_type=jnp.float32
    )


def split_columns(array, widths):
    parts, start = [], 0
    for width in widths:
        parts.append(array[:, start : start + width])
        start += width
    return parts


def layer_norm(stream, gain, shift):
    center = stream - jnp.mean(stream, axis=-1, keepdims=True)
    spread = jnp.mean(center * center, axis=-1, keepdims=True)
    return center * lax.rsqrt(spread + 1e-05) * gain + shift


def rotate(heads_in, direction):
    count_rows = heads_in.shape[0]
    halfway = heads_in.shape[-1] // 2
    frequency = jnp.power(10000.0, -jnp.arange(halfway, dtype=jnp.float32) / halfway)
    angles = jnp.arange(count_rows, dtype=jnp.float32)[:, None] * frequency[None, :]
    cosine = jnp.cos(angles)[:, None, :]
    sine_part = direction * jnp.sin(angles)[:, None, :]
    leading = heads_in[..., :halfway]
    trailing = heads_in[..., halfway:]
    return jnp.concatenate(
        [leading * cosine - trailing * sine_part, trailing * cosine + leading * sine_part], axis=-1
    )


def gelu_tanh(pre_act):
    return (
        0.5
        * pre_act
        * (1.0 + jnp.tanh(0.7978845608028654 * (pre_act + 0.044715 * pre_act * pre_act * pre_act)))
    )


def spread_rows(normed):
    return lax.all_gather(normed.astype(jnp.bfloat16), "tensor", axis=0, tiled=True)


def gather_grad(grad_in):
    return lax.all_gather(grad_in.astype(jnp.bfloat16), "tensor", axis=0, tiled=True)


def branch_total(partial_out):
    return lax.psum_scatter(
        partial_out.astype(jnp.bfloat16), "tensor", scatter_dimension=0, tiled=True
    ).astype(jnp.float32)


def grad_total(partial_grad):
    return lax.psum_scatter(
        partial_grad.astype(jnp.bfloat16), "tensor", scatter_dimension=0, tiled=True
    ).astype(jnp.float32)


def block_bounds(count_rows):
    block_rows = min(512, count_rows)
    return [(0, min(block_rows, count_rows))]


def masked_scores(block_queries, keys_part, first_row, score_scale):
    block_rows = block_queries.shape[0]
    scores = (
        jnp.einsum("qhd,khd->hqk", block_queries, keys_part, preferred_element_type=jnp.float32)
        * score_scale
    )
    query_pos = first_row + jnp.arange(block_rows, dtype=jnp.int32)
    key_pos = jnp.arange(keys_part.shape[0], dtype=jnp.int32)
    allowed = query_pos[:, None] >= key_pos[None, :]
    return jnp.where(allowed[None], scores, NEG_FILL)


def causal_forward(queries, keys_all, values_all, score_scale):
    count_rows, heads_local, head_width = queries.shape
    mixtures = []
    logsums = []
    for start, stop in block_bounds(count_rows):
        scores = masked_scores(queries, keys_all, start, score_scale)
        highest = jnp.max(scores, axis=-1, keepdims=True)
        raised = jnp.exp(scores - highest)
        totals = jnp.sum(raised, axis=-1, keepdims=True)
        attend = (raised / totals).astype(jnp.bfloat16)
        mixture = jnp.einsum("hqk,khd->qhd", attend, values_all, preferred_element_type=jnp.float32)
        mixtures.append(mixture.astype(jnp.bfloat16))
        logsums.append(highest + jnp.log(totals))
    mixture = mixtures[0]
    return (mixture.reshape(count_rows, heads_local * head_width), logsums)


def causal_backward(queries, keys_all, values_all, logsums, grad_mixture, score_scale):
    count_rows, heads_local, head_width = queries.shape
    grad_keys = jnp.zeros(keys_all.shape, jnp.float32)
    grad_values = jnp.zeros(keys_all.shape, jnp.float32)
    grad_pieces = []
    for turn, (start, stop) in enumerate(block_bounds(count_rows)):
        scores = masked_scores(queries, keys_all, start, score_scale)
        attend = jnp.exp(scores - logsums[turn])
        attend_low = attend.astype(jnp.bfloat16)
        grad_values = grad_values.at[:stop].add(
            jnp.einsum("hqk,qhd->khd", attend_low, grad_mixture, preferred_element_type=jnp.float32)
        )
        grad_attend = jnp.einsum(
            "qhd,khd->hqk", grad_mixture, values_all, preferred_element_type=jnp.float32
        )
        inner = jnp.sum(attend * grad_attend, axis=-1, keepdims=True)
        grad_scores = (attend * (grad_attend - inner)).astype(jnp.bfloat16)
        grad_pieces.append(
            jnp.einsum("hqk,khd->qhd", grad_scores, keys_all, preferred_element_type=jnp.float32)
            * score_scale
        )
        grad_keys = grad_keys.at[:stop].add(
            jnp.einsum("hqk,qhd->khd", grad_scores, queries, preferred_element_type=jnp.float32)
            * score_scale
        )
    grad_queries = grad_pieces[0]
    return (grad_queries, grad_keys, grad_values)


def cross_forward(cqueries, ckeys, cvalues, score_scale):
    scores = (
        jnp.einsum("cqhd,ckhd->chqk", cqueries, ckeys, preferred_element_type=jnp.float32)
        * score_scale
    )
    highest = jnp.max(scores, axis=-1, keepdims=True)
    raised = jnp.exp(scores - highest)
    totals = jnp.sum(raised, axis=-1, keepdims=True)
    attend = (raised / totals).astype(jnp.bfloat16)
    mixture = jnp.einsum("chqk,ckhd->cqhd", attend, cvalues, preferred_element_type=jnp.float32)
    return (mixture.astype(jnp.bfloat16), highest + jnp.log(totals))


def cross_backward(cqueries, ckeys, cvalues, logsum, grad_mixture, score_scale):
    scores = (
        jnp.einsum("cqhd,ckhd->chqk", cqueries, ckeys, preferred_element_type=jnp.float32)
        * score_scale
    )
    attend = jnp.exp(scores - logsum)
    attend_low = attend.astype(jnp.bfloat16)
    grad_values = jnp.einsum(
        "chqk,cqhd->ckhd", attend_low, grad_mixture, preferred_element_type=jnp.float32
    )
    grad_attend = jnp.einsum(
        "cqhd,ckhd->chqk", grad_mixture, cvalues, preferred_element_type=jnp.float32
    )
    inner = jnp.sum(attend * grad_attend, axis=-1, keepdims=True)
    grad_scores = (attend * (grad_attend - inner)).astype(jnp.bfloat16)
    grad_queries = (
        jnp.einsum("chqk,ckhd->cqhd", grad_scores, ckeys, preferred_element_type=jnp.float32)
        * score_scale
    )
    grad_keys = (
        jnp.einsum("chqk,cqhd->ckhd", grad_scores, cqueries, preferred_element_type=jnp.float32)
        * score_scale
    )
    return (grad_queries, grad_keys, grad_values)


def on_device(
    inputs,
    neighbours,
    nbr_index,
    ln1_gain,
    ln1_bias,
    ln2_gain,
    ln2_bias,
    ln3_gain,
    ln3_bias,
    w_query,
    w_key,
    w_value,
    c_query,
    c_key,
    c_value,
    w_up,
    w_out,
    c_out,
    w_down,
    cotangent,
):
    norms = jnp.stack([ln1_gain, ln1_bias, ln2_gain, ln2_bias, ln3_gain, ln3_bias], axis=1)
    norms = jnp.pad(norms, ((0, 0), (0, LANES - norms.shape[1])))
    width = w_query.shape[1]
    hidden = w_up.shape[1]
    columns = [norms, w_query, w_key, w_value, w_out.T, c_query, c_key, c_value, c_out.T, w_up, w_down.T]
    widths = [LANES] + [width] * 8 + [hidden] * 2
    first = 5
    packed = [jnp.concatenate([col.astype(jnp.bfloat16) for col in part], axis=1) for part in (columns[:first], columns[first:])]
    full = [lax.all_gather(part, "dp", axis=0, tiled=True) for part in packed]
    norms_w, query_w, key_w, value_w, out_t = split_columns(full[0], widths[:first])
    cquery_w, ckey_w, cvalue_w, cout_t, up_w, down_t = split_columns(full[1], widths[first:])
    out_w, cout_w, down_w = out_t.T, cout_t.T, down_t.T
    gain_one, shift_one, gain_two, shift_two, gain_three, shift_three = [norms_w[:, i] for i in range(6)]
    score_scale = HEAD_DIM ** (-0.5)
    stream = inputs.astype(jnp.float32)
    normed_one, norm_back_one = jax.vjp(
        layer_norm, stream, gain_one.astype(jnp.float32), shift_one.astype(jnp.float32)
    )
    self_rows = spread_rows(normed_one)
    seq_rows = self_rows.shape[0]
    heads_local = query_w.shape[1] // HEAD_DIM
    queries = rotate(
        product(self_rows, query_w).reshape(seq_rows, heads_local, HEAD_DIM), 1.0
    ).astype(jnp.bfloat16)
    keys_all = rotate(
        product(self_rows, key_w).reshape(seq_rows, heads_local, HEAD_DIM), 1.0
    ).astype(jnp.bfloat16)
    values_all = (
        product(self_rows, value_w).astype(jnp.bfloat16).reshape(seq_rows, heads_local, HEAD_DIM)
    )
    mixture, logsums = causal_forward(queries, keys_all, values_all, score_scale)
    after_self = stream + branch_total(product(mixture, out_w))
    normed_two, norm_back_two = jax.vjp(
        layer_norm, after_self, gain_two.astype(jnp.float32), shift_two.astype(jnp.float32)
    )
    cross_rows = spread_rows(normed_two)
    group_count = seq_rows // GROUP
    cqueries = (
        product(cross_rows, cquery_w)
        .astype(jnp.bfloat16)
        .reshape(group_count, GROUP, heads_local, HEAD_DIM)
    )
    pool_all = lax.all_gather(neighbours, "tensor", axis=0, tiled=True)
    pool_count = pool_all.shape[0]
    pool_flat = pool_all.reshape(pool_count * NBR_LEN, D)
    ckeys = product(pool_flat, ckey_w).astype(jnp.bfloat16)
    cvalues = product(pool_flat, cvalue_w).astype(jnp.bfloat16)
    chosen = nbr_index.reshape(-1)
    chosen_keys = ckeys.reshape(pool_count, -1)[chosen].reshape(
        group_count, NBRS * NBR_LEN, heads_local, HEAD_DIM
    )
    chosen_values = cvalues.reshape(pool_count, -1)[chosen].reshape(
        group_count, NBRS * NBR_LEN, heads_local, HEAD_DIM
    )
    cmixture, clogsum = cross_forward(cqueries, chosen_keys, chosen_values, score_scale)
    cmixture = cmixture.reshape(seq_rows, heads_local * HEAD_DIM)
    after_cross = after_self + branch_total(product(cmixture, cout_w))
    normed_three, norm_back_three = jax.vjp(
        layer_norm, after_cross, gain_three.astype(jnp.float32), shift_three.astype(jnp.float32)
    )
    mlp_rows = spread_rows(normed_three)
    pre_act = product(mlp_rows, up_w)
    activated, gelu_back = jax.vjp(gelu_tanh, pre_act)
    act_low = activated.astype(jnp.bfloat16)
    result = after_cross + branch_total(product(act_low, down_w))
    grad_out = cotangent.astype(jnp.float32)
    grad_full = gather_grad(grad_out)
    grad_down = outer_sum(grad_full, act_low)
    grad_act = back_product(grad_full, down_w)
    grad_pre = gelu_back(grad_act)[0].astype(jnp.bfloat16)
    grad_up = outer_sum(mlp_rows, grad_pre)
    grad_stream, grad_gain_three, grad_shift_three = norm_back_three(
        grad_total(back_product(grad_pre, up_w))
    )
    grad_cross_out = grad_out + grad_stream
    grad_full = gather_grad(grad_cross_out)
    grad_cout = outer_sum(grad_full, cmixture)
    grad_cmix = (
        back_product(grad_full, cout_w)
        .astype(jnp.bfloat16)
        .reshape(group_count, GROUP, heads_local, HEAD_DIM)
    )
    grad_cq, grad_ck, grad_cv = cross_backward(
        cqueries, chosen_keys, chosen_values, clogsum, grad_cmix, score_scale
    )
    grad_cq_low = grad_cq.reshape(seq_rows, heads_local * HEAD_DIM).astype(jnp.bfloat16)
    grad_cquery = outer_sum(cross_rows, grad_cq_low)
    picks = (jnp.arange(pool_count, dtype=jnp.int32)[:, None] == chosen[None, :]).astype(
        jnp.float32
    )
    pool_dkey = (
        jnp.dot(
            picks,
            grad_ck.reshape(group_count * NBRS, -1),
            precision=HIGHEST_MODE,
            preferred_element_type=jnp.float32,
        )
        .reshape(pool_count * NBR_LEN, -1)
        .astype(jnp.bfloat16)
    )
    pool_dvalue = (
        jnp.dot(
            picks,
            grad_cv.reshape(group_count * NBRS, -1),
            precision=HIGHEST_MODE,
            preferred_element_type=jnp.float32,
        )
        .reshape(pool_count * NBR_LEN, -1)
        .astype(jnp.bfloat16)
    )
    grad_ckey = outer_sum(pool_flat, pool_dkey)
    grad_cvalue = outer_sum(pool_flat, pool_dvalue)
    pool_partial = back_product(pool_dkey, ckey_w) + back_product(pool_dvalue, cvalue_w)
    grad_pool = lax.psum_scatter(
        pool_partial.reshape(pool_count, NBR_LEN, D).astype(jnp.bfloat16),
        "tensor",
        scatter_dimension=0,
        tiled=True,
    ).astype(jnp.float32)
    grad_stream, grad_gain_two, grad_shift_two = norm_back_two(
        grad_total(back_product(grad_cq_low, cquery_w))
    )
    grad_self_out = grad_cross_out + grad_stream
    grad_full = gather_grad(grad_self_out)
    grad_wout = outer_sum(grad_full, mixture)
    grad_mix = (
        back_product(grad_full, out_w).astype(jnp.bfloat16).reshape(seq_rows, heads_local, HEAD_DIM)
    )
    grad_queries, grad_keys, grad_values = causal_backward(
        queries, keys_all, values_all, logsums, grad_mix, score_scale
    )
    query_low = rotate(grad_queries, -1.0).reshape(seq_rows, -1).astype(jnp.bfloat16)
    key_low = rotate(grad_keys, -1.0).reshape(seq_rows, -1).astype(jnp.bfloat16)
    value_low = grad_values.reshape(seq_rows, -1).astype(jnp.bfloat16)
    grad_query = outer_sum(self_rows, query_low)
    grad_key = outer_sum(self_rows, key_low)
    grad_value = outer_sum(self_rows, value_low)
    partial_grad = (
        back_product(query_low, query_w)
        + back_product(key_low, key_w)
        + back_product(value_low, value_w)
    )
    grad_stream, grad_gain_one, grad_shift_one = norm_back_one(grad_total(partial_grad))
    grad_input = grad_self_out + grad_stream
    norm_sums = lax.psum(
        (
            grad_gain_one,
            grad_shift_one,
            grad_gain_two,
            grad_shift_two,
            grad_gain_three,
            grad_shift_three,
        ),
        "tensor",
    )
    norm_grads = jnp.pad(jnp.stack(norm_sums, axis=1), ((0, 0), (0, LANES - 6)))
    grads = jnp.concatenate(
        [grad.astype(jnp.bfloat16) for grad in (norm_grads, grad_query, grad_key, grad_value, grad_wout, grad_cquery, grad_ckey, grad_cvalue, grad_cout, grad_up, grad_down)],
        axis=1,
    )
    total = lax.psum_scatter(grads, "dp", scatter_dimension=0, tiled=True).astype(jnp.float32)
    parts = split_columns(total, widths)
    norm_part, part_q, part_k, part_v, part_o, part_cq, part_ck, part_cv, part_co, part_up, part_down = parts
    summed = tuple(norm_part[:, i] for i in range(6)) + (part_q, part_k, part_v, part_cq, part_ck, part_cv, part_up, part_o.T, part_co.T, part_down.T)
    return (
        result.astype(jnp.bfloat16),
        grad_input,
        grad_pool,
        summed[0],
        summed[1],
        summed[2],
        summed[3],
        summed[4],
        summed[5],
        summed[6],
        summed[7],
        summed[8],
        summed[9],
        summed[10],
        summed[11],
        summed[12],
        summed[13],
        summed[14],
        summed[15],
    )


def solution(mesh):
    return jax.shard_map(
        on_device,
        mesh=mesh,
        in_specs=(
            P(("dp", "tensor"), None),
            P(("dp", "tensor"), None, None),
            P("dp", None),
            P("dp"),
            P("dp"),
            P("dp"),
            P("dp"),
            P("dp"),
            P("dp"),
            P("dp", "tensor"),
            P("dp", "tensor"),
            P("dp", "tensor"),
            P("dp", "tensor"),
            P("dp", "tensor"),
            P("dp", "tensor"),
            P("dp", "tensor"),
            P("tensor", "dp"),
            P("tensor", "dp"),
            P("tensor", "dp"),
            P(("dp", "tensor"), None),
        ),
        out_specs=(
            P(("dp", "tensor"), None),
            P(("dp", "tensor"), None),
            P(("dp", "tensor"), None, None),
            P("dp"),
            P("dp"),
            P("dp"),
            P("dp"),
            P("dp"),
            P("dp"),
            P("dp", "tensor"),
            P("dp", "tensor"),
            P("dp", "tensor"),
            P("dp", "tensor"),
            P("dp", "tensor"),
            P("dp", "tensor"),
            P("dp", "tensor"),
            P("tensor", "dp"),
            P("tensor", "dp"),
            P("tensor", "dp"),
        ),
        check_vma=False,
    )
```

```python
import functools

import jax
import jax.numpy as jnp
import numpy as np
from jax import lax
from jax.experimental import pallas as pl
from jax.experimental.pallas import tpu as pltpu
from jax.sharding import PartitionSpec as P

HEAD_DIM = 64
GROUP = 64
NBR_LEN = 128
NBRS = 2
LANES = 128
NORMS = 6
NEG_FILL = -1e30
EPSILON = 1e-05
GELU_A = 0.7978845608028654
GELU_B = 0.044715
PLANES = 4
VMEM_BYTES = 40 * 2**20

bf16 = jnp.bfloat16
f32 = jnp.float32


def mm(left, right):
    return jnp.dot(left, right, preferred_element_type=f32)


def mm_nt(left, right):
    return lax.dot_general(left, right, (((1,), (1,)), ((), ())), preferred_element_type=f32)


def mm_tn(left, right):
    return lax.dot_general(left, right, (((0,), (0,)), ((), ())), preferred_element_type=f32)


def wide(array):
    return array.astype(f32)


def grid_perms(count):
    x_swap = [(i, i ^ 1) for i in range(count)]
    y_swap = [(i, i ^ 2) for i in range(count)]
    z_pair = [(i, i ^ 4) for i in range(count)]
    z_mid = [(i, 12 - 4 * (i // 4) + i % 4) for i in range(4, 12)]
    z_out = [(i, i ^ 4) for i in range(4, 12)]
    z_in = [(i ^ 4, i) for i in range(4, 12)]
    return x_swap, y_swap, z_pair, z_mid, z_out, z_in


def block_tables(count):
    table = np.zeros((count, 2 * count), np.int32)
    for device in range(count):
        z, y, x = device // 4, device // 2 % 2, device % 2
        inner = 1 if z in (1, 2) else 0
        slot = 0
        for plane in range(PLANES):
            column = 2 * (y ^ (plane >> 1)) + (x ^ (plane & 1))
            for half in range(2):
                for j in range(2):
                    table[device, slot] = 4 * (z ^ (2 * half + (j ^ (half & inner)))) + column
                    table[device, count + slot] = 4 * (z ^ (2 * half + j)) + column
                    slot += 1
    return table


def pieces_ok(count, rows):
    return count == 16 and rows % 16 == 0


def gather_pieces(shard, count):
    if not pieces_ok(count, shard.shape[0]):
        return (lax.all_gather(shard, "dp", axis=0, tiled=True),)
    x_swap, y_swap, z_pair, z_mid, z_out, _ = grid_perms(count)
    send = functools.partial(lax.ppermute, axis_name="dp")
    buddy = send(shard, perm=z_pair)
    first = jnp.concatenate([shard, buddy], axis=0)
    middle = send(first, perm=z_mid)
    outer = send(middle, perm=z_out)
    is_inner = (lax.axis_index("dp") // 4) % 3 != 0
    second = jnp.where(is_inner, middle, outer)
    x_first, y_first = send(first, perm=x_swap), send(first, perm=y_swap)
    d_first = send(y_first, perm=x_swap)
    x_second, y_second = send(second, perm=x_swap), send(second, perm=y_swap)
    d_second = send(x_second, perm=y_swap)
    return (first, second, x_first, x_second, y_first, y_second, d_first, d_second)


def swap_blocks(array):
    half = array.shape[0] // 2
    return jnp.concatenate([array[half:], array[:half]], axis=0)


def reduce_pieces(pieces, count):
    if len(pieces) == 1:
        return wide(lax.psum_scatter(pieces[0], "dp", scatter_dimension=0, tiled=True))
    first, second, x_first, x_second, y_first, y_second, d_first, d_second = pieces
    x_swap, y_swap, z_pair, z_mid, _, z_in = grid_perms(count)
    send = functools.partial(lax.ppermute, axis_name="dp")
    from_x = send(d_first, perm=x_swap)
    from_y = send(d_second, perm=y_swap)
    got_x_first = send(x_first, perm=x_swap)
    got_y_second = send(y_second, perm=y_swap)
    got_x_second = send((wide(x_second) + wide(from_y)).astype(bf16), perm=x_swap)
    got_y_first = send((wide(y_first) + wide(from_x)).astype(bf16), perm=y_swap)
    other = (wide(second) + wide(got_x_second) + wide(got_y_second)).astype(bf16)
    own = wide(first) + wide(got_x_first) + wide(got_y_first)
    from_out = send(other, perm=z_in)
    other = (wide(other) + wide(swap_blocks(from_out))).astype(bf16)
    from_mid = send(other, perm=z_mid)
    own = own + wide(swap_blocks(from_mid))
    half = own.shape[0] // 2
    from_pair = send(own[half:].astype(bf16), perm=z_pair)
    return own[:half] + wide(from_pair)


def sum_small(array, count):
    step = 1
    while step < count:
        array = array + lax.ppermute(array, "dp", [(i, i ^ step) for i in range(count)])
        step *= 2
    return array


def swap_cores(array):
    return lax.ppermute(array, "tensor", [(0, 1), (1, 0)])


def join_cores(array):
    other = swap_cores(array)
    low = lax.axis_index("tensor") == 0
    return jnp.concatenate(
        [jnp.where(low, array, other), jnp.where(low, other, array)], axis=0
    )


def fetch(table, pieces, target, sems, columns, sem_from=0):
    start, size = columns
    copies = []
    if len(pieces) == 1:
        copies.append(
            pltpu.make_async_copy(pieces[0].at[:, pl.ds(start, size)], target, sems.at[sem_from])
        )
    else:
        rows = pieces[0].shape[0] // 2
        for slot in range(2 * len(pieces)):
            first = pl.multiple_of(table[slot] * rows, 16)
            copies.append(
                pltpu.make_async_copy(
                    pieces[slot // 2].at[pl.ds(slot % 2 * rows, rows), pl.ds(start, size)],
                    target.at[pl.ds(first, rows), :],
                    sems.at[sem_from + slot],
                )
            )
    for copy in copies:
        copy.start()
    return copies


def put(table, source, pieces, sems, columns, sem_from=0):
    start, size = columns
    copies = []
    if len(pieces) == 1:
        copies.append(
            pltpu.make_async_copy(source, pieces[0].at[:, pl.ds(start, size)], sems.at[sem_from])
        )
    else:
        rows = pieces[0].shape[0] // 2
        for slot in range(2 * len(pieces)):
            first = pl.multiple_of(table[2 * len(pieces) + slot] * rows, 16)
            copies.append(
                pltpu.make_async_copy(
                    source.at[pl.ds(first, rows), :],
                    pieces[slot // 2].at[pl.ds(slot % 2 * rows, rows), pl.ds(start, size)],
                    sems.at[sem_from + slot],
                )
            )
    for copy in copies:
        copy.start()
    return copies


def finish(copies):
    for copy in copies:
        copy.wait()


def norm_parts(stream):
    center = stream - jnp.mean(stream, axis=-1, keepdims=True)
    spread = jnp.mean(center * center, axis=-1, keepdims=True)
    scale = lax.rsqrt(spread + EPSILON)
    return center * scale, scale


def norm_back(grad, normal, scale, gain):
    inner = grad * gain
    return scale * (
        inner
        - jnp.mean(inner, axis=-1, keepdims=True)
        - normal * jnp.mean(inner * normal, axis=-1, keepdims=True)
    )


def turn(pair, cosine, sine):
    lane = lax.broadcasted_iota(jnp.int32, pair.shape, 1)
    low_half = lane % HEAD_DIM < HEAD_DIM // 2
    partner = jnp.where(
        low_half,
        pltpu.roll(pair, LANES - HEAD_DIM // 2, 1),
        pltpu.roll(pair, HEAD_DIM // 2, 1),
    )
    return pair * cosine + partner * sine


def stack_heads(pair):
    lane = lax.broadcasted_iota(jnp.int32, pair.shape, 1)
    zero = jnp.zeros_like(pair)
    return jnp.concatenate(
        [jnp.where(lane < HEAD_DIM, pair, zero), jnp.where(lane < HEAD_DIM, zero, pair)], axis=0
    )


def merge_heads(stacked):
    rows = stacked.shape[0] // 2
    lane = lax.broadcasted_iota(jnp.int32, (rows, stacked.shape[1]), 1)
    return jnp.where(lane < HEAD_DIM, stacked[:rows], stacked[rows:])


def softmax_low(scores):
    raised = jnp.exp(scores - jnp.max(scores, axis=-1, keepdims=True))
    return (raised * (1.0 / jnp.sum(raised, axis=-1, keepdims=True))).astype(bf16)


def pairs_of(width):
    return [(pair, slice(pair * LANES, (pair + 1) * LANES)) for pair in range(width // LANES)]


SCALE = HEAD_DIM ** (-0.5)


def self_forward(count, table, x_ref, cos_ref, sin_ref, *refs):
    pieces, refs = refs[:count], refs[count:]
    part, h_out, q_out, k_out, v_out, p_out, o_out, norms_out, weights, sems = refs
    width = q_out.shape[1]
    copies = fetch(table, pieces, weights, sems, (0, weights.shape[1]))
    normal, _ = norm_parts(wide(x_ref[...]))
    finish(copies)
    rows = wide(weights[:, :LANES]).T[:8]
    norms_out[...] = rows
    hidden = (normal * rows[0:1] + rows[1:2]).astype(bf16)
    h_out[...] = hidden
    mixed = mm(hidden, weights[:, LANES : LANES + 3 * width])
    cosine, sine = cos_ref[...], sin_ref[...]
    count_rows = hidden.shape[0]
    query_pos = lax.broadcasted_iota(jnp.int32, (2 * count_rows, count_rows), 0) % count_rows
    allowed = query_pos >= lax.broadcasted_iota(jnp.int32, (2 * count_rows, count_rows), 1)
    for pair, lanes in pairs_of(width):
        queries = turn(mixed[:, lanes], cosine, sine).astype(bf16)
        keys = turn(mixed[:, width + pair * LANES : width + (pair + 1) * LANES], cosine, sine).astype(bf16)
        values = mixed[:, 2 * width + pair * LANES : 2 * width + (pair + 1) * LANES].astype(bf16)
        q_out[:, lanes] = queries
        k_out[:, lanes] = keys
        v_out[:, lanes] = values
        scores = jnp.where(allowed, mm_nt(stack_heads(queries), keys) * SCALE, NEG_FILL)
        attend = softmax_low(scores)
        p_out[pair] = attend
        o_out[:, lanes] = merge_heads(mm(attend, values)).astype(bf16)
    part[...] = mm_nt(o_out[...], weights[:, LANES + 3 * width :]).astype(bf16)


def pool_forward(count, table, pool_ref, *refs):
    pieces, refs = refs[:count], refs[count:]
    k_out, v_out, weights, sems = refs
    width = k_out.shape[1]
    finish(fetch(table, pieces, weights, sems, (width, 2 * width)))
    mixed = mm(pool_ref[...], weights[...])
    k_out[...] = mixed[:, :width].astype(bf16)
    v_out[...] = mixed[:, width:].astype(bf16)


def chosen_rows(chosen, block, ref, lanes):
    return jnp.concatenate(
        [
            ref[pl.ds(pl.multiple_of(chosen[NBRS * block + j] * NBR_LEN, NBR_LEN), NBR_LEN), lanes]
            for j in range(NBRS)
        ],
        axis=0,
    )


def cross_forward(count, table, chosen, x_ref, own_ref, got_ref, norms, k_ref, v_ref, *refs):
    pieces, refs = refs[:count], refs[count:]
    part, x_out, h_out, q_out, p_out, o_out, in_w, out_w, sems, sems_out = refs
    width = q_out.shape[1]
    copies = fetch(table, pieces, in_w, sems, (0, width))
    copies_out = fetch(table, pieces, out_w, sems_out, (3 * width, width))
    stream = wide(x_ref[...]) + (wide(own_ref[...]) + wide(got_ref[...]))
    x_out[...] = stream
    normal, _ = norm_parts(stream)
    hidden = (normal * norms[2:3] + norms[3:4]).astype(bf16)
    h_out[...] = hidden
    finish(copies)
    queries = mm(hidden, in_w[...]).astype(bf16)
    q_out[...] = queries
    pair_count = width // LANES
    for block in range(queries.shape[0] // GROUP):
        rows = slice(block * GROUP, (block + 1) * GROUP)
        for pair, lanes in pairs_of(width):
            keys = chosen_rows(chosen, block, k_ref, lanes)
            values = chosen_rows(chosen, block, v_ref, lanes)
            attend = softmax_low(mm_nt(stack_heads(queries[rows, lanes]), keys) * SCALE)
            p_out[block * pair_count + pair] = attend
            o_out[rows, lanes] = merge_heads(mm(attend, values)).astype(bf16)
    finish(copies_out)
    part[...] = mm_nt(o_out[...], out_w[...]).astype(bf16)


def feed_forward(count, slices, table, x_ref, own_ref, got_ref, norms, g_ref, *refs):
    pieces, refs = refs[:count], refs[count:]
    part, x_out, dh_out = refs[:3]
    grads, refs = refs[3 : 3 + count], refs[3 + count :]
    up_w, down_w, up_g, down_g, sems, sems_out = refs
    total = up_w.shape[0] * up_w.shape[2]
    size = total // slices
    block_count = max(1, 2 * count) if count > 1 else 1
    copies = []
    for turn_of in range(slices):
        copies.append(
            fetch(table, pieces, up_w.at[turn_of], sems, (turn_of * size, size), 2 * turn_of * block_count)
            + fetch(table, pieces, down_w.at[turn_of], sems, (total + turn_of * size, size), (2 * turn_of + 1) * block_count)
        )
    stream = wide(x_ref[...]) + (wide(own_ref[...]) + wide(got_ref[...]))
    x_out[...] = stream
    normal, _ = norm_parts(stream)
    hidden = (normal * norms[4:5] + norms[5:6]).astype(bf16)
    grad = g_ref[...]
    hidden_t, grad_t = hidden.T, grad.T
    out = jnp.zeros(stream.shape, f32)
    back = jnp.zeros(stream.shape, f32)
    sent = []
    for turn_of in range(slices):
        finish(copies[turn_of])
        pre = mm(hidden, up_w[turn_of])
        grad_act = mm(grad, down_w[turn_of])
        square = pre * pre
        bend = jnp.tanh(GELU_A * (pre + GELU_B * square * pre))
        gate = 0.5 * (1.0 + bend)
        act = (pre * gate).astype(bf16)
        slope = gate + 0.5 * pre * (1.0 - bend * bend) * (GELU_A * (1.0 + 3.0 * GELU_B * square))
        grad_pre = (grad_act * slope).astype(bf16)
        up_g[turn_of] = mm(hidden_t, grad_pre).astype(bf16)
        down_g[turn_of] = mm(grad_t, act).astype(bf16)
        sent += put(table, up_g.at[turn_of], grads, sems_out, (turn_of * size, size), 2 * turn_of * block_count)
        sent += put(table, down_g.at[turn_of], grads, sems_out, (total + turn_of * size, size), (2 * turn_of + 1) * block_count)
        out = out + mm_nt(act, down_w[turn_of])
        back = back + mm_nt(grad_pre, up_w[turn_of])
    part[...] = out.astype(bf16)
    dh_out[...] = back.astype(bf16)
    finish(sent)


def attention_back(stacked_grad, outputs, attend, keys, values, stacked_queries):
    both = jnp.concatenate([outputs, outputs], axis=0)
    inner = jnp.sum(wide(stacked_grad) * wide(both), axis=-1, keepdims=True)
    grad_scores = (wide(attend) * (mm_nt(stacked_grad, values) - inner)).astype(bf16)
    grad_q = merge_heads(mm(grad_scores, keys)) * SCALE
    grad_k = mm_tn(grad_scores, stacked_queries) * SCALE
    grad_v = mm_tn(attend, stacked_grad)
    return grad_q, grad_k, grad_v


def cross_back(count, table, chosen, g_ref, x_ref, norms, own_ref, got_ref, p_ref, o_ref, q_ref, k_ref, v_ref, *refs):
    pieces, refs = refs[:count], refs[count:]
    dx_out, low_out, dh_out, dq_out, dk_out, dv_out, sums_out, in_w, out_w, dk_acc, dv_acc, sems, sems_out = refs
    width = q_ref.shape[1]
    copies = fetch(table, pieces, out_w, sems_out, (3 * width, width))
    copies_in = fetch(table, pieces, in_w, sems, (0, width))
    normal, scale = norm_parts(x_ref[...])
    grad = wide(own_ref[...]) + wide(got_ref[...])
    dx = wide(g_ref[...]) + norm_back(grad, normal, scale, norms[4:5])
    dx_out[...] = dx
    sums_out[0:1] = jnp.sum(grad * normal, axis=0, keepdims=True)
    sums_out[1:2] = jnp.sum(grad, axis=0, keepdims=True)
    low = dx.astype(bf16)
    low_out[...] = low
    dk_acc[...] = jnp.zeros_like(dk_acc)
    dv_acc[...] = jnp.zeros_like(dv_acc)
    finish(copies)
    grad_mix = mm(low, out_w[...]).astype(bf16)
    pair_count = width // LANES
    for block in range(low.shape[0] // GROUP):
        rows = slice(block * GROUP, (block + 1) * GROUP)
        for pair, lanes in pairs_of(width):
            keys = chosen_rows(chosen, block, k_ref, lanes)
            values = chosen_rows(chosen, block, v_ref, lanes)
            grad_q, grad_k, grad_v = attention_back(
                stack_heads(grad_mix[rows, lanes]),
                o_ref[rows, lanes],
                p_ref[block * pair_count + pair],
                keys,
                values,
                stack_heads(q_ref[rows, lanes]),
            )
            dq_out[rows, lanes] = grad_q.astype(bf16)
            for j in range(NBRS):
                place = pl.ds(pl.multiple_of(chosen[NBRS * block + j] * NBR_LEN, NBR_LEN), NBR_LEN)
                part = slice(j * NBR_LEN, (j + 1) * NBR_LEN)
                dk_acc[place, lanes] += grad_k[part]
                dv_acc[place, lanes] += grad_v[part]
    dk_out[...] = dk_acc[...].astype(bf16)
    dv_out[...] = dv_acc[...].astype(bf16)
    finish(copies_in)
    dh_out[...] = mm_nt(dq_out[...], in_w[...]).astype(bf16)


def cross_weights(count, table, low_ref, o_ref, h_ref, dq_ref, pool_ref, dk_ref, dv_ref, *refs):
    pieces, refs = refs[:count], refs[count:]
    pool_out = refs[0]
    grads, refs = refs[1 : 1 + count], refs[1 + count :]
    weights, made, sems, sems_out = refs
    width = dq_ref.shape[1]
    block_count = max(1, 2 * count) if count > 1 else 1
    copies = fetch(table, pieces, weights, sems, (width, 2 * width))
    made[3] = mm_tn(low_ref[...], o_ref[...]).astype(bf16)
    made[0] = mm_tn(h_ref[...], dq_ref[...]).astype(bf16)
    pool_t = pool_ref[...].T
    made[1] = mm(pool_t, dk_ref[...]).astype(bf16)
    made[2] = mm(pool_t, dv_ref[...]).astype(bf16)
    sent = []
    for part in range(4):
        sent += put(table, made.at[part], grads, sems_out, (part * width, width), part * block_count)
    finish(copies)
    pool_out[...] = (mm_nt(dk_ref[...], weights[:, :width]) + mm_nt(dv_ref[...], weights[:, width:])).astype(bf16)
    finish(sent)


def self_back(count, table, dx_ref, x_ref, norms, own_ref, got_ref, p_ref, o_ref, q_ref, k_ref, v_ref, cos_ref, sin_ref, *refs):
    pieces, refs = refs[:count], refs[count:]
    dx_out, low_out, dh_out, dq_out, dk_out, dv_out, sums_out, weights, sems = refs
    width = q_ref.shape[1]
    copies = fetch(table, pieces, weights, sems, (LANES, 4 * width))
    normal, scale = norm_parts(x_ref[...])
    grad = wide(own_ref[...]) + wide(got_ref[...])
    dx = dx_ref[...] + norm_back(grad, normal, scale, norms[2:3])
    dx_out[...] = dx
    sums_out[0:1] = jnp.sum(grad * normal, axis=0, keepdims=True)
    sums_out[1:2] = jnp.sum(grad, axis=0, keepdims=True)
    low = dx.astype(bf16)
    low_out[...] = low
    finish(copies)
    grad_mix = mm(low, weights[:, 3 * width :]).astype(bf16)
    cosine, sine = cos_ref[...], -sin_ref[...]
    for pair, lanes in pairs_of(width):
        grad_q, grad_k, grad_v = attention_back(
            stack_heads(grad_mix[:, lanes]),
            o_ref[:, lanes],
            p_ref[pair],
            k_ref[:, lanes],
            v_ref[:, lanes],
            stack_heads(q_ref[:, lanes]),
        )
        dq_out[:, lanes] = turn(grad_q, cosine, sine).astype(bf16)
        dk_out[:, lanes] = turn(grad_k, cosine, sine).astype(bf16)
        dv_out[:, lanes] = grad_v.astype(bf16)
    dh_out[...] = (
        mm_nt(dq_out[...], weights[:, :width])
        + mm_nt(dk_out[...], weights[:, width : 2 * width])
        + mm_nt(dv_out[...], weights[:, 2 * width : 3 * width])
    ).astype(bf16)


def self_weights(count, table, low_ref, o_ref, h_ref, dq_ref, dk_ref, dv_ref, *refs):
    grads, refs = refs[:count], refs[count:]
    made, sems_out = refs
    width = dq_ref.shape[1]
    block_count = max(1, 2 * count) if count > 1 else 1
    made[3] = mm_tn(low_ref[...], o_ref[...]).astype(bf16)
    hidden_t = h_ref[...].T
    made[0] = mm(hidden_t, dq_ref[...]).astype(bf16)
    made[1] = mm(hidden_t, dk_ref[...]).astype(bf16)
    made[2] = mm(hidden_t, dv_ref[...]).astype(bf16)
    sent = []
    for part in range(4):
        sent += put(table, made.at[part], grads, sems_out, (part * width, width), part * block_count)
    finish(sent)


def input_back(dx_ref, x_ref, norms, own_ref, got_ref, dx_out, sums_out):
    normal, scale = norm_parts(wide(x_ref[...]))
    grad = wide(own_ref[...]) + wide(got_ref[...])
    dx_out[...] = dx_ref[...] + norm_back(grad, normal, scale, norms[0:1])
    sums_out[0:1] = jnp.sum(grad * normal, axis=0, keepdims=True)
    sums_out[1:2] = jnp.sum(grad, axis=0, keepdims=True)


SMEM = pl.BlockSpec(memory_space=pltpu.SMEM)
VMEM = pl.BlockSpec(memory_space=pltpu.VMEM)
ANY = pl.BlockSpec(memory_space=pl.ANY)


def call(body, name, scalars, arrays, pieces, outs, grads, scratch, flops):
    shapes = [jax.ShapeDtypeStruct(shape, dtype) for shape, dtype in list(outs) + list(grads)]
    moved = sum(a.size * a.dtype.itemsize for a in list(arrays) + list(pieces))
    moved += sum(int(np.prod(s.shape)) * s.dtype.itemsize for s in shapes)
    return pl.pallas_call(
        body,
        name=name,
        out_shape=shapes,
        in_specs=[SMEM] * len(scalars) + [VMEM] * len(arrays) + [ANY] * len(pieces),
        out_specs=[VMEM] * len(outs) + [ANY] * len(grads),
        scratch_shapes=scratch,
        compiler_params=pltpu.CompilerParams(vmem_limit_bytes=VMEM_BYTES),
        cost_estimate=pl.CostEstimate(flops=int(flops), bytes_accessed=int(moved), transcendentals=0),
    )(*scalars, *arrays, *pieces)


def rope_tables(rows):
    half = HEAD_DIM // 2
    frequency = np.power(np.float32(10000.0), -np.arange(half, dtype=np.float32) / np.float32(half))
    angles = np.arange(rows, dtype=np.float32)[:, None] * frequency[None, :]
    cosine, sine = np.cos(angles), np.sin(angles)
    return (
        jnp.asarray(np.concatenate([cosine] * 4, axis=1), f32),
        jnp.asarray(np.concatenate([-sine, sine] * 2, axis=1), f32),
    )


def dma_sems(count, uses=1):
    blocks = 2 * count if count > 1 else 1
    return pltpu.SemaphoreType.DMA((blocks * uses,))


def on_device(count, inputs, neighbours, nbr_index, ln1_gain, ln1_bias, ln2_gain, ln2_bias, ln3_gain, ln3_bias,
              w_query, w_key, w_value, c_query, c_key, c_value, w_up, w_out, c_out, w_down, cotangent):
    width, hidden = w_query.shape[1], w_up.shape[1]
    shard_rows = w_query.shape[0]
    model = shard_rows * count
    rows = 2 * inputs.shape[0]
    norms = jnp.stack([ln1_gain, ln1_bias, ln2_gain, ln2_bias, ln3_gain, ln3_bias], axis=1)
    norms = jnp.pad(norms, ((0, 0), (0, LANES - NORMS)))

    def pack(*columns):
        return jnp.concatenate([column.astype(bf16) for column in columns], axis=1)

    self_w = gather_pieces(pack(norms, w_query, w_key, w_value, w_out.T), count)
    cross_w = gather_pieces(pack(c_query, c_key, c_value, c_out.T), count)
    ff_w = gather_pieces(pack(w_up, w_down.T), count)
    pieces = len(self_w)
    if pieces > 1:
        table = jnp.asarray(block_tables(count))[lax.axis_index("dp")]
    else:
        table = jnp.zeros((1,), jnp.int32)
    grad_rows = (2 * shard_rows) if pieces > 1 else model

    def bind(body, *extra):
        return functools.partial(body, pieces, *extra)

    stream = join_cores(inputs)
    cot = join_cores(cotangent)
    pool = join_cores(neighbours.reshape(-1, neighbours.shape[-1]))
    pool_rows = pool.shape[0]
    chosen = nbr_index.reshape(-1)
    cosine, sine = rope_tables(rows)
    pairs = width // LANES
    blocks = rows // GROUP
    tall, low = ((rows, model), f32), ((rows, model), bf16)
    slim = ((rows, width), bf16)
    rank8 = ((8, model), f32)
    dense = 2 * rows * model * width

    part, h_one, queries, keys, values, attend, mixture, norm_rows = call(
        bind(self_forward), "self_forward", [table], [stream, cosine, sine], self_w,
        [low, low, slim, slim, slim, ((pairs, 2 * rows, rows), bf16), slim, rank8], [],
        [pltpu.VMEM((model, LANES + 4 * width), bf16), dma_sems(pieces)], 4 * dense)
    got = swap_cores(part)
    ckeys, cvalues = call(
        bind(pool_forward), "pool_forward", [table], [pool], cross_w,
        [((pool_rows, width), bf16)] * 2, [],
        [pltpu.VMEM((model, 2 * width), bf16), dma_sems(pieces)], 4 * pool_rows * model * width)
    part, after_self, h_two, cqueries, cattend, cmixture = call(
        bind(cross_forward), "cross_forward", [table, chosen], [stream, part, got, norm_rows, ckeys, cvalues], cross_w,
        [low, tall, low, slim, ((blocks * pairs, 2 * GROUP, NBRS * NBR_LEN), bf16), slim], [],
        [pltpu.VMEM((model, width), bf16), pltpu.VMEM((model, width), bf16), dma_sems(pieces), dma_sems(pieces)], 2 * dense)
    got = swap_cores(part)
    slices = 3
    size = hidden // slices
    part, after_cross, grad_part, *ff_grads = call(
        bind(feed_forward, slices), "feed_forward", [table], [after_self, part, got, norm_rows, cot], ff_w,
        [low, tall, low], [((grad_rows, 2 * hidden), bf16)] * pieces,
        [pltpu.VMEM((slices, model, size), bf16)] * 4 + [dma_sems(pieces, 2 * slices)] * 2, 12 * rows * model * hidden)
    got = swap_cores(grad_part)
    d_ff = reduce_pieces(ff_grads, count)
    here = lax.axis_index("tensor") * inputs.shape[0]
    there = inputs.shape[0] - here

    def part_of(array, start, size):
        return lax.dynamic_slice_in_dim(array, start, size, 0)

    result = part_of(after_cross, here, inputs.shape[0]) + (
        wide(part_of(part, here, inputs.shape[0])) + wide(swap_cores(part_of(part, there, inputs.shape[0])))
    )
    acc = pltpu.VMEM((pool_rows, width), f32)
    grad_cross, low_cross, grad_part, dcq, dck, dcv, sums_three = call(
        bind(cross_back), "cross_back", [table, chosen],
        [cot, after_cross, norm_rows, grad_part, got, cattend, cmixture, cqueries, ckeys, cvalues], cross_w,
        [tall, low, low, slim, ((pool_rows, width), bf16), ((pool_rows, width), bf16), rank8], [],
        [pltpu.VMEM((model, width), bf16), pltpu.VMEM((model, width), bf16), acc, acc, dma_sems(pieces), dma_sems(pieces)], 3 * dense)
    got = swap_cores(grad_part)
    pool_part, *cross_grads = call(
        bind(cross_weights), "cross_weights", [table], [low_cross, cmixture, h_two, dcq, pool, dck, dcv], cross_w,
        [((pool_rows, model), bf16)], [((grad_rows, 4 * width), bf16)] * pieces,
        [pltpu.VMEM((model, 2 * width), bf16), pltpu.VMEM((4, model, width), bf16), dma_sems(pieces), dma_sems(pieces, 4)],
        2 * dense + 8 * pool_rows * model * width)
    d_cross = reduce_pieces(cross_grads, count)
    grad_self, low_self, grad_part, dq, dk, dv, sums_two = call(
        bind(self_back), "self_back", [table],
        [grad_cross, after_self, norm_rows, grad_part, got, attend, mixture, queries, keys, values, cosine, sine], self_w,
        [tall, low, low, slim, slim, slim, rank8], [],
        [pltpu.VMEM((model, 4 * width), bf16), dma_sems(pieces)], 5 * dense)
    got = swap_cores(grad_part)
    self_grads = call(
        bind(self_weights), "self_weights", [table], [low_self, mixture, h_one, dq, dk, dv], [],
        [], [((grad_rows, 4 * width), bf16)] * pieces,
        [pltpu.VMEM((4, model, width), bf16), dma_sems(pieces, 4)], 4 * dense)
    d_self = reduce_pieces(self_grads, count)
    grad_input, sums_one = call(
        input_back, "input_back", [], [grad_self, stream, norm_rows, grad_part, got], [], [tall, rank8], [], [], rows * model)
    grad_input = part_of(grad_input, here, inputs.shape[0])
    pool_half = pool_rows // 2
    pool_here = lax.axis_index("tensor") * pool_half
    grad_pool = wide(part_of(pool_part, pool_here, pool_half)) + wide(
        swap_cores(part_of(pool_part, pool_half - pool_here, pool_half))
    )
    sums = jnp.concatenate([sums_one[:2], sums_two[:2], sums_three[:2], jnp.zeros((2, model), f32)], axis=0)
    sums = sum_small(sums, count)
    mine = lax.dynamic_slice_in_dim(sums, lax.axis_index("dp") * shard_rows, shard_rows, 1)

    def cut(array, index, size):
        return array[:, index * size : (index + 1) * size]

    return (
        result.astype(bf16),
        grad_input,
        grad_pool.reshape(neighbours.shape),
        mine[0],
        mine[1],
        mine[2],
        mine[3],
        mine[4],
        mine[5],
        cut(d_self, 0, width),
        cut(d_self, 1, width),
        cut(d_self, 2, width),
        cut(d_cross, 0, width),
        cut(d_cross, 1, width),
        cut(d_cross, 2, width),
        cut(d_ff, 0, hidden),
        cut(d_self, 3, width).T,
        cut(d_cross, 3, width).T,
        cut(d_ff, 1, hidden).T,
    )


def solution(mesh):
    both = P(("dp", "tensor"), None)
    pool = P(("dp", "tensor"), None, None)
    norm = P("dp")
    tall, flat = P("dp", "tensor"), P("tensor", "dp")
    return jax.shard_map(
        functools.partial(on_device, mesh.shape["dp"]),
        mesh=mesh,
        in_specs=(both, pool, P("dp", None)) + (norm,) * 6 + (tall,) * 7 + (flat,) * 3 + (both,),
        out_specs=(both, both, pool) + (norm,) * 6 + (tall,) * 7 + (flat,) * 3,
        check_vma=False,
    )
```

```python
import functools

import jax
import jax.numpy as jnp
import numpy as np
from jax import lax
from jax.experimental import pallas as pl
from jax.experimental.pallas import tpu as pltpu
from jax.sharding import PartitionSpec as P

HEAD_DIM = 64
GROUP = 64
NBR_LEN = 128
NBRS = 2
LANES = 128
NORMS = 6
NEG_FILL = -1e30
EPSILON = 1e-05
GELU_A = 0.7978845608028654
GELU_B = 0.044715
PLANES = 4
BLOCKS = 16
MIB = 2**20

bf16 = jnp.bfloat16
f32 = jnp.float32


def mm(left, right):
    return jnp.dot(left, right, preferred_element_type=f32)


def mm_nt(left, right):
    return lax.dot_general(left, right, (((1,), (1,)), ((), ())), preferred_element_type=f32)


def mm_tn(left, right):
    return lax.dot_general(left, right, (((0,), (0,)), ((), ())), preferred_element_type=f32)


def wide(array):
    return array.astype(f32)


def grid_perms(count):
    steps = {"x": 1, "y": 2, "near": 4, "far": 8}
    return {name: [(i, i ^ step) for i in range(count)] for name, step in steps.items()}


def block_tables(count):
    orders = [
        [4 * z + plane for plane in range(PLANES) for z in (0, 2, 1, 3)],
        [4 * z + plane for z in (0, 2, 1, 3) for plane in range(PLANES)],
    ]
    return np.array([[[device ^ step for step in order] for device in range(count)] for order in orders], np.int32)


def pieces_ok(count, rows):
    return count == BLOCKS and rows % 16 == 0


def tie(arrays, gate=()):
    arrays = tuple(arrays)
    if len(arrays) + len(gate) < 2:
        return arrays
    return lax.optimization_barrier(arrays + tuple(gate))[: len(arrays)]


def stack(*arrays):
    return jnp.concatenate(arrays, axis=0)


class Rounds:
    def __init__(self, count):
        self.perms = grid_perms(count)

    def go(self, gate, *sends):
        out = []
        for array, name in sends:
            (array,) = tie([array], gate)
            out.append(lax.ppermute(array, "dp", self.perms[name]))
        return out


def gather_all(a, b, c, d, count, early):
    if not pieces_ok(count, a.shape[0]):
        gathered = [(lax.all_gather(shard, "dp", axis=0, tiled=True),) for shard in (a, b, c, d)]
        return gathered + [(), (), ()]
    go = Rounds(count).go
    (a_far,) = go((), (a, "far"))
    d_x, d_y = go((), (d, "x"), (d, "y"))
    a1 = stack(a, a_far)
    r0 = (d_x, d_y)
    r1 = ax1, ay1, a2, d_d = go((), (a1, "x"), (a1, "y"), (a1, "near"), (d_y, "x"))
    (b_far,) = go((a_far,), (b, "far"))
    b1, column = stack(b, b_far), stack(d, d_x, d_y, d_d)
    r2 = bx1, by1, b2, c_far = go(r0, (b1, "x"), (b1, "y"), (b1, "near"), (c, "far"))
    c1 = stack(c, c_far)
    r3 = ax2, ay2 = go(r1 + list(early), (a2, "x"), (a2, "y"))
    (column_far,) = go(r1, (column, "far"))
    r4 = bx2, by2 = go(r2, (b2, "x"), (b2, "y"))
    (column_near,) = go(r2, (column, "near"))
    r5 = ad1, ad2 = go(r3, (ay1, "x"), (ax2, "y"))
    r6 = bd1, bd2, c2 = go(r4, (by1, "x"), (bx2, "y"), (c1, "near"))
    r7 = cx1, cy1 = go(r5 + [column_far], (c1, "x"), (c1, "y"))
    (column_both,) = go(r5, (column_far, "near"))
    r8 = cx2, cy2 = go(r6 + [column_near], (c2, "x"), (c2, "y"))
    cd1, cd2 = go(r7, (cy1, "x"), (cx2, "y"))
    return [
        (a1, a2, ax1, ax2, ay1, ay2, ad1, ad2),
        (b1, b2, bx1, bx2, by1, by2, bd1, bd2),
        (c1, c2, cx1, cx2, cy1, cy2, cd1, cd2),
        (column, column_far, column_near, column_both),
        tuple(r4),
        tuple(r6),
        tuple(r7),
    ]


def add_half(own, got):
    return (wide(own) + wide(got)).astype(bf16)


def add_diagonal(x_in, y_in, from_x, from_y, x_out, y_out, x_buf, y_buf, sems):
    half = from_x.shape[0]
    loads = [
        pltpu.make_async_copy(x_in.at[pl.ds(half, half), :], x_buf, sems.at[0]),
        pltpu.make_async_copy(y_in.at[pl.ds(0, half), :], y_buf, sems.at[1]),
    ]
    for load in loads:
        load.start()
    finish(loads)
    x_buf[...] = add_half(x_buf[...], from_y[...])
    y_buf[...] = add_half(y_buf[...], from_x[...])
    stores = [
        pltpu.make_async_copy(x_buf, x_out.at[pl.ds(half, half), :], sems.at[2]),
        pltpu.make_async_copy(y_buf, y_out.at[pl.ds(0, half), :], sems.at[3]),
    ]
    for store in stores:
        store.start()
    finish(stores)


def add_plane(own, got_x, got_y, kept, other):
    half = kept.shape[0]
    total = wide(own[...]) + wide(got_x[...]) + wide(got_y[...])
    kept[...] = total[:half]
    other[...] = total[half:].astype(bf16)


def add_near(kept, got, mine, other):
    rows = mine.shape[0]
    total = kept[...] + wide(got[...])
    mine[...] = total[:rows]
    other[...] = total[rows:].astype(bf16)


def write_outs(turned, total, outs):
    start = 0
    for out, flip in zip(outs, turned):
        if flip:
            columns = max(out.shape[0], LANES)
            out[...] = total[:, start : start + columns].T[: out.shape[0]]
            start += columns
        else:
            out[...] = total[:, start : start + out.shape[1]]
            start += out.shape[1]


def add_far(turned, mine, got, *outs):
    write_outs(turned, mine[...] + wide(got[...]), outs)


class Reduction:
    def __init__(self, pieces, count, widths, turned):
        self.pieces, self.widths, self.turned = pieces, widths, turned
        self.perms = grid_perms(count)
        self.ended = ()
        self.outs = None
        if len(pieces) == 1:
            total = wide(lax.psum_scatter(pieces[0], "dp", scatter_dimension=0, tiled=True))
            self.outs, start = [], 0
            for width, flip in zip(widths, turned):
                part = total[:, start : start + width]
                self.outs.append(part.T if flip else part)
                start += max(width, LANES)

    def out_shapes(self, rows):
        return [((width, rows) if flip else (rows, width), f32) for width, flip in zip(self.widths, self.turned)]

    def send(self, arrays, names, gate):
        out = []
        for array, name in zip(arrays, names):
            (array,) = tie([array], gate)
            out.append(lax.ppermute(array, "dp", self.perms[name]))
        self.ended = tie(out)
        return self.ended

    def diagonal(self, gate=()):
        if self.outs is not None:
            return
        own, x_col, y_col, d_first, d_second = self.pieces
        half, columns = d_first.shape
        from_x, from_y = self.send([d_first, d_second], ["x", "y"], gate)
        buffer = pltpu.VMEM((half, columns), bf16)
        self.sides = pl.pallas_call(
            add_diagonal, name="add_diagonal", out_shape=[pltpu.HBM(x_col.shape, bf16)] * 2,
            in_specs=[HBM, HBM, VMEM, VMEM], out_specs=[HBM, HBM], input_output_aliases={0: 0, 1: 1},
            scratch_shapes=[buffer, buffer, pltpu.SemaphoreType.DMA((4,))],
            compiler_params=pltpu.CompilerParams(vmem_limit_bytes=60 * MIB), cost_estimate=cost(2),
        )(x_col, y_col, from_x, from_y)

    def plane(self, gate=()):
        if self.outs is not None:
            return
        half, columns = self.pieces[3].shape
        got_x, got_y = self.send(self.sides, ["x", "y"], gate)
        self.kept, self.other = call(
            add_plane, "add_plane", [], [self.pieces[0], got_x, got_y], [],
            [((half, columns), f32), ((half, columns), bf16)], [], [], 2, mib=60)

    def near(self, gate=()):
        if self.outs is not None:
            return
        half, columns = self.pieces[3].shape
        (got,) = self.send([self.other], ["near"], gate)
        self.mine, self.other = call(
            add_near, "add_near", [], [self.kept, got], [],
            [((half // 2, columns), f32), ((half // 2, columns), bf16)], [], [], 1, mib=60)

    def far(self, gate=()):
        if self.outs is not None:
            return
        (got,) = self.send([self.other], ["far"], gate)
        shapes = self.out_shapes(self.pieces[3].shape[0] // 2)
        self.outs = call(
            functools.partial(add_far, self.turned), "add_far", [], [self.mine, got], [], shapes, [], [], 1, mib=60)


def add_two(left, right, out):
    out[...] = add_half(left[...], right[...])


def add_column(own, got_near, got_far, mine, x_out, y_out, d_out):
    rows = mine.shape[0]
    total = wide(own[...]) + wide(got_near[...]) + wide(got_far[...])
    mine[...] = total[:rows]
    for place, out in enumerate((x_out, y_out, d_out)):
        out[...] = total[(place + 1) * rows : (place + 2) * rows].astype(bf16)


def add_sides(turned, mine, got_x, got_y, *outs):
    write_outs(turned, mine[...] + wide(got_x[...]) + wide(got_y[...]), outs)


class FlatReduction(Reduction):
    def near(self, gate=()):
        if self.outs is not None:
            return
        own, across, beside, corner = self.pieces
        (got_across,) = self.send([corner], ["near"], gate)
        self.got_across = got_across
        (self.got_own,) = self.send([beside], ["near"], gate)
        (self.across,) = call(add_two, "add_two", [], [across, got_across], [], [(across.shape, bf16)], [], [], 1, mib=60)

    def far(self, gate=()):
        if self.outs is not None:
            return
        own = self.pieces[0]
        (got,) = self.send([self.across], ["far"], gate)
        self.rows = own.shape[0] // PLANES
        block = (self.rows, own.shape[1])
        self.mine, *self.sides = call(
            add_column, "add_column", [], [own, self.got_own, got], [], [(block, f32)] + [(block, bf16)] * 3, [], [], 2, mib=60)

    def diagonal(self, gate=()):
        if self.outs is not None:
            return
        (got,) = self.send([self.sides[2]], ["x"], gate)
        (self.y_side,) = call(add_two, "add_two", [], [self.sides[1], got], [], [(got.shape, bf16)], [], [], 1, mib=60)

    def plane(self, gate=()):
        if self.outs is not None:
            return
        got_x, got_y = self.send([self.sides[0], self.y_side], ["x", "y"], gate)
        self.outs = call(
            functools.partial(add_sides, self.turned), "add_sides", [], [self.mine, got_x, got_y], [],
            self.out_shapes(self.rows), [], [], 1, mib=60)


def swap_cores(array):
    return lax.ppermute(array, "tensor", [(0, 1), (1, 0)])


def join_cores(array):
    other = swap_cores(array)
    low = lax.axis_index("tensor") == 0
    return jnp.concatenate(
        [jnp.where(low, array, other), jnp.where(low, other, array)], axis=0
    )


def fetch(table, pieces, target, sems, columns, sem_from=0):
    start, size = columns
    copies = []
    if len(pieces) == 1:
        copies.append(
            pltpu.make_async_copy(pieces[0].at[:, pl.ds(start, size)], target, sems.at[sem_from])
        )
    else:
        rows = target.shape[0] // table.shape[0]
        slot = 0
        for piece in pieces:
            for j in range(piece.shape[0] // rows):
                first = pl.multiple_of(table[slot] * rows, 16)
                copies.append(
                    pltpu.make_async_copy(
                        piece.at[pl.ds(j * rows, rows), pl.ds(start, size)],
                        target.at[pl.ds(first, rows), :],
                        sems.at[sem_from + slot],
                    )
                )
                slot += 1
    for copy in copies:
        copy.start()
    return copies


def put(table, source, pieces, sems, columns, sem_from=0):
    start, size = columns
    copies = []
    if len(pieces) == 1:
        copies.append(
            pltpu.make_async_copy(source, pieces[0].at[:, pl.ds(start, size)], sems.at[sem_from])
        )
    else:
        rows = source.shape[0] // table.shape[0]
        slot = 0
        for piece in pieces:
            for j in range(piece.shape[0] // rows):
                first = pl.multiple_of(table[slot] * rows, 16)
                copies.append(
                    pltpu.make_async_copy(
                        source.at[pl.ds(first, rows), :],
                        piece.at[pl.ds(j * rows, rows), pl.ds(start, size)],
                        sems.at[sem_from + slot],
                    )
                )
                slot += 1
    for copy in copies:
        copy.start()
    return copies


def finish(copies):
    for copy in copies:
        copy.wait()


def norm_parts(stream):
    center = stream - jnp.mean(stream, axis=-1, keepdims=True)
    spread = jnp.mean(center * center, axis=-1, keepdims=True)
    scale = lax.rsqrt(spread + EPSILON)
    return center * scale, scale


def norm_back(grad, normal, scale, gain):
    inner = grad * gain
    return scale * (
        inner
        - jnp.mean(inner, axis=-1, keepdims=True)
        - normal * jnp.mean(inner * normal, axis=-1, keepdims=True)
    )


def turn(pair, cosine, sine):
    lane = lax.broadcasted_iota(jnp.int32, pair.shape, 1)
    low_half = lane % HEAD_DIM < HEAD_DIM // 2
    partner = jnp.where(
        low_half,
        pltpu.roll(pair, LANES - HEAD_DIM // 2, 1),
        pltpu.roll(pair, HEAD_DIM // 2, 1),
    )
    return pair * cosine + partner * sine


def stack_heads(pair):
    lane = lax.broadcasted_iota(jnp.int32, pair.shape, 1)
    zero = jnp.zeros_like(pair)
    return jnp.concatenate(
        [jnp.where(lane < HEAD_DIM, pair, zero), jnp.where(lane < HEAD_DIM, zero, pair)], axis=0
    )


def merge_heads(stacked):
    rows = stacked.shape[0] // 2
    lane = lax.broadcasted_iota(jnp.int32, (rows, stacked.shape[1]), 1)
    return jnp.where(lane < HEAD_DIM, stacked[:rows], stacked[rows:])


def softmax_low(scores):
    raised = jnp.exp(scores - jnp.max(scores, axis=-1, keepdims=True))
    return (raised * (1.0 / jnp.sum(raised, axis=-1, keepdims=True))).astype(bf16)


def pairs_of(width):
    return [(pair, slice(pair * LANES, (pair + 1) * LANES)) for pair in range(width // LANES)]


SCALE = HEAD_DIM ** (-0.5)


def self_forward(count, table, x_ref, cos_ref, sin_ref, *refs):
    pieces, refs = refs[:count], refs[count:]
    part, h_out, q_out, k_out, v_out, p_out, o_out, norms_out, weights, sems = refs
    width = q_out.shape[1]
    copies = fetch(table, pieces, weights, sems, (0, weights.shape[1]))
    normal, _ = norm_parts(wide(x_ref[...]))
    finish(copies)
    rows = wide(weights[:, :LANES]).T[:8]
    norms_out[...] = rows
    hidden = (normal * rows[0:1] + rows[1:2]).astype(bf16)
    h_out[...] = hidden
    mixed = mm(hidden, weights[:, LANES : LANES + 3 * width])
    cosine, sine = cos_ref[...], sin_ref[...]
    count_rows = hidden.shape[0]
    query_pos = lax.broadcasted_iota(jnp.int32, (2 * count_rows, count_rows), 0) % count_rows
    allowed = query_pos >= lax.broadcasted_iota(jnp.int32, (2 * count_rows, count_rows), 1)
    for pair, lanes in pairs_of(width):
        queries = turn(mixed[:, lanes], cosine, sine).astype(bf16)
        keys = turn(mixed[:, width + pair * LANES : width + (pair + 1) * LANES], cosine, sine).astype(bf16)
        values = mixed[:, 2 * width + pair * LANES : 2 * width + (pair + 1) * LANES].astype(bf16)
        q_out[:, lanes] = queries
        k_out[:, lanes] = keys
        v_out[:, lanes] = values
        scores = jnp.where(allowed, mm_nt(stack_heads(queries), keys) * SCALE, NEG_FILL)
        attend = softmax_low(scores)
        p_out[pair] = attend
        o_out[:, lanes] = merge_heads(mm(attend, values)).astype(bf16)
    part[...] = mm_nt(o_out[...], weights[:, LANES + 3 * width :]).astype(bf16)


def pool_forward(count, table, pool_ref, *refs):
    pieces, refs = refs[:count], refs[count:]
    k_out, v_out, weights, sems = refs
    width = k_out.shape[1]
    finish(fetch(table, pieces, weights, sems, (width, 2 * width)))
    mixed = mm(pool_ref[...], weights[...])
    k_out[...] = mixed[:, :width].astype(bf16)
    v_out[...] = mixed[:, width:].astype(bf16)


def chosen_rows(chosen, block, ref, lanes):
    return jnp.concatenate(
        [
            ref[pl.ds(pl.multiple_of(chosen[NBRS * block + j] * NBR_LEN, NBR_LEN), NBR_LEN), lanes]
            for j in range(NBRS)
        ],
        axis=0,
    )


def cross_forward(count, table, chosen, x_ref, own_ref, got_ref, norms, k_ref, v_ref, *refs):
    pieces, refs = refs[:count], refs[count:]
    part, x_out, h_out, q_out, p_out, o_out, in_w, out_w, sems, sems_out = refs
    width = q_out.shape[1]
    copies = fetch(table, pieces, in_w, sems, (0, width))
    copies_out = fetch(table, pieces, out_w, sems_out, (3 * width, width))
    stream = wide(x_ref[...]) + (wide(own_ref[...]) + wide(got_ref[...]))
    x_out[...] = stream
    normal, _ = norm_parts(stream)
    hidden = (normal * norms[2:3] + norms[3:4]).astype(bf16)
    h_out[...] = hidden
    finish(copies)
    queries = mm(hidden, in_w[...]).astype(bf16)
    q_out[...] = queries
    pair_count = width // LANES
    for block in range(queries.shape[0] // GROUP):
        rows = slice(block * GROUP, (block + 1) * GROUP)
        for pair, lanes in pairs_of(width):
            keys = chosen_rows(chosen, block, k_ref, lanes)
            values = chosen_rows(chosen, block, v_ref, lanes)
            attend = softmax_low(mm_nt(stack_heads(queries[rows, lanes]), keys) * SCALE)
            p_out[block * pair_count + pair] = attend
            o_out[rows, lanes] = merge_heads(mm(attend, values)).astype(bf16)
    finish(copies_out)
    part[...] = mm_nt(o_out[...], out_w[...]).astype(bf16)


def feed_forward(count, grad_count, slices, table, grad_table, side, x_ref, own_ref, got_ref, norms, g_ref, out_ref, back_ref, *refs):
    pieces, refs = refs[:count], refs[count:]
    part, x_out, dh_out, mine, other = refs[:5]
    grads, refs = refs[5 : 5 + grad_count], refs[5 + grad_count :]
    up_w, down_w, up_g, down_g, sems, sems_out = refs
    half = mine.shape[0]
    here = pl.ds(pl.multiple_of(side[0] * half, half), half)
    there = pl.ds(pl.multiple_of((1 - side[0]) * half, half), half)
    total = up_w.shape[0] * up_w.shape[2]
    size = total // slices
    block_count = table.shape[0] if count > 1 else 1
    copies = []
    for turn_of in range(slices):
        copies.append(
            fetch(table, pieces, up_w.at[turn_of], sems, (turn_of * size, size), 2 * turn_of * block_count)
            + fetch(table, pieces, down_w.at[turn_of], sems, (total + turn_of * size, size), (2 * turn_of + 1) * block_count)
        )
    stream = wide(x_ref[...]) + (wide(own_ref[...]) + wide(got_ref[...]))
    x_out[...] = stream
    normal, _ = norm_parts(stream)
    hidden = (normal * norms[4:5] + norms[5:6]).astype(bf16)
    grad = g_ref[...]
    hidden_t, grad_t = hidden.T, grad.T
    out = out_ref[...]
    back = back_ref[...]
    sent = []
    for turn_of in range(slices):
        finish(copies[turn_of])
        pre = mm(hidden, up_w[turn_of])
        grad_act = mm(grad, down_w[turn_of])
        square = pre * pre
        bend = jnp.tanh(GELU_A * (pre + GELU_B * square * pre))
        gate = 0.5 * (1.0 + bend)
        act = (pre * gate).astype(bf16)
        slope = gate + 0.5 * pre * (1.0 - bend * bend) * (GELU_A * (1.0 + 3.0 * GELU_B * square))
        grad_pre = (grad_act * slope).astype(bf16)
        up_g[turn_of] = mm(hidden_t, grad_pre).astype(bf16)
        down_g[turn_of] = mm(grad_t, act).astype(bf16)
        sent += put(grad_table, up_g.at[turn_of], grads, sems_out, (turn_of * size, size), 2 * turn_of * block_count)
        sent += put(grad_table, down_g.at[turn_of], grads, sems_out, (total + turn_of * size, size), (2 * turn_of + 1) * block_count)
        out = out + mm_nt(act, down_w[turn_of])
        back = back + mm_nt(grad_pre, up_w[turn_of])
    part[...] = out
    mine[...] = x_out[here, :] + part[here, :]
    other[...] = part[there, :].astype(bf16)
    dh_out[...] = back.astype(dh_out.dtype)
    finish(sent)


def attention_back(stacked_grad, outputs, attend, keys, values, stacked_queries):
    both = jnp.concatenate([outputs, outputs], axis=0)
    inner = jnp.sum(wide(stacked_grad) * wide(both), axis=-1, keepdims=True)
    grad_scores = (wide(attend) * (mm_nt(stacked_grad, values) - inner)).astype(bf16)
    grad_q = merge_heads(mm(grad_scores, keys)) * SCALE
    grad_k = mm_tn(grad_scores, stacked_queries) * SCALE
    grad_v = mm_tn(attend, stacked_grad)
    return grad_q, grad_k, grad_v


def cross_back(count, table, chosen, g_ref, x_ref, norms, own_ref, got_ref, p_ref, o_ref, q_ref, k_ref, v_ref, *refs):
    pieces, refs = refs[:count], refs[count:]
    dx_out, low_out, dh_out, dq_out, dk_out, dv_out, sums_out, in_w, out_w, dk_acc, dv_acc, sems, sems_out = refs
    width = q_ref.shape[1]
    copies = fetch(table, pieces, out_w, sems_out, (3 * width, width))
    copies_in = fetch(table, pieces, in_w, sems, (0, width))
    normal, scale = norm_parts(x_ref[...])
    grad = wide(own_ref[...]) + wide(got_ref[...])
    dx = wide(g_ref[...]) + norm_back(grad, normal, scale, norms[4:5])
    dx_out[...] = dx
    sums_out[0:1] = jnp.sum(grad * normal, axis=0, keepdims=True)
    sums_out[1:2] = jnp.sum(grad, axis=0, keepdims=True)
    low = dx.astype(bf16)
    low_out[...] = low
    dk_acc[...] = jnp.zeros_like(dk_acc)
    dv_acc[...] = jnp.zeros_like(dv_acc)
    finish(copies)
    grad_mix = mm(low, out_w[...]).astype(bf16)
    pair_count = width // LANES
    for block in range(low.shape[0] // GROUP):
        rows = slice(block * GROUP, (block + 1) * GROUP)
        for pair, lanes in pairs_of(width):
            keys = chosen_rows(chosen, block, k_ref, lanes)
            values = chosen_rows(chosen, block, v_ref, lanes)
            grad_q, grad_k, grad_v = attention_back(
                stack_heads(grad_mix[rows, lanes]),
                o_ref[rows, lanes],
                p_ref[block * pair_count + pair],
                keys,
                values,
                stack_heads(q_ref[rows, lanes]),
            )
            dq_out[rows, lanes] = grad_q.astype(bf16)
            for j in range(NBRS):
                place = pl.ds(pl.multiple_of(chosen[NBRS * block + j] * NBR_LEN, NBR_LEN), NBR_LEN)
                part = slice(j * NBR_LEN, (j + 1) * NBR_LEN)
                dk_acc[place, lanes] += grad_k[part]
                dv_acc[place, lanes] += grad_v[part]
    dk_out[...] = dk_acc[...].astype(bf16)
    dv_out[...] = dv_acc[...].astype(bf16)
    finish(copies_in)
    dh_out[...] = mm_nt(dq_out[...], in_w[...]).astype(bf16)


def cross_weights(count, grad_count, table, side, low_ref, o_ref, h_ref, dq_ref, pool_ref, dk_ref, dv_ref, *refs):
    pieces, refs = refs[:count], refs[count:]
    pool_out, pool_other = refs[:2]
    grads, refs = refs[2 : 2 + grad_count], refs[2 + grad_count :]
    weights, made, full, sems, sems_out = refs
    width = dq_ref.shape[1]
    block_count = table.shape[0] if count > 1 else 1
    copies = fetch(table, pieces, weights, sems, (width, 2 * width))
    made[3] = mm_tn(low_ref[...], o_ref[...]).astype(bf16)
    made[0] = mm_tn(h_ref[...], dq_ref[...]).astype(bf16)
    pool_t = pool_ref[...].T
    made[1] = mm(pool_t, dk_ref[...]).astype(bf16)
    made[2] = mm(pool_t, dv_ref[...]).astype(bf16)
    sent = []
    for part in range(4):
        sent += put(table, made.at[part], grads, sems_out, (part * width, width), part * block_count)
    finish(copies)
    full[...] = mm_nt(dk_ref[...], weights[:, :width]) + mm_nt(dv_ref[...], weights[:, width:])
    half = pool_out.shape[0]
    pool_out[...] = full[pl.ds(pl.multiple_of(side[0] * half, half), half), :].astype(bf16)
    pool_other[...] = full[pl.ds(pl.multiple_of((1 - side[0]) * half, half), half), :].astype(bf16)
    finish(sent)


def self_back(count, table, dx_ref, x_ref, norms, own_ref, got_ref, p_ref, o_ref, q_ref, k_ref, v_ref, cos_ref, sin_ref, *refs):
    pieces, refs = refs[:count], refs[count:]
    dx_out, low_out, dh_out, dq_out, dk_out, dv_out, sums_out, weights, sems = refs
    width = q_ref.shape[1]
    copies = fetch(table, pieces, weights, sems, (LANES, 4 * width))
    normal, scale = norm_parts(x_ref[...])
    grad = wide(own_ref[...]) + wide(got_ref[...])
    dx = dx_ref[...] + norm_back(grad, normal, scale, norms[2:3])
    dx_out[...] = dx
    sums_out[0:1] = jnp.sum(grad * normal, axis=0, keepdims=True)
    sums_out[1:2] = jnp.sum(grad, axis=0, keepdims=True)
    low = dx.astype(bf16)
    low_out[...] = low
    finish(copies)
    grad_mix = mm(low, weights[:, 3 * width :]).astype(bf16)
    cosine, sine = cos_ref[...], -sin_ref[...]
    for pair, lanes in pairs_of(width):
        grad_q, grad_k, grad_v = attention_back(
            stack_heads(grad_mix[:, lanes]),
            o_ref[:, lanes],
            p_ref[pair],
            k_ref[:, lanes],
            v_ref[:, lanes],
            stack_heads(q_ref[:, lanes]),
        )
        dq_out[:, lanes] = turn(grad_q, cosine, sine).astype(bf16)
        dk_out[:, lanes] = turn(grad_k, cosine, sine).astype(bf16)
        dv_out[:, lanes] = grad_v.astype(bf16)
    dh_out[...] = (
        mm_nt(dq_out[...], weights[:, :width])
        + mm_nt(dk_out[...], weights[:, width : 2 * width])
        + mm_nt(dv_out[...], weights[:, 2 * width : 3 * width])
    ).astype(bf16)


def self_weights(count, grad_count, table, low_ref, o_ref, h_ref, dq_ref, dk_ref, dv_ref, one_ref, two_ref, three_ref, *refs):
    grads, refs = refs[:grad_count], refs[grad_count:]
    made, norms, sems_out, sems_norm = refs
    width = dq_ref.shape[1]
    block_count = table.shape[0] if grad_count > 1 else 1
    made[3] = mm_tn(low_ref[...], o_ref[...]).astype(bf16)
    hidden_t = h_ref[...].T
    made[0] = mm(hidden_t, dq_ref[...]).astype(bf16)
    made[1] = mm(hidden_t, dk_ref[...]).astype(bf16)
    made[2] = mm(hidden_t, dv_ref[...]).astype(bf16)
    sent = []
    for part in range(4):
        sent += put(table, made.at[part], grads, sems_out, (part * width, width), part * block_count)
    sums = [one_ref[:2], two_ref[:2], three_ref[:2], jnp.zeros((LANES - NORMS, one_ref.shape[1]), f32)]
    norms[...] = jnp.concatenate(sums, axis=0).T.astype(bf16)
    sent += put(table, norms, grads, sems_norm, (4 * width, LANES))
    finish(sent)


def input_back(side, dx_ref, x_ref, norms, own_ref, got_ref, dx_out, sums_out, full):
    normal, scale = norm_parts(wide(x_ref[...]))
    grad = wide(own_ref[...]) + wide(got_ref[...])
    full[...] = dx_ref[...] + norm_back(grad, normal, scale, norms[0:1])
    half = dx_out.shape[0]
    dx_out[...] = full[pl.ds(pl.multiple_of(side[0] * half, half), half), :]
    sums_out[0:1] = jnp.sum(grad * normal, axis=0, keepdims=True)
    sums_out[1:2] = jnp.sum(grad, axis=0, keepdims=True)


SMEM = pl.BlockSpec(memory_space=pltpu.SMEM)
VMEM = pl.BlockSpec(memory_space=pltpu.VMEM)
ANY = pl.BlockSpec(memory_space=pl.ANY)
HBM = pl.BlockSpec(memory_space=pltpu.HBM)


def cost(microseconds):
    return pl.CostEstimate(flops=int(microseconds * 3.85e+08), bytes_accessed=0, transcendentals=0)


def call(body, name, scalars, arrays, pieces, outs, grads, scratch, microseconds, mib=60, gate=()):
    if gate:
        arrays = list(tie(arrays, gate))
    shapes = [pltpu.VMEM(*out[:2]) if len(out) > 2 else jax.ShapeDtypeStruct(*out) for out in outs]
    shapes += [pltpu.HBM(shape, dtype) for shape, dtype in grads]
    return pl.pallas_call(
        body,
        name=name,
        out_shape=shapes,
        in_specs=[SMEM] * len(scalars) + [VMEM] * len(arrays) + [ANY] * len(pieces),
        out_specs=[VMEM] * len(outs) + [HBM] * len(grads),
        scratch_shapes=scratch,
        compiler_params=pltpu.CompilerParams(vmem_limit_bytes=mib * MIB),
        cost_estimate=cost(microseconds),
    )(*scalars, *arrays, *pieces)


def rope_tables(rows):
    half = HEAD_DIM // 2
    frequency = np.power(np.float32(10000.0), -np.arange(half, dtype=np.float32) / np.float32(half))
    angles = np.arange(rows, dtype=np.float32)[:, None] * frequency[None, :]
    cosine, sine = np.cos(angles), np.sin(angles)
    return (
        jnp.asarray(np.concatenate([cosine] * 4, axis=1), f32),
        jnp.asarray(np.concatenate([-sine, sine] * 2, axis=1), f32),
    )


def dma_sems(count, uses=1):
    blocks = BLOCKS if count > 1 else 1
    return pltpu.SemaphoreType.DMA((blocks * uses,))


def pack(*columns):
    return jnp.concatenate([column.astype(bf16) for column in columns], axis=1)


def pack_kernel(*refs):
    norms, (query, key, value, out_w, packed) = refs[:NORMS], refs[NORMS:]
    rows, width = query.shape
    lines = [norm[...] for norm in norms] + [jnp.zeros((LANES - NORMS, rows), f32)]
    packed[:, :LANES] = jnp.concatenate(lines, axis=0).T.astype(bf16)
    for place, ref in enumerate((query, key, value)):
        packed[:, LANES + place * width : LANES + (place + 1) * width] = ref[...].astype(bf16)
    packed[:, LANES + 3 * width :] = out_w[...].T.astype(bf16)


def pack_self(norms, query, key, value, out_w, fast):
    if not fast:
        lines = jnp.pad(jnp.stack(norms, axis=1), ((0, 0), (0, LANES - NORMS)))
        return pack(lines, query, key, value, out_w.T)
    lines = [norm.reshape(1, -1) for norm in norms]
    shape = (query.shape[0], LANES + 4 * query.shape[1])
    return call(pack_kernel, "pack_self", [], lines + [query, key, value, out_w], [], [(shape, bf16)], [], [], 2, mib=60)[0]


def on_device(count, inputs, neighbours, nbr_index, ln1_gain, ln1_bias, ln2_gain, ln2_bias, ln3_gain, ln3_bias,
              w_query, w_key, w_value, c_query, c_key, c_value, w_up, w_out, c_out, w_down, cotangent):
    width, hidden = w_query.shape[1], w_up.shape[1]
    shard_rows = w_query.shape[0]
    model = shard_rows * count
    rows = 2 * inputs.shape[0]
    norms = [ln1_gain, ln1_bias, ln2_gain, ln2_bias, ln3_gain, ln3_bias]

    stream = join_cores(inputs)
    cot = join_cores(cotangent)
    pool = join_cores(neighbours.reshape(-1, neighbours.shape[-1]))
    down_t = w_down.T
    part_hidden = hidden // 2
    cuts = [slice(0, part_hidden), slice(part_hidden, hidden)]
    self_w, cross_w, *ff_w, gate_self, gate_pool, gate_cross = gather_all(
        pack_self(norms, w_query, w_key, w_value, w_out, pieces_ok(count, shard_rows)),
        pack(c_query, c_key, c_value, c_out.T),
        pack(w_up[:, cuts[0]], down_t[:, cuts[0]]),
        pack(w_up[:, cuts[1]], down_t[:, cuts[1]]),
        count,
        (stream, cot, pool),
    )
    ff_w = ff_w[::-1]
    side = lax.axis_index("tensor").astype(jnp.int32).reshape(1)
    pieces = len(self_w)
    if pieces > 1:
        tables = jnp.asarray(block_tables(count))
        table, flat_table = (tables[i][lax.axis_index("dp")] for i in range(2))
        grad_rows = [shard_rows * blocks for blocks in (4, 4, 4, 2, 2)]
        flat_rows = [shard_rows * PLANES] * 4
    else:
        table = flat_table = jnp.zeros((1,), jnp.int32)
        grad_rows = flat_rows = [model]
    grad_count = len(grad_rows)

    def bind(body, *extra):
        return functools.partial(body, pieces, *extra)

    pool_rows = pool.shape[0]
    chosen = nbr_index.reshape(-1)
    cosine, sine = rope_tables(rows)
    pairs = width // LANES
    blocks = rows // GROUP
    tall, low = ((rows, model), f32), ((rows, model), bf16)
    slim = ((rows, width), bf16)
    rank8 = ((8, model), f32)
    half_tall, half_low = ((rows // 2, model), f32), ((rows // 2, model), bf16)

    def kept(out):
        return out


    part, h_one, queries, keys, values, attend, mixture, norm_rows = call(
        bind(self_forward), "self_forward", [table], [stream, cosine, sine], self_w,
        [low, kept(low), kept(slim), kept(slim), kept(slim), kept(((pairs, 2 * rows, rows), bf16)), kept(slim), rank8], [],
        [pltpu.VMEM((model, LANES + 4 * width), bf16), dma_sems(pieces)], 8, mib=60, gate=gate_self)
    got = swap_cores(part)
    ckeys, cvalues = call(
        bind(pool_forward), "pool_forward", [table], [pool], cross_w,
        [kept(((pool_rows, width), bf16))] * 2, [],
        [pltpu.VMEM((model, 2 * width), bf16), dma_sems(pieces)], 3, mib=60, gate=gate_pool)
    part, after_self, h_two, cqueries, cattend, cmixture = call(
        bind(cross_forward), "cross_forward", [table, chosen], [stream, part, got, norm_rows, ckeys, cvalues], cross_w,
        [low, kept(tall), kept(low), kept(slim), kept(((blocks * pairs, 2 * GROUP, NBRS * NBR_LEN), bf16)), kept(slim)], [],
        [pltpu.VMEM((model, width), bf16), pltpu.VMEM((model, width), bf16), dma_sems(pieces), dma_sems(pieces)], 6, mib=60, gate=gate_cross)
    got = swap_cores(part)
    slices = 2
    size = part_hidden // slices
    out, back = jnp.zeros((rows, model), f32), jnp.zeros((rows, model), f32)
    ff_grads = []
    forms = [(flat_table, flat_table, flat_rows, tall, ()), (table, table, grad_rows, low, ())]
    for ff_pieces, (from_table, to_table, to_rows, form, gate) in zip(ff_w, forms):
        out, after_cross, back, result, result_other, *grads = call(
            functools.partial(feed_forward, len(ff_pieces), len(to_rows), slices), "feed_forward", [from_table, to_table, side],
            [after_self, part, got, norm_rows, cot, out, back], ff_pieces,
            [tall, kept(tall), form, half_tall, half_low], [((count_of, 2 * part_hidden), bf16) for count_of in to_rows],
            [pltpu.VMEM((slices, model, size), bf16)] * 4 + [dma_sems(pieces, 2 * slices)] * 2, 10, mib=60, gate=gate)
        ff_grads.append(grads)
    grad_part = back
    got = swap_cores(grad_part)
    ff_widths, ff_turned = [part_hidden] * 2, [False, True]
    one = FlatReduction(ff_grads[0], count, ff_widths, ff_turned)
    two = Reduction(ff_grads[1], count, ff_widths, ff_turned)
    one.near()
    two.diagonal()
    two.plane()
    one.far()
    acc = pltpu.VMEM((pool_rows, width), f32)
    grad_cross, low_cross, grad_part, dcq, dck, dcv, sums_three = call(
        bind(cross_back), "cross_back", [table, chosen],
        [cot, after_cross, norm_rows, grad_part, got, cattend, cmixture, cqueries, ckeys, cvalues], cross_w,
        [tall, low, low, slim, ((pool_rows, width), bf16), ((pool_rows, width), bf16), rank8], [],
        [pltpu.VMEM((model, width), bf16), pltpu.VMEM((model, width), bf16), acc, acc, dma_sems(pieces), dma_sems(pieces)], 8, mib=60, gate=(one.got_across,) if pieces > 1 else ())
    got = swap_cores(grad_part)
    pool_part, pool_other, *cross_grads = call(
        bind(cross_weights, grad_count), "cross_weights", [table, side], [low_cross, cmixture, h_two, dcq, pool, dck, dcv], cross_w,
        [((pool_rows // 2, model), bf16)] * 2, [((count_of, 4 * width), bf16) for count_of in grad_rows],
        [pltpu.VMEM((model, 2 * width), bf16), pltpu.VMEM((4, model, width), bf16), pltpu.VMEM((pool_rows, model), f32), dma_sems(pieces), dma_sems(pieces, 4)],
        8, mib=60, gate=(one.got_own,) if pieces > 1 else ())
    grad_self, low_self, grad_part, dq, dk, dv, sums_two = call(
        bind(self_back), "self_back", [table],
        [grad_cross, after_self, norm_rows, grad_part, got, attend, mixture, queries, keys, values, cosine, sine], self_w,
        [tall, low, low, slim, slim, slim, rank8], [],
        [pltpu.VMEM((model, 4 * width), bf16), dma_sems(pieces)], 7, mib=60, gate=tuple(two.sides) + (one.across,) if pieces > 1 else ())
    got = swap_cores(grad_part)
    three = Reduction(cross_grads, count, [width] * 4, [False] * 3 + [True])
    three.diagonal()
    grad_input, sums_one = call(
        input_back, "input_back", [side], [grad_self, stream, norm_rows, grad_part, got], [], [half_tall, rank8], [],
        [pltpu.VMEM((rows, model), f32)], 2, mib=60)
    self_grads = call(
        functools.partial(self_weights, pieces, grad_count), "self_weights", [table],
        [low_self, mixture, h_one, dq, dk, dv, sums_one, sums_two, sums_three], [],
        [], [((count_of, 4 * width + LANES), bf16) for count_of in grad_rows],
        [pltpu.VMEM((4, model, width), bf16), pltpu.VMEM((model, LANES), bf16), dma_sems(pieces, 4), dma_sems(pieces)], 4,
        mib=60, gate=two.ended)
    four = Reduction(self_grads, count, [width] * 4 + [8], [False] * 3 + [True] * 2)
    two.near()
    four.diagonal()
    three.plane()
    four.plane(one.ended + two.ended)
    one.diagonal()
    three.near()
    two.far(three.ended[:0])
    one.plane(three.ended)
    four.near()
    three.far(one.ended)
    four.far()
    d_ff, d_cross, d_self = [one.outs, two.outs], three.outs, four.outs
    d_up = jnp.concatenate([part_of_ff[0] for part_of_ff in d_ff[::-1]], axis=1)
    d_down = jnp.concatenate([part_of_ff[1] for part_of_ff in d_ff[::-1]], axis=0)
    grad_pool = wide(pool_part) + wide(swap_cores(pool_other))
    mine = d_self[4]
    return (
        (result + wide(swap_cores(result_other))).astype(bf16),
        grad_input,
        grad_pool.reshape(neighbours.shape),
        mine[0],
        mine[1],
        mine[2],
        mine[3],
        mine[4],
        mine[5],
        *d_self[:3],
        *d_cross[:3],
        d_up,
        d_self[3],
        d_cross[3],
        d_down,
    )


def solution(mesh):
    both = P(("dp", "tensor"), None)
    pool = P(("dp", "tensor"), None, None)
    norm = P("dp")
    tall, flat = P("dp", "tensor"), P("tensor", "dp")
    return jax.shard_map(
        functools.partial(on_device, mesh.shape["dp"]),
        mesh=mesh,
        in_specs=(both, pool, P("dp", None)) + (norm,) * 6 + (tall,) * 7 + (flat,) * 3 + (both,),
        out_specs=(both, both, pool) + (norm,) * 6 + (tall,) * 7 + (flat,) * 3,
        check_vma=False,
    )
```

```python
import functools

import jax
import jax.numpy as jnp
import numpy as np
from jax import lax
from jax.experimental import pallas as pl
from jax.experimental.pallas import tpu as pltpu
from jax.sharding import PartitionSpec as P

HEAD_DIM = 64
GROUP = 64
NBR_LEN = 128
NBRS = 2
LANES = 128
NORMS = 6
NEG_FILL = -1e30
EPSILON = 1e-05
GELU_A = 0.7978845608028654
GELU_B = 0.044715
PLANES = 4
BLOCKS = 16
MIB = 2**20

bf16 = jnp.bfloat16
f32 = jnp.float32


def mm(left, right):
    return jnp.dot(left, right, preferred_element_type=f32)


def mm_nt(left, right):
    return lax.dot_general(left, right, (((1,), (1,)), ((), ())), preferred_element_type=f32)


def mm_tn(left, right):
    return lax.dot_general(left, right, (((0,), (0,)), ((), ())), preferred_element_type=f32)


def wide(array):
    return array.astype(f32)


def grid_perms(count):
    steps = {"x": 1, "y": 2, "near": 4, "far": 8}
    return {name: [(i, i ^ step) for i in range(count)] for name, step in steps.items()}


def block_tables(count):
    orders = [
        [4 * z + plane for plane in range(PLANES) for z in (0, 2, 1, 3)],
        [4 * z + plane for z in (0, 2, 1, 3) for plane in range(PLANES)],
    ]
    return np.array([[[device ^ step for step in order] for device in range(count)] for order in orders], np.int32)


def pieces_ok(count, rows):
    return count == BLOCKS and rows % 16 == 0


def tie(arrays, gate=()):
    arrays = tuple(arrays)
    if len(arrays) + len(gate) < 2:
        return arrays
    return lax.optimization_barrier(arrays + tuple(gate))[: len(arrays)]


def stack(*arrays):
    return jnp.concatenate(arrays, axis=0)


class Rounds:
    def __init__(self, count):
        self.perms = grid_perms(count)

    def go(self, gate, *sends):
        out = []
        for array, name in sends:
            (array,) = tie([array], gate)
            out.append(lax.ppermute(array, "dp", self.perms[name]))
        return out


def gather_all(a, b, c, d, count, early):
    if not pieces_ok(count, a.shape[0]):
        gathered = [(lax.all_gather(shard, "dp", axis=0, tiled=True),) for shard in (a, b, c, d)]
        return gathered + [(), (), ()]
    go = Rounds(count).go
    (a_far,) = go((), (a, "far"))
    d_x, d_y = go((a_far,), (d, "x"), (d, "y"))
    a1 = stack(a, a_far)
    r0 = (d_x, d_y)
    r1 = ax1, ay1, a2 = go((), (a1, "x"), (a1, "y"), (a1, "near"))
    (d_d,) = go((), (d_y, "x"))
    (b_far,) = go((a_far, d_x, d_y), (b, "far"))
    b1, column = stack(b, b_far), stack(d, d_x, d_y, d_d)
    r2 = bx1, by1, b2, c_far = go(r0, (b1, "x"), (b1, "y"), (b1, "near"), (c, "far"))
    c1 = stack(c, c_far)
    r3 = ax2, ay2 = go(tuple(r1) + tuple(early), (a2, "x"), (a2, "y"))
    (column_far,) = go(tuple(r1) + (c_far,), (column, "far"))
    r4 = bx2, by2 = go(r2, (b2, "x"), (b2, "y"))
    (column_near,) = go(r2, (column, "near"))
    r5 = ad1, ad2 = go(r3, (ay1, "x"), (ax2, "y"))
    r6 = bd1, bd2, c2 = go(r4, (by1, "x"), (bx2, "y"), (c1, "near"))
    r7 = cx1, cy1 = go(r5, (c1, "x"), (c1, "y"))
    (column_both,) = go(r5, (column_far, "near"))
    r8 = cx2, cy2 = go(r6, (c2, "x"), (c2, "y"))
    cd1, cd2 = go(r7, (cy1, "x"), (cx2, "y"))
    return [
        (a1, a2, ax1, ax2, ay1, ay2, ad1, ad2),
        (b1, b2, bx1, bx2, by1, by2, bd1, bd2),
        (c1, c2, cx1, cx2, cy1, cy2, cd1, cd2),
        (column, column_far, column_near, column_both),
        tuple(r4),
        tuple(r7),
        (column_near,),
    ]


def add_half(own, got):
    return (wide(own) + wide(got)).astype(bf16)


def add_diagonal(x_in, y_in, from_x, from_y, x_out, y_out, x_buf, y_buf, sems):
    half = from_x.shape[0]
    loads = [
        pltpu.make_async_copy(x_in.at[pl.ds(half, half), :], x_buf, sems.at[0]),
        pltpu.make_async_copy(y_in.at[pl.ds(0, half), :], y_buf, sems.at[1]),
    ]
    for load in loads:
        load.start()
    finish(loads)
    x_buf[...] = add_half(x_buf[...], from_y[...])
    y_buf[...] = add_half(y_buf[...], from_x[...])
    stores = [
        pltpu.make_async_copy(x_buf, x_out.at[pl.ds(half, half), :], sems.at[2]),
        pltpu.make_async_copy(y_buf, y_out.at[pl.ds(0, half), :], sems.at[3]),
    ]
    for store in stores:
        store.start()
    finish(stores)


def add_plane(own, got_x, got_y, kept, other):
    half = kept.shape[0]
    total = wide(own[...]) + wide(got_x[...]) + wide(got_y[...])
    kept[...] = total[:half]
    other[...] = total[half:].astype(bf16)


def add_near(kept, got, mine, other):
    rows = mine.shape[0]
    total = kept[...] + wide(got[...])
    mine[...] = total[:rows]
    other[...] = total[rows:].astype(bf16)


def write_outs(turned, total, outs):
    start = 0
    for out, flip in zip(outs, turned):
        if flip:
            columns = max(out.shape[0], LANES)
            out[...] = total[:, start : start + columns].T[: out.shape[0]]
            start += columns
        else:
            out[...] = total[:, start : start + out.shape[1]]
            start += out.shape[1]


def add_far(turned, mine, got, *outs):
    write_outs(turned, mine[...] + wide(got[...]), outs)


class Reduction:
    def __init__(self, pieces, count, widths, turned):
        self.pieces, self.widths, self.turned = pieces, widths, turned
        self.perms = grid_perms(count)
        self.ended = ()
        self.outs = None
        if len(pieces) == 1:
            total = wide(lax.psum_scatter(pieces[0], "dp", scatter_dimension=0, tiled=True))
            self.outs, start = [], 0
            for width, flip in zip(widths, turned):
                part = total[:, start : start + width]
                self.outs.append(part.T if flip else part)
                start += max(width, LANES)

    def out_shapes(self, rows):
        return [((width, rows) if flip else (rows, width), f32) for width, flip in zip(self.widths, self.turned)]

    def move(self, arrays, names, gate):
        out = []
        for array, name in zip(arrays, names):
            (array,) = tie([array], gate)
            out.append(lax.ppermute(array, "dp", self.perms[name]))
        self.ended = tie(out)
        return self.ended

    def diagonal(self, gate=()):
        if self.outs is not None:
            return
        own, x_col, y_col, d_first, d_second = self.pieces
        half, columns = d_first.shape
        from_x, from_y = self.move([d_first, d_second], ["x", "y"], gate)
        buffer = pltpu.VMEM((half, columns), bf16)
        self.sides = pl.pallas_call(
            add_diagonal, name="add_diagonal", out_shape=[pltpu.HBM(x_col.shape, bf16)] * 2,
            in_specs=[HBM, HBM, VMEM, VMEM], out_specs=[HBM, HBM], input_output_aliases={0: 0, 1: 1},
            scratch_shapes=[buffer, buffer, pltpu.SemaphoreType.DMA((4,))],
            compiler_params=pltpu.CompilerParams(vmem_limit_bytes=8 * MIB), cost_estimate=cost(2 * COSTS['add_diagonal']),
        )(x_col, y_col, from_x, from_y)

    def plane(self, gate=()):
        if self.outs is not None:
            return
        half, columns = self.pieces[3].shape
        got_x, got_y = self.move(self.sides, ["x", "y"], gate)
        self.kept, self.other = call(
            add_plane, "add_plane", [], [self.pieces[0], got_x, got_y], [],
            [((half, columns), f32), ((half, columns), bf16)], [], [], 2, mib=10)

    def near(self, gate=()):
        if self.outs is not None:
            return
        half, columns = self.pieces[3].shape
        (got,) = self.move([self.other], ["near"], gate)
        self.mine, self.other = call(
            add_near, "add_near", [], [self.kept, got], [],
            [((half // 2, columns), f32), ((half // 2, columns), bf16)], [], [], 1, mib=8)

    def far(self, gate=(), last=True):
        if self.outs is not None:
            return
        (got,) = self.move([self.other], ["far"], gate)
        self.got_far = got
        if not last:
            return
        shapes = self.out_shapes(self.pieces[3].shape[0] // 2)
        self.outs = call(
            functools.partial(add_far, self.turned), "add_far", [], [self.mine, got], [], shapes, [], [], 1, mib=8)


def add_two(left, right, out):
    out[...] = add_half(left[...], right[...])


def add_column(own, got_near, got_far, mine, x_out, y_out, d_out):
    rows = mine.shape[0]
    total = wide(own[...]) + wide(got_near[...]) + wide(got_far[...])
    mine[...] = total[:rows]
    for place, out in enumerate((x_out, y_out, d_out)):
        out[...] = total[(place + 1) * rows : (place + 2) * rows].astype(bf16)


def add_sides(mine, got_x, got_y, first_mine, first_got, up, down):
    second = mine[...] + wide(got_x[...]) + wide(got_y[...])
    first = first_mine[...] + wide(first_got[...])
    half = up.shape[1] // 2
    for place, out in enumerate((up, down)):
        out[:, :half] = first[:, place * half : (place + 1) * half]
        out[:, half:] = second[:, place * half : (place + 1) * half]


class FlatReduction(Reduction):
    def near(self, gate=()):
        if self.outs is not None:
            return
        own, across, beside, corner = self.pieces
        (got_across,) = self.move([corner], ["near"], gate)
        self.got_across = got_across
        (self.got_own,) = self.move([beside], ["near"], gate)
        (self.across,) = call(add_two, "add_two", [], [across, got_across], [], [(across.shape, bf16)], [], [], 1, mib=8)

    def far(self, gate=()):
        if self.outs is not None:
            return
        (self.got,) = self.move([self.across], ["far"], gate)

    def column(self, gate=()):
        if self.outs is not None:
            return
        own, got = self.pieces[0], self.got
        self.rows = own.shape[0] // PLANES
        block = (self.rows, own.shape[1])
        self.mine, *self.sides = call(
            add_column, "add_column", [], [own, self.got_own, got], [], [(block, f32)] + [(block, bf16)] * 3, [], [], 2, mib=8, gate=gate)

    def diagonal(self, gate=()):
        if self.outs is not None:
            return
        (got,) = self.move([self.sides[2]], ["x"], gate)
        (self.y_side,) = call(add_two, "add_two", [], [self.sides[1], got], [], [(got.shape, bf16)], [], [], 1, mib=8)

    def plane(self, gate=()):
        if self.outs is not None:
            return
        got_x, got_y = self.move([self.sides[0], self.y_side], ["x", "y"], gate)
        self.got_sides = (got_x, got_y)

    def join(self, first):
        if self.outs is not None:
            return
        shape = (self.rows, 2 * self.widths[0])
        self.joined = call(
            add_sides, "add_sides", [], [self.mine, *self.got_sides, first.mine, first.got_far], [], [(shape, f32)] * 2, [], [], 1, mib=8)


def swap_cores(array):
    return lax.ppermute(array, "tensor", [(0, 1), (1, 0)])


def join_cores(array):
    other = swap_cores(array)
    low = lax.axis_index("tensor") == 0
    return jnp.concatenate(
        [jnp.where(low, array, other), jnp.where(low, other, array)], axis=0
    )


def fetch(table, pieces, target, sems, columns, sem_from=0):
    start, size = columns
    copies = []
    if len(pieces) == 1:
        copies.append(
            pltpu.make_async_copy(pieces[0].at[:, pl.ds(start, size)], target, sems.at[sem_from])
        )
    else:
        rows = target.shape[0] // table.shape[0]
        slot = 0
        for piece in pieces:
            for j in range(piece.shape[0] // rows):
                first = pl.multiple_of(table[slot] * rows, 16)
                copies.append(
                    pltpu.make_async_copy(
                        piece.at[pl.ds(j * rows, rows), pl.ds(start, size)],
                        target.at[pl.ds(first, rows), :],
                        sems.at[sem_from + slot],
                    )
                )
                slot += 1
    for copy in copies:
        copy.start()
    return copies


def put(table, source, pieces, sems, columns, sem_from=0):
    start, size = columns
    copies = []
    if len(pieces) == 1:
        copies.append(
            pltpu.make_async_copy(source, pieces[0].at[:, pl.ds(start, size)], sems.at[sem_from])
        )
    else:
        rows = source.shape[0] // table.shape[0]
        slot = 0
        for piece in pieces:
            for j in range(piece.shape[0] // rows):
                first = pl.multiple_of(table[slot] * rows, 16)
                copies.append(
                    pltpu.make_async_copy(
                        source.at[pl.ds(first, rows), :],
                        piece.at[pl.ds(j * rows, rows), pl.ds(start, size)],
                        sems.at[sem_from + slot],
                    )
                )
                slot += 1
    for copy in copies:
        copy.start()
    return copies


def finish(copies):
    for copy in copies:
        copy.wait()


def norm_parts(stream):
    center = stream - jnp.mean(stream, axis=-1, keepdims=True)
    spread = jnp.mean(center * center, axis=-1, keepdims=True)
    scale = lax.rsqrt(spread + EPSILON)
    return center * scale, scale


def norm_back(grad, normal, scale, gain):
    inner = grad * gain
    return scale * (
        inner
        - jnp.mean(inner, axis=-1, keepdims=True)
        - normal * jnp.mean(inner * normal, axis=-1, keepdims=True)
    )


def turn(pair, cosine, sine):
    lane = lax.broadcasted_iota(jnp.int32, pair.shape, 1)
    low_half = lane % HEAD_DIM < HEAD_DIM // 2
    partner = jnp.where(
        low_half,
        pltpu.roll(pair, LANES - HEAD_DIM // 2, 1),
        pltpu.roll(pair, HEAD_DIM // 2, 1),
    )
    return pair * cosine + partner * sine


def stack_heads(pair):
    lane = lax.broadcasted_iota(jnp.int32, pair.shape, 1)
    zero = jnp.zeros_like(pair)
    return jnp.concatenate(
        [jnp.where(lane < HEAD_DIM, pair, zero), jnp.where(lane < HEAD_DIM, zero, pair)], axis=0
    )


def merge_heads(stacked):
    rows = stacked.shape[0] // 2
    lane = lax.broadcasted_iota(jnp.int32, (rows, stacked.shape[1]), 1)
    return jnp.where(lane < HEAD_DIM, stacked[:rows], stacked[rows:])


def softmax_low(scores):
    raised = jnp.exp(scores - jnp.max(scores, axis=-1, keepdims=True))
    return (raised * (1.0 / jnp.sum(raised, axis=-1, keepdims=True))).astype(bf16)


def pairs_of(width):
    return [(pair, slice(pair * LANES, (pair + 1) * LANES)) for pair in range(width // LANES)]


SCALE = HEAD_DIM ** (-0.5)


def self_forward(count, table, x_ref, cos_ref, sin_ref, *refs):
    pieces, refs = refs[:count], refs[count:]
    part, h_out, q_out, k_out, v_out, p_out, o_out, norms_out, weights, sems = refs
    width = q_out.shape[1]
    copies = fetch(table, pieces, weights.buffer, sems, (0, weights.shape[1]))
    normal, _ = norm_parts(wide(x_ref[...]))
    finish(copies)
    send(weights)
    rows = wide(weights[:, :LANES]).T[:8]
    norms_out[...] = rows
    hidden = (normal * rows[0:1] + rows[1:2]).astype(bf16)
    h_out[...] = hidden
    send(h_out)
    mixed = mm(hidden, weights[:, LANES : LANES + 3 * width])
    cosine, sine = cos_ref[...], sin_ref[...]
    count_rows = hidden.shape[0]
    query_pos = lax.broadcasted_iota(jnp.int32, (2 * count_rows, count_rows), 0) % count_rows
    allowed = query_pos >= lax.broadcasted_iota(jnp.int32, (2 * count_rows, count_rows), 1)
    for pair, lanes in pairs_of(width):
        queries = turn(mixed[:, lanes], cosine, sine).astype(bf16)
        keys = turn(mixed[:, width + pair * LANES : width + (pair + 1) * LANES], cosine, sine).astype(bf16)
        values = mixed[:, 2 * width + pair * LANES : 2 * width + (pair + 1) * LANES].astype(bf16)
        q_out[:, lanes] = queries
        k_out[:, lanes] = keys
        v_out[:, lanes] = values
        scores = jnp.where(allowed, mm_nt(stack_heads(queries), keys) * SCALE, NEG_FILL)
        attend = softmax_low(scores)
        p_out[pair] = attend
        o_out[:, lanes] = merge_heads(mm(attend, values)).astype(bf16)
    send(q_out, k_out, v_out, p_out, o_out)
    part[...] = mm_nt(o_out[...], weights[:, LANES + 3 * width :]).astype(bf16)


def pool_forward(count, table, pool_ref, *refs):
    pieces, refs = refs[:count], refs[count:]
    k_out, v_out, weights, sems = refs
    width = k_out.shape[1]
    finish(fetch(table, pieces, weights.buffer, sems, (width, 2 * width)))
    send(weights)
    mixed = mm(pool_ref[...], weights[...])
    k_out[...] = mixed[:, :width].astype(bf16)
    v_out[...] = mixed[:, width:].astype(bf16)


def chosen_rows(chosen, block, ref, lanes):
    return jnp.concatenate(
        [
            ref[pl.ds(pl.multiple_of(chosen[NBRS * block + j] * NBR_LEN, NBR_LEN), NBR_LEN), lanes]
            for j in range(NBRS)
        ],
        axis=0,
    )


def cross_forward(count, table, chosen, x_ref, own_ref, got_ref, norms, k_ref, v_ref, *refs):
    pieces, refs = refs[:count], refs[count:]
    part, x_out, h_out, q_out, p_out, o_out, in_w, out_w, sems, sems_out = refs
    width = q_out.shape[1]
    copies = fetch(table, pieces, in_w.buffer, sems, (0, width))
    copies_out = fetch(table, pieces, out_w.buffer, sems_out, (3 * width, width))
    stream = wide(x_ref[...]) + (wide(own_ref[...]) + wide(got_ref[...]))
    x_out[...] = stream
    send(x_out)
    normal, _ = norm_parts(stream)
    hidden = (normal * norms[2:3] + norms[3:4]).astype(bf16)
    h_out[...] = hidden
    send(h_out)
    finish(copies)
    send(in_w)
    queries = mm(hidden, in_w[...]).astype(bf16)
    q_out[...] = queries
    pair_count = width // LANES
    for block in range(queries.shape[0] // GROUP):
        rows = slice(block * GROUP, (block + 1) * GROUP)
        for pair, lanes in pairs_of(width):
            keys = chosen_rows(chosen, block, k_ref, lanes)
            values = chosen_rows(chosen, block, v_ref, lanes)
            attend = softmax_low(mm_nt(stack_heads(queries[rows, lanes]), keys) * SCALE)
            p_out[block * pair_count + pair] = attend
            o_out[rows, lanes] = merge_heads(mm(attend, values)).astype(bf16)
    finish(copies_out)
    send(out_w, q_out, p_out, o_out)
    part[...] = mm_nt(o_out[...], out_w[...]).astype(bf16)


def feed_forward(count, grad_count, slices, leading, table, grad_table, side, x_ref, norms, g_ref, one_ref, two_ref, *refs):
    pieces, refs = refs[:count], refs[count:]
    results = refs[:3]
    grads, refs = refs[3 : 3 + grad_count], refs[3 + grad_count :]
    up_w, down_w, up_g, down_g, *full, sems, sems_out = refs
    total = up_w.shape[0] * up_w.shape[2]
    size = total // slices
    block_count = table.shape[0] if count > 1 else 1
    copies = []
    for turn_of in range(slices):
        copies.append(
            fetch(table, pieces, up_w.at[turn_of], sems, (turn_of * size, size), 2 * turn_of * block_count)
            + fetch(table, pieces, down_w.at[turn_of], sems, (total + turn_of * size, size), (2 * turn_of + 1) * block_count)
        )
    if leading:
        stream = wide(x_ref[...]) + (wide(one_ref[...]) + wide(two_ref[...]))
        results[0][...] = stream
        send(results[0])
    else:
        stream = x_ref[...]
    normal, _ = norm_parts(stream)
    hidden = (normal * norms[4:5] + norms[5:6]).astype(bf16)
    grad = g_ref[...]
    hidden_t, grad_t = hidden.T, grad.T
    kept = results[1:] if leading else full
    sent = []
    for turn_of in range(slices):
        finish(copies[turn_of])
        pre = mm(hidden, up_w[turn_of])
        grad_act = mm(grad, down_w[turn_of])
        square = pre * pre
        bend = jnp.tanh(GELU_A * (pre + GELU_B * square * pre))
        gate = 0.5 * (1.0 + bend)
        act = (pre * gate).astype(bf16)
        slope = gate + 0.5 * pre * (1.0 - bend * bend) * (GELU_A * (1.0 + 3.0 * GELU_B * square))
        grad_pre = (grad_act * slope).astype(bf16)
        up_g[turn_of] = mm(hidden_t, grad_pre).astype(bf16)
        down_g[turn_of] = mm(grad_t, act).astype(bf16)
        sent += put(grad_table, up_g.at[turn_of], grads, sems_out, (turn_of * size, size), 2 * turn_of * block_count)
        sent += put(grad_table, down_g.at[turn_of], grads, sems_out, (total + turn_of * size, size), (2 * turn_of + 1) * block_count)
        more, less = mm_nt(act, down_w[turn_of]), mm_nt(grad_pre, up_w[turn_of])
        for keep, add, given in zip(kept, (more, less), (one_ref, two_ref)):
            base = keep[...] if turn_of else None if leading else given[...]
            keep[...] = add if base is None else base + add
    if not leading:
        results[2][...] = full[1][...].astype(bf16)
        full[1][...] = full[0][...] + stream
        half = results[0].shape[0]
        results[0][...] = full[1][pl.ds(pl.multiple_of(side[0] * half, half), half), :]
        results[1][...] = full[0][pl.ds(pl.multiple_of((1 - side[0]) * half, half), half), :].astype(bf16)
    finish(sent)


def attention_back(stacked_grad, outputs, attend, keys, values, stacked_queries):
    both = jnp.concatenate([outputs, outputs], axis=0)
    inner = jnp.sum(wide(stacked_grad) * wide(both), axis=-1, keepdims=True)
    grad_scores = (wide(attend) * (mm_nt(stacked_grad, values) - inner)).astype(bf16)
    grad_q = merge_heads(mm(grad_scores, keys)) * SCALE
    grad_k = mm_tn(grad_scores, stacked_queries) * SCALE
    grad_v = mm_tn(attend, stacked_grad)
    return grad_q, grad_k, grad_v


def cross_back(chosen, own_ref, got_ref, norms, x_ref, g_ref, out_w, o_ref, p_ref, v_ref, k_ref, q_ref, in_w, *refs):
    dx_out, low_out, dh_out, dq_out, dk_out, dv_out, sums_out, dk_acc, dv_acc = refs
    width = q_ref.shape[1]
    normal, scale = norm_parts(x_ref[...])
    grad = wide(own_ref[...]) + wide(got_ref[...])
    dx = wide(g_ref[...]) + norm_back(grad, normal, scale, norms[4:5])
    dx_out[...] = dx
    send(dx_out)
    sums_out[0:1] = jnp.sum(grad * normal, axis=0, keepdims=True)
    sums_out[1:2] = jnp.sum(grad, axis=0, keepdims=True)
    low = dx.astype(bf16)
    low_out[...] = low
    send(low_out)
    dk_acc[...] = jnp.zeros_like(dk_acc)
    dv_acc[...] = jnp.zeros_like(dv_acc)
    grad_mix = mm(low, out_w[...]).astype(bf16)
    pair_count = width // LANES
    for block in range(low.shape[0] // GROUP):
        rows = slice(block * GROUP, (block + 1) * GROUP)
        for pair, lanes in pairs_of(width):
            keys = chosen_rows(chosen, block, k_ref, lanes)
            values = chosen_rows(chosen, block, v_ref, lanes)
            grad_q, grad_k, grad_v = attention_back(
                stack_heads(grad_mix[rows, lanes]),
                o_ref[rows, lanes],
                p_ref[block * pair_count + pair],
                keys,
                values,
                stack_heads(q_ref[rows, lanes]),
            )
            dq_out[rows, lanes] = grad_q.astype(bf16)
            for j in range(NBRS):
                place = pl.ds(pl.multiple_of(chosen[NBRS * block + j] * NBR_LEN, NBR_LEN), NBR_LEN)
                part = slice(j * NBR_LEN, (j + 1) * NBR_LEN)
                dk_acc[place, lanes] += grad_k[part]
                dv_acc[place, lanes] += grad_v[part]
    dk_out[...] = dk_acc[...].astype(bf16)
    dv_out[...] = dv_acc[...].astype(bf16)
    send(dq_out, dk_out, dv_out)
    dh_out[...] = mm_nt(dq_out[...], in_w[...]).astype(bf16)


def cross_weights(grad_count, table, side, h_ref, dq_ref, pool_ref, dk_ref, dv_ref, low_ref, o_ref, weights, *refs):
    pool_out, pool_other = refs[:2]
    grads, refs = refs[2 : 2 + grad_count], refs[2 + grad_count :]
    made, full, sems_out = refs
    width = dq_ref.shape[1]
    block_count = table.shape[0] if grad_count > 1 else 1
    sent = []

    def leave(part):
        sent.extend(put(table, made.at[part], grads, sems_out, (part * width, width), part * block_count))

    made[0] = mm_tn(h_ref[...], dq_ref[...]).astype(bf16)
    leave(0)
    pool_t = pool_ref[...].T
    made[1] = mm(pool_t, dk_ref[...]).astype(bf16)
    leave(1)
    made[2] = mm(pool_t, dv_ref[...]).astype(bf16)
    leave(2)
    made[3] = mm_tn(low_ref[...], o_ref[...]).astype(bf16)
    leave(3)
    full[...] = mm_nt(dk_ref[...], weights[:, :width]) + mm_nt(dv_ref[...], weights[:, width:])
    half = pool_out.shape[0]
    pool_out[...] = full[pl.ds(pl.multiple_of(side[0] * half, half), half), :].astype(bf16)
    pool_other[...] = full[pl.ds(pl.multiple_of((1 - side[0]) * half, half), half), :].astype(bf16)
    finish(sent)


def self_back(own_ref, got_ref, norms, x_ref, dx_ref, weights, o_ref, p_ref, v_ref, k_ref, q_ref, cos_ref, sin_ref, *refs):
    dx_out, low_out, dh_out, dq_out, dk_out, dv_out, sums_out = refs
    width = q_ref.shape[1]
    normal, scale = norm_parts(x_ref[...])
    grad = wide(own_ref[...]) + wide(got_ref[...])
    dx = dx_ref[...] + norm_back(grad, normal, scale, norms[2:3])
    dx_out[...] = dx
    send(dx_out)
    sums_out[0:1] = jnp.sum(grad * normal, axis=0, keepdims=True)
    sums_out[1:2] = jnp.sum(grad, axis=0, keepdims=True)
    low = dx.astype(bf16)
    low_out[...] = low
    send(low_out)
    grad_mix = mm(low, weights[:, LANES + 3 * width :]).astype(bf16)
    cosine, sine = cos_ref[...], -sin_ref[...]
    for pair, lanes in pairs_of(width):
        grad_q, grad_k, grad_v = attention_back(
            stack_heads(grad_mix[:, lanes]),
            o_ref[:, lanes],
            p_ref[pair],
            k_ref[:, lanes],
            v_ref[:, lanes],
            stack_heads(q_ref[:, lanes]),
        )
        dq_out[:, lanes] = turn(grad_q, cosine, sine).astype(bf16)
        dk_out[:, lanes] = turn(grad_k, cosine, sine).astype(bf16)
        dv_out[:, lanes] = grad_v.astype(bf16)
    send(dq_out, dk_out, dv_out)
    dh_out[...] = (
        mm_nt(dq_out[...], weights[:, LANES : LANES + width])
        + mm_nt(dk_out[...], weights[:, LANES + width : LANES + 2 * width])
        + mm_nt(dv_out[...], weights[:, LANES + 2 * width : LANES + 3 * width])
    ).astype(bf16)


def self_weights(grad_count, table, one_ref, two_ref, three_ref, h_ref, dq_ref, dk_ref, dv_ref, low_ref, o_ref, *refs):
    grads, refs = refs[:grad_count], refs[grad_count:]
    made, norms, sems_out, sems_norm = refs
    width = dq_ref.shape[1]
    block_count = table.shape[0] if grad_count > 1 else 1
    sent = []

    def leave(part):
        sent.extend(put(table, made.at[part], grads, sems_out, (part * width, width), part * block_count))

    sums = [one_ref[:2], two_ref[:2], three_ref[:2], jnp.zeros((LANES - NORMS, one_ref.shape[1]), f32)]
    norms[...] = jnp.concatenate(sums, axis=0).T.astype(bf16)
    sent += put(table, norms, grads, sems_norm, (4 * width, LANES))
    hidden_t = h_ref[...].T
    for part, grad in enumerate((dq_ref, dk_ref, dv_ref)):
        made[part] = mm(hidden_t, grad[...]).astype(bf16)
        leave(part)
    made[3] = mm_tn(low_ref[...], o_ref[...]).astype(bf16)
    leave(3)
    finish(sent)


def input_back(side, dx_ref, x_ref, norms, own_ref, got_ref, dx_out, sums_out, full):
    normal, scale = norm_parts(wide(x_ref[...]))
    grad = wide(own_ref[...]) + wide(got_ref[...])
    full[...] = dx_ref[...] + norm_back(grad, normal, scale, norms[0:1])
    half = dx_out.shape[0]
    dx_out[...] = full[pl.ds(pl.multiple_of(side[0] * half, half), half), :]
    sums_out[0:1] = jnp.sum(grad * normal, axis=0, keepdims=True)
    sums_out[1:2] = jnp.sum(grad, axis=0, keepdims=True)


SMEM = pl.BlockSpec(memory_space=pltpu.SMEM)
VMEM = pl.BlockSpec(memory_space=pltpu.VMEM)
ANY = pl.BlockSpec(memory_space=pl.ANY)
HBM = pl.BlockSpec(memory_space=pltpu.HBM)


def cost(microseconds):
    return pl.CostEstimate(flops=int(microseconds * 1.1e9), bytes_accessed=0, transcendentals=0)


class Arriving:
    def __init__(self, source, buffer, sem):
        self.copy = pltpu.make_async_copy(source, buffer, sem)
        self.copy.start()
        self.buffer, self.shape, self.waiting = buffer, buffer.shape, True

    def __getitem__(self, index):
        if self.waiting:
            self.copy.wait()
            self.waiting = False
        return self.buffer[index]


class Leaving:
    def __init__(self, buffer, target, sem):
        self.copy = pltpu.make_async_copy(buffer, target, sem)
        self.buffer, self.shape, self.dtype, self.sent = buffer, buffer.shape, buffer.dtype, False

    def __getitem__(self, index):
        return self.buffer[index]

    def __setitem__(self, index, value):
        self.buffer[index] = value

    def send(self):
        if not self.sent:
            self.copy.start()
            self.sent = True


def send(*results):
    for result in results:
        if isinstance(result, Leaving):
            result.send()


def streamed(body, counts, far_in, far_out, *refs):
    scalars, arrays, pieces, outs, grads, own = counts
    parts, start = [], 0
    for size in (scalars, arrays, pieces, outs, grads, own, len(far_in), len(far_out), 2):
        parts.append(list(refs[start : start + size]))
        start += size
    scalars, arrays, pieces, outs, grads, own, in_buffers, out_buffers, (in_sems, out_sems) = parts
    for place, index in enumerate(far_in):
        arrays[index] = Arriving(arrays[index], in_buffers[place], in_sems.at[place])
    for place, index in enumerate(far_out):
        outs[index] = Leaving(out_buffers[place], outs[index], out_sems.at[place])
    body(*scalars, *arrays, *pieces, *outs, *grads, *own)
    for index in far_in:
        if arrays[index].waiting:
            arrays[index].copy.wait()
    for index in far_out:
        outs[index].send()
    for index in far_out:
        outs[index].copy.wait()


COSTS = {"self_forward": 0.7, "pool_forward": 0.7, "cross_forward": 0.7, "feed_forward": 0.7, "cross_back": 0.7, "cross_weights": 0.7, "self_back": 0.7, "self_weights": 0.7, "input_back": 0.7, "adds": 0.7, "add_diagonal": 0.7, "pack_self": 0.7}


def call(body, name, scalars, arrays, pieces, outs, grads, scratch, microseconds, mib=20, gate=(), far=()):
    if gate:
        arrays = list(tie(arrays, gate))
    shapes = [pltpu.HBM(*out[:2]) if len(out) > 2 else jax.ShapeDtypeStruct(*out) for out in outs]
    shapes += [pltpu.HBM(shape, dtype) for shape, dtype in grads]
    far = list(far)
    far_out = [index for index, out in enumerate(outs) if len(out) > 2]
    scratch = list(scratch)
    if far or far_out:
        counts = (len(scalars), len(arrays), len(pieces), len(outs), len(grads), len(scratch))
        body = functools.partial(streamed, body, counts, far, far_out)
        scratch += [pltpu.VMEM(arrays[index].shape, arrays[index].dtype) for index in far]
        scratch += [pltpu.VMEM(*outs[index][:2]) for index in far_out]
        scratch += [pltpu.SemaphoreType.DMA((max(len(some), 1),)) for some in (far, far_out)]
    return pl.pallas_call(
        body,
        name=name,
        out_shape=shapes,
        in_specs=[SMEM] * len(scalars)
        + [HBM if index in far else VMEM for index in range(len(arrays))]
        + [ANY] * len(pieces),
        out_specs=[HBM if index in far_out else VMEM for index in range(len(outs))] + [HBM] * len(grads),
        scratch_shapes=scratch,
        compiler_params=pltpu.CompilerParams(vmem_limit_bytes=mib * MIB),
        cost_estimate=cost(COSTS['adds' if name.startswith('add_') else name] * microseconds),
    )(*scalars, *arrays, *pieces)


def rope_tables(rows):
    half = HEAD_DIM // 2
    frequency = np.power(np.float32(10000.0), -np.arange(half, dtype=np.float32) / np.float32(half))
    angles = np.arange(rows, dtype=np.float32)[:, None] * frequency[None, :]
    cosine, sine = np.cos(angles), np.sin(angles)
    return (
        jnp.asarray(np.concatenate([cosine] * 4, axis=1), f32),
        jnp.asarray(np.concatenate([-sine, sine] * 2, axis=1), f32),
    )


def dma_sems(count, uses=1):
    blocks = BLOCKS if count > 1 else 1
    return pltpu.SemaphoreType.DMA((blocks * uses,))


def pack(*columns):
    return jnp.concatenate([column.astype(bf16) for column in columns], axis=1)


def pack_kernel(*refs):
    norms, (query, key, value, out_w, packed) = refs[:NORMS], refs[NORMS:]
    rows, width = query.shape
    lines = [norm[...] for norm in norms] + [jnp.zeros((LANES - NORMS, rows), f32)]
    packed[:, :LANES] = jnp.concatenate(lines, axis=0).T.astype(bf16)
    for place, ref in enumerate((query, key, value)):
        packed[:, LANES + place * width : LANES + (place + 1) * width] = ref[...].astype(bf16)
    packed[:, LANES + 3 * width :] = out_w[...].astype(bf16)


def pack_self(norms, query, key, value, out_w, fast):
    if not fast:
        lines = jnp.pad(jnp.stack(norms, axis=1), ((0, 0), (0, LANES - NORMS)))
        return pack(lines, query, key, value, out_w)
    lines = [norm.reshape(1, -1) for norm in norms]
    shape = (query.shape[0], LANES + 4 * query.shape[1])
    return call(pack_kernel, "pack_self", [], lines + [query, key, value, out_w], [], [(shape, bf16)], [], [], 2, mib=60)[0]


def on_device(count, inputs, neighbours, nbr_index, ln1_gain, ln1_bias, ln2_gain, ln2_bias, ln3_gain, ln3_bias,
              w_query, w_key, w_value, c_query, c_key, c_value, w_up, w_out, c_out, w_down, cotangent):
    width, hidden = w_query.shape[1], w_up.shape[1]
    shard_rows = w_query.shape[0]
    model = shard_rows * count
    rows = 2 * inputs.shape[0]
    norms = [ln1_gain, ln1_bias, ln2_gain, ln2_bias, ln3_gain, ln3_bias]

    stream = join_cores(inputs)
    cot = join_cores(cotangent)
    pool = join_cores(neighbours.reshape(-1, neighbours.shape[-1]))
    down_t = w_down.T
    part_hidden = hidden // 2
    cuts = [slice(0, part_hidden), slice(part_hidden, hidden)]
    self_w, cross_w, *ff_w, gate_self, gate_pool, gate_cross = gather_all(
        pack_self(norms, w_query, w_key, w_value, w_out.T, pieces_ok(count, shard_rows)),
        pack(c_query, c_key, c_value, c_out.T),
        pack(w_up[:, cuts[0]], down_t[:, cuts[0]]),
        pack(w_up[:, cuts[1]], down_t[:, cuts[1]]),
        count,
        (stream, cot, pool),
    )
    ff_w = ff_w[::-1]
    side = lax.axis_index("tensor").astype(jnp.int32).reshape(1)
    pieces = len(self_w)
    if pieces > 1:
        tables = jnp.asarray(block_tables(count))
        table, flat_table = (tables[i][lax.axis_index("dp")] for i in range(2))
        grad_rows = [shard_rows * blocks for blocks in (4, 4, 4, 2, 2)]
        flat_rows = [shard_rows * PLANES] * 4
    else:
        table = flat_table = jnp.zeros((1,), jnp.int32)
        grad_rows = flat_rows = [model]
    grad_count = len(grad_rows)

    def bind(body, *extra):
        return functools.partial(body, pieces, *extra)

    pool_rows = pool.shape[0]
    chosen = nbr_index.reshape(-1)
    cosine, sine = rope_tables(rows)
    pairs = width // LANES
    blocks = rows // GROUP
    tall, low = ((rows, model), f32), ((rows, model), bf16)
    slim = ((rows, width), bf16)
    rank8 = ((8, model), f32)
    half_tall, half_low = ((rows // 2, model), f32), ((rows // 2, model), bf16)

    def kept(out):
        return out + ("hbm",)


    part, h_one, queries, keys, values, attend, mixture, norm_rows, self_full = call(
        bind(self_forward), "self_forward", [table], [stream, cosine, sine], self_w,
        [low, kept(low), kept(slim), kept(slim), kept(slim), kept(((pairs, 2 * rows, rows), bf16)), kept(slim), rank8, kept(((model, LANES + 4 * width), bf16))], [],
        [dma_sems(pieces)], 8, mib=60, gate=gate_self, far=[0, 1, 2])
    got = swap_cores(part)
    ckeys, cvalues, cross_full = call(
        bind(pool_forward), "pool_forward", [table], [pool], cross_w,
        [kept(((pool_rows, width), bf16))] * 2 + [kept(((model, 2 * width), bf16))], [],
        [dma_sems(pieces)], 3, mib=60, gate=gate_pool, far=[0])
    part, after_self, h_two, cqueries, cattend, cmixture, cquery_full, cout_full = call(
        bind(cross_forward), "cross_forward", [table, chosen], [stream, part, got, norm_rows, ckeys, cvalues], cross_w,
        [low, kept(tall), kept(low), kept(slim), kept(((blocks * pairs, 2 * GROUP, NBRS * NBR_LEN), bf16)), kept(slim)] + [kept(((model, width), bf16))] * 2, [],
        [dma_sems(pieces), dma_sems(pieces)], 6, mib=60, gate=gate_cross, far=[0, 4, 5])
    got = swap_cores(part)
    slices = 2
    size = part_hidden // slices
    def ff_call(leading, ff_pieces, from_table, to_table, to_rows, arrays, outs, far):
        wide_scratch = [] if leading else [pltpu.VMEM((rows, model), f32)] * 2
        results = call(
            functools.partial(feed_forward, len(ff_pieces), len(to_rows), slices, leading), "feed_forward",
            [from_table, to_table, side], arrays, ff_pieces, outs, [((count_of, 2 * part_hidden), bf16) for count_of in to_rows],
            [pltpu.VMEM((slices, model, size), bf16)] * 4 + wide_scratch + [dma_sems(pieces, 2 * slices)] * 2, 10,
            mib=34, far=far)
        return *results[:3], results[3:]

    after_cross, out, back, last_grads = ff_call(
        True, ff_w[0], flat_table, flat_table, flat_rows, [after_self, norm_rows, cot, part, got],
        [kept(tall)] * 3, [0, 2])
    result, result_other, back, first_grads = ff_call(
        False, ff_w[1], table, table, grad_rows, [after_cross, norm_rows, cot, out, back], [half_tall, half_low, low], [0, 2, 3, 4])
    ff_grads = [last_grads, first_grads]
    grad_part = back
    got = swap_cores(grad_part)
    ff_widths, ff_turned = [part_hidden] * 2, [False, False]
    one = FlatReduction(ff_grads[0], count, ff_widths, ff_turned)
    two = Reduction(ff_grads[1], count, ff_widths, ff_turned)
    one.near()
    two.diagonal()
    two.plane()
    one.far()
    acc = pltpu.VMEM((pool_rows, width), f32)
    grad_cross, low_cross, grad_part, dcq, dck, dcv, sums_three = call(
        cross_back, "cross_back", [chosen],
        [grad_part, got, norm_rows, after_cross, cot, cout_full, cmixture, cattend, cvalues, ckeys, cqueries, cquery_full], [],
        [kept(tall), kept(low), low, kept(slim), kept(((pool_rows, width), bf16)), kept(((pool_rows, width), bf16)), rank8], [],
        [acc, acc], 8, mib=24, gate=(one.got_across,) if pieces > 1 else (), far=range(3, 12))
    got = swap_cores(grad_part)
    pool_part, pool_other, *cross_grads = call(
        functools.partial(cross_weights, grad_count), "cross_weights", [table, side],
        [h_two, dcq, pool, dck, dcv, low_cross, cmixture, cross_full], [],
        [((pool_rows // 2, model), bf16)] * 2, [((count_of, 4 * width), bf16) for count_of in grad_rows],
        [pltpu.VMEM((4, model, width), bf16), pltpu.VMEM((pool_rows, model), f32), dma_sems(pieces, 4)],
        8, mib=24, gate=(one.got_own,) if pieces > 1 else (), far=range(8))
    grad_self, low_self, grad_part, dq, dk, dv, sums_two = call(
        self_back, "self_back", [],
        [grad_part, got, norm_rows, after_self, grad_cross, self_full, mixture, attend, values, keys, queries, cosine, sine], [],
        [kept(tall), kept(low), low, kept(slim), kept(slim), kept(slim), rank8], [],
        [], 7, mib=20, gate=tuple(two.sides) + (one.across,) if pieces > 1 else (), far=range(3, 13))
    got = swap_cores(grad_part)
    three = Reduction(cross_grads, count, [width] * 4, [False] * 4)
    three.diagonal()
    grad_input, sums_one = call(
        input_back, "input_back", [side], [grad_self, stream, norm_rows, grad_part, got], [], [half_tall, rank8], [],
        [pltpu.VMEM((rows, model), f32)], 2, mib=12, far=[0, 1])
    self_grads = call(
        functools.partial(self_weights, grad_count), "self_weights", [table],
        [sums_one, sums_two, sums_three, h_one, dq, dk, dv, low_self, mixture], [],
        [], [((count_of, 4 * width + LANES), bf16) for count_of in grad_rows],
        [pltpu.VMEM((4, model, width), bf16), pltpu.VMEM((model, LANES), bf16), dma_sems(pieces, 4), dma_sems(pieces)], 4,
        mib=16, gate=(two.ended) if pieces > 1 else (), far=range(3, 9))
    four = Reduction(self_grads, count, [width] * 4 + [8], [False] * 4 + [True])
    one.column((self_grads[-1],))
    one.diagonal()
    sent_one = one.ended
    two.near()
    four.diagonal(())
    one.plane()
    three.plane(sent_one)
    four.plane(two.ended + sent_one)
    two.far((), False)
    three.near()
    four.near((two.got_far,) if pieces > 1 else ())
    three.far()
    four.far(three.ended)
    one.join(two)
    d_cross, d_self = three.outs, four.outs
    if pieces > 1:
        d_up, d_down = one.joined
    else:
        d_up, d_down = (jnp.concatenate([two.outs[i], one.outs[i]], axis=1) for i in range(2))
    grad_pool = wide(pool_part) + wide(swap_cores(pool_other))
    mine = d_self[4]
    return (
        (result + wide(swap_cores(result_other))).astype(bf16),
        grad_input,
        grad_pool.reshape(neighbours.shape),
        mine[0],
        mine[1],
        mine[2],
        mine[3],
        mine[4],
        mine[5],
        *d_self[:3],
        *d_cross[:3],
        d_up,
        d_self[3].T,
        d_cross[3].T,
        d_down.T,
    )


def solution(mesh):
    both = P(("dp", "tensor"), None)
    pool = P(("dp", "tensor"), None, None)
    norm = P("dp")
    tall, flat = P("dp", "tensor"), P("tensor", "dp")
    return jax.shard_map(
        functools.partial(on_device, mesh.shape["dp"]),
        mesh=mesh,
        in_specs=(both, pool, P("dp", None)) + (norm,) * 6 + (tall,) * 7 + (flat,) * 3 + (both,),
        out_specs=(both, both, pool) + (norm,) * 6 + (tall,) * 7 + (flat,) * 3,
        check_vma=False,
    )
```

```python
import functools

import jax
import jax.numpy as jnp
import numpy as np
from jax import lax
from jax.experimental import pallas as pl
from jax.experimental.pallas import tpu as pltpu
from jax.sharding import PartitionSpec as P

HEAD_DIM = 64
GROUP = 64
NBR_LEN = 128
NBRS = 2
LANES = 128
NORMS = 6
NEG_FILL = -1e30
EPSILON = 1e-05
GELU_A = 0.7978845608028654
GELU_B = 0.044715
PLANES = 4
BLOCKS = 16
MIB = 2**20

bf16 = jnp.bfloat16
f32 = jnp.float32


def mm(left, right):
    return jnp.dot(left, right, preferred_element_type=f32)


def mm_nt(left, right):
    return lax.dot_general(left, right, (((1,), (1,)), ((), ())), preferred_element_type=f32)


def mm_tn(left, right):
    return lax.dot_general(left, right, (((0,), (0,)), ((), ())), preferred_element_type=f32)


def wide(array):
    return array.astype(f32)


def grid_perms(count):
    steps = {"x": 1, "y": 2, "near": 4, "far": 8}
    return {name: [(i, i ^ step) for i in range(count)] for name, step in steps.items()}


def block_tables(count):
    orders = [
        [4 * z + plane for plane in range(PLANES) for z in (0, 2, 1, 3)],
        [4 * z + plane for z in (0, 2, 1, 3) for plane in range(PLANES)],
    ]
    return np.array([[[device ^ step for step in order] for device in range(count)] for order in orders], np.int32)


def pieces_ok(count, rows):
    return count == BLOCKS and rows % 16 == 0


def tie(arrays, gate=()):
    arrays = tuple(arrays)
    if len(arrays) + len(gate) < 2:
        return arrays
    return lax.optimization_barrier(arrays + tuple(gate))[: len(arrays)]


def stack(*arrays):
    return jnp.concatenate(arrays, axis=0)


class Rounds:
    def __init__(self, count):
        self.perms = grid_perms(count)

    def go(self, gate, *sends):
        out = []
        for array, name in sends:
            (array,) = tie([array], gate)
            out.append(lax.ppermute(array, "dp", self.perms[name]))
        return out


def gather_all(a, b, c, d, count, early):
    if not pieces_ok(count, a.shape[0]):
        gathered = [(lax.all_gather(shard, "dp", axis=0, tiled=True),) for shard in (a, b, c, d)]
        return gathered + [(), (), ()]
    go = Rounds(count).go
    (a_far,) = go((), (a, "far"))
    d_x, d_y = go((a, early[0]), (d, "x"), (d, "y"))
    a1 = stack(a, a_far)
    r0 = (d_x, d_y)
    r1 = ax1, ay1, a2 = go((), (a1, "x"), (a1, "y"), (a1, "near"))
    (d_d,) = go((), (d_y, "x"))
    (b_far,) = go((a_far, d_y), (b, "far"))
    b1, column = stack(b, b_far), stack(d, d_x, d_y, d_d)
    r2 = bx1, by1, b2, c_far = go(r0 + (ay1,), (b1, "x"), (b1, "y"), (b1, "near"), (c, "far"))
    c1 = stack(c, c_far)
    r3 = ax2, ay2 = go(tuple(r1) + tuple(early), (a2, "x"), (a2, "y"))
    (column_far,) = go(tuple(r1) + (c_far,), (column, "far"))
    r4 = bx2, by2 = go(r2, (b2, "x"), (b2, "y"))
    (column_near,) = go(r4, (column, "near"))
    r5 = ad1, ad2 = go(r3, (ay1, "x"), (ax2, "y"))
    r6 = bd1, bd2, c2 = go(r4, (by1, "x"), (bx2, "y"), (c1, "near"))
    r7 = cx1, cy1 = go(r5, (c1, "x"), (c1, "y"))
    (column_both,) = go(r5, (column_far, "near"))
    r8 = cx2, cy2 = go(r6, (c2, "x"), (c2, "y"))
    cd1, cd2 = go(r7, (cy1, "x"), (cx2, "y"))
    return [
        (a1, a2, ax1, ax2, ay1, ay2, ad1, ad2),
        (b1, b2, bx1, bx2, by1, by2, bd1, bd2),
        (c1, c2, cx1, cx2, cy1, cy2, cd1, cd2),
        (column, column_far, column_near, column_both),
        tuple(r4),
        tuple(r7),
        (column_near,),
    ]


def add_half(own, got):
    return (wide(own) + wide(got)).astype(bf16)


def add_diagonal(x_in, y_in, from_x, from_y, x_out, y_out, x_buf, y_buf, sems):
    half = from_x.shape[0]
    loads = [
        pltpu.make_async_copy(x_in.at[pl.ds(half, half), :], x_buf, sems.at[0]),
        pltpu.make_async_copy(y_in.at[pl.ds(0, half), :], y_buf, sems.at[1]),
    ]
    for load in loads:
        load.start()
    finish(loads)
    x_buf[...] = add_half(x_buf[...], from_y[...])
    y_buf[...] = add_half(y_buf[...], from_x[...])
    stores = [
        pltpu.make_async_copy(x_buf, x_out.at[pl.ds(half, half), :], sems.at[2]),
        pltpu.make_async_copy(y_buf, y_out.at[pl.ds(0, half), :], sems.at[3]),
    ]
    for store in stores:
        store.start()
    finish(stores)


def add_plane(own, got_x, got_y, kept, other):
    half = kept.shape[0]
    total = wide(own[...]) + wide(got_x[...]) + wide(got_y[...])
    kept[...] = total[:half]
    other[...] = total[half:].astype(bf16)


def add_near(kept, got, mine, other):
    rows = mine.shape[0]
    total = kept[...] + wide(got[...])
    mine[...] = total[:rows]
    other[...] = total[rows:].astype(bf16)


def write_outs(turned, total, outs):
    start = 0
    for out, flip in zip(outs, turned):
        if flip:
            columns = max(out.shape[0], LANES)
            out[...] = total[:, start : start + columns].T[: out.shape[0]]
            start += columns
        else:
            out[...] = total[:, start : start + out.shape[1]]
            start += out.shape[1]


def add_far(turned, mine, got, *outs):
    write_outs(turned, mine[...] + wide(got[...]), outs)


class Reduction:
    def __init__(self, pieces, count, widths, turned):
        self.pieces, self.widths, self.turned = pieces, widths, turned
        self.perms = grid_perms(count)
        self.ended = ()
        self.outs = None
        if len(pieces) == 1:
            total = wide(lax.psum_scatter(pieces[0], "dp", scatter_dimension=0, tiled=True))
            self.outs, start = [], 0
            for width, flip in zip(widths, turned):
                part = total[:, start : start + width]
                self.outs.append(part.T if flip else part)
                start += max(width, LANES)

    def out_shapes(self, rows):
        return [((width, rows) if flip else (rows, width), f32) for width, flip in zip(self.widths, self.turned)]

    def move(self, arrays, names, gate):
        out = []
        for array, name in zip(arrays, names):
            (array,) = tie([array], gate)
            out.append(lax.ppermute(array, "dp", self.perms[name]))
        self.ended = tie(out)
        return self.ended

    def diagonal(self, gate=()):
        if self.outs is not None:
            return
        own, x_col, y_col, d_first, d_second = self.pieces
        half, columns = d_first.shape
        from_x, from_y = self.move([d_first, d_second], ["x", "y"], gate)
        buffer = pltpu.VMEM((half, columns), bf16)
        self.sides = pl.pallas_call(
            add_diagonal, name="add_diagonal", out_shape=[pltpu.HBM(x_col.shape, bf16)] * 2,
            in_specs=[HBM, HBM, VMEM, VMEM], out_specs=[HBM, HBM], input_output_aliases={0: 0, 1: 1},
            scratch_shapes=[buffer, buffer, pltpu.SemaphoreType.DMA((4,))],
            compiler_params=pltpu.CompilerParams(vmem_limit_bytes=8 * MIB), cost_estimate=cost(2 * COSTS['add_diagonal']),
        )(x_col, y_col, from_x, from_y)

    def plane(self, gate=()):
        if self.outs is not None:
            return
        half, columns = self.pieces[3].shape
        got_x, got_y = self.move(self.sides, ["x", "y"], gate)
        self.kept, self.other = call(
            add_plane, "add_plane", [], [self.pieces[0], got_x, got_y], [],
            [((half, columns), f32), ((half, columns), bf16)], [], [], 2, mib=10)

    def near(self, gate=()):
        if self.outs is not None:
            return
        half, columns = self.pieces[3].shape
        (got,) = self.move([self.other], ["near"], gate)
        self.mine, self.other = call(
            add_near, "add_near", [], [self.kept, got], [],
            [((half // 2, columns), f32), ((half // 2, columns), bf16)], [], [], 1, mib=8)

    def far(self, gate=(), last=True):
        if self.outs is not None:
            return
        (got,) = self.move([self.other], ["far"], gate)
        self.got_far = got
        if not last:
            return
        shapes = self.out_shapes(self.pieces[3].shape[0] // 2)
        self.outs = call(
            functools.partial(add_far, self.turned), "add_far", [], [self.mine, got], [], shapes, [], [], 1, mib=8)


def add_two(left, right, out):
    out[...] = add_half(left[...], right[...])


def add_column(own, got_near, got_far, mine, x_out, y_out, d_out):
    rows = mine.shape[0]
    total = wide(own[...]) + wide(got_near[...]) + wide(got_far[...])
    mine[...] = total[:rows]
    for place, out in enumerate((x_out, y_out, d_out)):
        out[...] = total[(place + 1) * rows : (place + 2) * rows].astype(bf16)


def add_sides(mine, got_x, got_y, first_mine, first_got, up, down):
    second = mine[...] + wide(got_x[...]) + wide(got_y[...])
    first = first_mine[...] + wide(first_got[...])
    half = up.shape[1] // 2
    for place, out in enumerate((up, down)):
        out[:, :half] = first[:, place * half : (place + 1) * half]
        out[:, half:] = second[:, place * half : (place + 1) * half]


class FlatReduction(Reduction):
    def near(self, gate=()):
        if self.outs is not None:
            return
        own, across, beside, corner = self.pieces
        (got_across,) = self.move([corner], ["near"], gate)
        self.got_across = got_across
        (self.got_own,) = self.move([beside], ["near"], gate)
        (self.across,) = call(add_two, "add_two", [], [across, got_across], [], [(across.shape, bf16)], [], [], 1, mib=8)

    def far(self, gate=()):
        if self.outs is not None:
            return
        (self.got,) = self.move([self.across], ["far"], gate)

    def column(self, gate=()):
        if self.outs is not None:
            return
        own, got = self.pieces[0], self.got
        self.rows = own.shape[0] // PLANES
        block = (self.rows, own.shape[1])
        self.mine, *self.sides = call(
            add_column, "add_column", [], [own, self.got_own, got], [], [(block, f32)] + [(block, bf16)] * 3, [], [], 2, mib=8, gate=gate)

    def diagonal(self, gate=()):
        if self.outs is not None:
            return
        (got,) = self.move([self.sides[2]], ["x"], gate)
        (self.y_side,) = call(add_two, "add_two", [], [self.sides[1], got], [], [(got.shape, bf16)], [], [], 1, mib=8)

    def plane(self, gate=()):
        if self.outs is not None:
            return
        got_x, got_y = self.move([self.sides[0], self.y_side], ["x", "y"], gate)
        self.got_sides = (got_x, got_y)

    def join(self, first):
        if self.outs is not None:
            return
        shape = (self.rows, 2 * self.widths[0])
        self.joined = call(
            add_sides, "add_sides", [], [self.mine, *self.got_sides, first.mine, first.got_far], [], [(shape, f32)] * 2, [], [], 1, mib=8)


def swap_cores(array):
    return lax.ppermute(array, "tensor", [(0, 1), (1, 0)])


def join_cores(array):
    other = swap_cores(array)
    low = lax.axis_index("tensor") == 0
    return jnp.concatenate(
        [jnp.where(low, array, other), jnp.where(low, other, array)], axis=0
    )


def fetch(table, pieces, target, sems, columns, sem_from=0):
    start, size = columns
    copies = []
    if len(pieces) == 1:
        copies.append(
            pltpu.make_async_copy(pieces[0].at[:, pl.ds(start, size)], target, sems.at[sem_from])
        )
    else:
        rows = target.shape[0] // table.shape[0]
        slot = 0
        for piece in pieces:
            for j in range(piece.shape[0] // rows):
                first = pl.multiple_of(table[slot] * rows, 16)
                copies.append(
                    pltpu.make_async_copy(
                        piece.at[pl.ds(j * rows, rows), pl.ds(start, size)],
                        target.at[pl.ds(first, rows), :],
                        sems.at[sem_from + slot],
                    )
                )
                slot += 1
    for copy in copies:
        copy.start()
    return copies


def put(table, source, pieces, sems, columns, sem_from=0):
    start, size = columns
    copies = []
    if len(pieces) == 1:
        copies.append(
            pltpu.make_async_copy(source, pieces[0].at[:, pl.ds(start, size)], sems.at[sem_from])
        )
    else:
        rows = source.shape[0] // table.shape[0]
        slot = 0
        for piece in pieces:
            for j in range(piece.shape[0] // rows):
                first = pl.multiple_of(table[slot] * rows, 16)
                copies.append(
                    pltpu.make_async_copy(
                        source.at[pl.ds(first, rows), :],
                        piece.at[pl.ds(j * rows, rows), pl.ds(start, size)],
                        sems.at[sem_from + slot],
                    )
                )
                slot += 1
    for copy in copies:
        copy.start()
    return copies


def finish(copies):
    for copy in copies:
        copy.wait()


def norm_parts(stream):
    center = stream - jnp.mean(stream, axis=-1, keepdims=True)
    spread = jnp.mean(center * center, axis=-1, keepdims=True)
    scale = lax.rsqrt(spread + EPSILON)
    return center * scale, scale


def norm_back(grad, normal, scale, gain):
    inner = grad * gain
    return scale * (
        inner
        - jnp.mean(inner, axis=-1, keepdims=True)
        - normal * jnp.mean(inner * normal, axis=-1, keepdims=True)
    )


def turn(pair, cosine, sine):
    lane = lax.broadcasted_iota(jnp.int32, pair.shape, 1)
    low_half = lane % HEAD_DIM < HEAD_DIM // 2
    partner = jnp.where(
        low_half,
        pltpu.roll(pair, LANES - HEAD_DIM // 2, 1),
        pltpu.roll(pair, HEAD_DIM // 2, 1),
    )
    return pair * cosine + partner * sine


def stack_heads(pair):
    lane = lax.broadcasted_iota(jnp.int32, pair.shape, 1)
    zero = jnp.zeros_like(pair)
    return jnp.concatenate(
        [jnp.where(lane < HEAD_DIM, pair, zero), jnp.where(lane < HEAD_DIM, zero, pair)], axis=0
    )


def merge_heads(stacked):
    rows = stacked.shape[0] // 2
    lane = lax.broadcasted_iota(jnp.int32, (rows, stacked.shape[1]), 1)
    return jnp.where(lane < HEAD_DIM, stacked[:rows], stacked[rows:])


def softmax_low(scores):
    raised = jnp.exp(scores - jnp.max(scores, axis=-1, keepdims=True))
    return (raised * (1.0 / jnp.sum(raised, axis=-1, keepdims=True))).astype(bf16)


def pairs_of(width):
    return [(pair, slice(pair * LANES, (pair + 1) * LANES)) for pair in range(width // LANES)]


SCALE = HEAD_DIM ** (-0.5)


def self_forward(count, table, x_ref, cos_ref, sin_ref, *refs):
    pieces, refs = refs[:count], refs[count:]
    part, h_out, q_out, k_out, v_out, p_out, o_out, norms_out, weights, sems = refs
    width = q_out.shape[1]
    copies = fetch(table, pieces, weights.buffer, sems, (0, weights.shape[1]))
    normal, _ = norm_parts(wide(x_ref[...]))
    finish(copies)
    send(weights)
    rows = wide(weights[:, :LANES]).T[:8]
    norms_out[...] = rows
    hidden = (normal * rows[0:1] + rows[1:2]).astype(bf16)
    h_out[...] = hidden
    send(h_out)
    mixed = mm(hidden, weights[:, LANES : LANES + 3 * width])
    cosine, sine = cos_ref[...], sin_ref[...]
    count_rows = hidden.shape[0]
    query_pos = lax.broadcasted_iota(jnp.int32, (2 * count_rows, count_rows), 0) % count_rows
    allowed = query_pos >= lax.broadcasted_iota(jnp.int32, (2 * count_rows, count_rows), 1)
    for pair, lanes in pairs_of(width):
        queries = turn(mixed[:, lanes], cosine, sine).astype(bf16)
        keys = turn(mixed[:, width + pair * LANES : width + (pair + 1) * LANES], cosine, sine).astype(bf16)
        values = mixed[:, 2 * width + pair * LANES : 2 * width + (pair + 1) * LANES].astype(bf16)
        q_out[:, lanes] = queries
        k_out[:, lanes] = keys
        v_out[:, lanes] = values
        scores = jnp.where(allowed, mm_nt(stack_heads(queries), keys) * SCALE, NEG_FILL)
        attend = softmax_low(scores)
        p_out[pair] = attend
        o_out[:, lanes] = merge_heads(mm(attend, values)).astype(bf16)
    send(q_out, k_out, v_out, p_out, o_out)
    part[...] = mm_nt(o_out[...], weights[:, LANES + 3 * width :]).astype(bf16)


def pool_forward(count, table, pool_ref, *refs):
    pieces, refs = refs[:count], refs[count:]
    k_out, v_out, weights, sems = refs
    width = k_out.shape[1]
    finish(fetch(table, pieces, weights.buffer, sems, (2 * width, 2 * width)))
    send(weights)
    mixed = mm(pool_ref[...], weights[...])
    k_out[...] = mixed[:, :width].astype(bf16)
    v_out[...] = mixed[:, width:].astype(bf16)


def chosen_rows(chosen, block, ref, lanes):
    return jnp.concatenate(
        [
            ref[pl.ds(pl.multiple_of(chosen[NBRS * block + j] * NBR_LEN, NBR_LEN), NBR_LEN), lanes]
            for j in range(NBRS)
        ],
        axis=0,
    )


def cross_forward(count, table, chosen, x_ref, own_ref, got_ref, norms, k_ref, v_ref, *refs):
    pieces, refs = refs[:count], refs[count:]
    part, x_out, h_out, q_out, p_out, o_out, both_w, sems = refs
    width = q_out.shape[1]
    copies = fetch(table, pieces, both_w.buffer, sems, (0, 2 * width))
    stream = wide(x_ref[...]) + (wide(own_ref[...]) + wide(got_ref[...]))
    x_out[...] = stream
    send(x_out)
    normal, _ = norm_parts(stream)
    hidden = (normal * norms[2:3] + norms[3:4]).astype(bf16)
    h_out[...] = hidden
    send(h_out)
    finish(copies)
    send(both_w)
    queries = mm(hidden, both_w[:, :width]).astype(bf16)
    q_out[...] = queries
    send(q_out)
    pair_count = width // LANES
    for block in range(queries.shape[0] // GROUP):
        rows = slice(block * GROUP, (block + 1) * GROUP)
        for pair, lanes in pairs_of(width):
            keys = chosen_rows(chosen, block, k_ref, lanes)
            values = chosen_rows(chosen, block, v_ref, lanes)
            attend = softmax_low(mm_nt(stack_heads(queries[rows, lanes]), keys) * SCALE)
            p_out[block * pair_count + pair] = attend
            o_out[rows, lanes] = merge_heads(mm(attend, values)).astype(bf16)
    send(p_out, o_out)
    part[...] = mm_nt(o_out[...], both_w[:, width:]).astype(bf16)


def feed_forward(count, grad_count, slices, leading, table, grad_table, side, x_ref, norms, g_ref, one_ref, two_ref, *refs):
    pieces, refs = refs[:count], refs[count:]
    results = refs[:3]
    grads, refs = refs[3 : 3 + grad_count], refs[3 + grad_count :]
    up_w, down_w, up_g, down_g, *full, sems, sems_out = refs
    total = up_w.shape[0] * up_w.shape[2]
    size = total // slices
    block_count = table.shape[0] if count > 1 else 1
    copies = []
    for turn_of in range(slices):
        copies.append(
            fetch(table, pieces, up_w.at[turn_of], sems, (turn_of * size, size), 2 * turn_of * block_count)
            + fetch(table, pieces, down_w.at[turn_of], sems, (total + turn_of * size, size), (2 * turn_of + 1) * block_count)
        )
    if leading:
        stream = wide(x_ref[...]) + (wide(one_ref[...]) + wide(two_ref[...]))
        results[0][...] = stream
        send(results[0])
    else:
        stream = x_ref[...]
    normal, _ = norm_parts(stream)
    hidden = (normal * norms[4:5] + norms[5:6]).astype(bf16)
    grad = g_ref[...]
    hidden_t, grad_t = hidden.T, grad.T
    kept = results[1:] if leading else full
    sent = []
    for turn_of in range(slices):
        finish(copies[turn_of])
        pre = mm(hidden, up_w[turn_of])
        grad_act = mm(grad, down_w[turn_of])
        square = pre * pre
        bend = jnp.tanh(GELU_A * (pre + GELU_B * square * pre))
        gate = 0.5 * (1.0 + bend)
        act = (pre * gate).astype(bf16)
        slope = gate + 0.5 * pre * (1.0 - bend * bend) * (GELU_A * (1.0 + 3.0 * GELU_B * square))
        grad_pre = (grad_act * slope).astype(bf16)
        more, less = mm_nt(act, down_w[turn_of]), mm_nt(grad_pre, up_w[turn_of])
        for keep, add, given in zip(kept, (more, less), (one_ref, two_ref)):
            base = keep[...] if turn_of else None if leading else given[...]
            keep[...] = add if base is None else base + add
        if turn_of == slices - 1:
            if leading:
                send(results[1], results[2])
            else:
                results[2][...] = full[1][...].astype(bf16)
                full[1][...] = full[0][...] + stream
                half = results[0].shape[0]
                results[0][...] = full[1][pl.ds(pl.multiple_of(side[0] * half, half), half), :]
                results[1][...] = full[0][pl.ds(pl.multiple_of((1 - side[0]) * half, half), half), :].astype(bf16)
        up_g[turn_of] = mm(hidden_t, grad_pre).astype(bf16)
        down_g[turn_of] = mm(grad_t, act).astype(bf16)
        sent += put(grad_table, up_g.at[turn_of], grads, sems_out, (turn_of * size, size), 2 * turn_of * block_count)
        sent += put(grad_table, down_g.at[turn_of], grads, sems_out, (total + turn_of * size, size), (2 * turn_of + 1) * block_count)
    finish(sent)


def attention_back(stacked_grad, outputs, attend, keys, values, stacked_queries):
    both = jnp.concatenate([outputs, outputs], axis=0)
    inner = jnp.sum(wide(stacked_grad) * wide(both), axis=-1, keepdims=True)
    grad_scores = (wide(attend) * (mm_nt(stacked_grad, values) - inner)).astype(bf16)
    grad_q = merge_heads(mm(grad_scores, keys)) * SCALE
    grad_k = mm_tn(grad_scores, stacked_queries) * SCALE
    grad_v = mm_tn(attend, stacked_grad)
    return grad_q, grad_k, grad_v


def cross_back(chosen, own_ref, got_ref, norms, x_ref, g_ref, both_w, o_ref, p_ref, v_ref, k_ref, q_ref, *refs):
    dx_out, low_out, dh_out, dq_out, dk_out, dv_out, sums_out, dk_acc, dv_acc = refs
    width = q_ref.shape[1]
    normal, scale = norm_parts(x_ref[...])
    grad = wide(own_ref[...]) + wide(got_ref[...])
    dx = wide(g_ref[...]) + norm_back(grad, normal, scale, norms[4:5])
    dx_out[...] = dx
    send(dx_out)
    sums_out[0:1] = jnp.sum(grad * normal, axis=0, keepdims=True)
    sums_out[1:2] = jnp.sum(grad, axis=0, keepdims=True)
    low = dx.astype(bf16)
    low_out[...] = low
    send(low_out)
    dk_acc[...] = jnp.zeros_like(dk_acc)
    dv_acc[...] = jnp.zeros_like(dv_acc)
    grad_mix = mm(low, both_w[:, width:]).astype(bf16)
    pair_count = width // LANES
    for block in range(low.shape[0] // GROUP):
        rows = slice(block * GROUP, (block + 1) * GROUP)
        for pair, lanes in pairs_of(width):
            keys = chosen_rows(chosen, block, k_ref, lanes)
            values = chosen_rows(chosen, block, v_ref, lanes)
            grad_q, grad_k, grad_v = attention_back(
                stack_heads(grad_mix[rows, lanes]),
                o_ref[rows, lanes],
                p_ref[block * pair_count + pair],
                keys,
                values,
                stack_heads(q_ref[rows, lanes]),
            )
            dq_out[rows, lanes] = grad_q.astype(bf16)
            for j in range(NBRS):
                place = pl.ds(pl.multiple_of(chosen[NBRS * block + j] * NBR_LEN, NBR_LEN), NBR_LEN)
                part = slice(j * NBR_LEN, (j + 1) * NBR_LEN)
                dk_acc[place, lanes] += grad_k[part]
                dv_acc[place, lanes] += grad_v[part]
    dk_out[...] = dk_acc[...].astype(bf16)
    dv_out[...] = dv_acc[...].astype(bf16)
    send(dq_out, dk_out, dv_out)
    dh_out[...] = mm_nt(dq_out[...], both_w[:, :width]).astype(bf16)


def cross_weights(grad_count, table, side, h_ref, dq_ref, pool_ref, dk_ref, dv_ref, low_ref, o_ref, weights, *refs):
    pool_out, pool_other = refs[:2]
    grads, refs = refs[2 : 2 + grad_count], refs[2 + grad_count :]
    made, full, sems_out = refs
    width = dq_ref.shape[1]
    block_count = table.shape[0] if grad_count > 1 else 1
    made[:, :width] = mm_tn(h_ref[...], dq_ref[...]).astype(bf16)
    pool_t = pool_ref[...].T
    made[:, width : 2 * width] = mm(pool_t, dk_ref[...]).astype(bf16)
    made[:, 2 * width : 3 * width] = mm(pool_t, dv_ref[...]).astype(bf16)
    made[:, 3 * width :] = mm_tn(low_ref[...], o_ref[...]).astype(bf16)
    sent = put(table, made, grads, sems_out, (0, 4 * width))
    full[...] = mm_nt(dk_ref[...], weights[:, :width]) + mm_nt(dv_ref[...], weights[:, width:])
    half = pool_out.shape[0]
    pool_out[...] = full[pl.ds(pl.multiple_of(side[0] * half, half), half), :].astype(bf16)
    pool_other[...] = full[pl.ds(pl.multiple_of((1 - side[0]) * half, half), half), :].astype(bf16)
    finish(sent)


def self_back(own_ref, got_ref, norms, x_ref, dx_ref, weights, o_ref, p_ref, v_ref, k_ref, q_ref, cos_ref, sin_ref, *refs):
    dx_out, low_out, dh_out, dq_out, dk_out, dv_out, sums_out = refs
    width = q_ref.shape[1]
    normal, scale = norm_parts(x_ref[...])
    grad = wide(own_ref[...]) + wide(got_ref[...])
    dx = dx_ref[...] + norm_back(grad, normal, scale, norms[2:3])
    dx_out[...] = dx
    send(dx_out)
    sums_out[0:1] = jnp.sum(grad * normal, axis=0, keepdims=True)
    sums_out[1:2] = jnp.sum(grad, axis=0, keepdims=True)
    low = dx.astype(bf16)
    low_out[...] = low
    send(low_out)
    grad_mix = mm(low, weights[:, LANES + 3 * width :]).astype(bf16)
    cosine, sine = cos_ref[...], -sin_ref[...]
    for pair, lanes in pairs_of(width):
        grad_q, grad_k, grad_v = attention_back(
            stack_heads(grad_mix[:, lanes]),
            o_ref[:, lanes],
            p_ref[pair],
            k_ref[:, lanes],
            v_ref[:, lanes],
            stack_heads(q_ref[:, lanes]),
        )
        dq_out[:, lanes] = turn(grad_q, cosine, sine).astype(bf16)
        dk_out[:, lanes] = turn(grad_k, cosine, sine).astype(bf16)
        dv_out[:, lanes] = grad_v.astype(bf16)
    send(dq_out, dk_out, dv_out)
    dh_out[...] = (
        mm_nt(dq_out[...], weights[:, LANES : LANES + width])
        + mm_nt(dk_out[...], weights[:, LANES + width : LANES + 2 * width])
        + mm_nt(dv_out[...], weights[:, LANES + 2 * width : LANES + 3 * width])
    ).astype(bf16)


def self_weights(grad_count, table, one_ref, two_ref, three_ref, h_ref, dq_ref, dk_ref, dv_ref, low_ref, o_ref, *refs):
    grads, refs = refs[:grad_count], refs[grad_count:]
    made, sems_out = refs
    width = dq_ref.shape[1]
    sums = [one_ref[:2], two_ref[:2], three_ref[:2], jnp.zeros((LANES - NORMS, one_ref.shape[1]), f32)]
    made[:, 4 * width :] = jnp.concatenate(sums, axis=0).T.astype(bf16)
    hidden_t = h_ref[...].T
    for part, grad in enumerate((dq_ref, dk_ref, dv_ref)):
        made[:, part * width : (part + 1) * width] = mm(hidden_t, grad[...]).astype(bf16)
    made[:, 3 * width : 4 * width] = mm_tn(low_ref[...], o_ref[...]).astype(bf16)
    finish(put(table, made, grads, sems_out, (0, 4 * width + LANES)))


def input_back(side, dx_ref, x_ref, norms, own_ref, got_ref, dx_out, sums_out, full):
    normal, scale = norm_parts(wide(x_ref[...]))
    grad = wide(own_ref[...]) + wide(got_ref[...])
    full[...] = dx_ref[...] + norm_back(grad, normal, scale, norms[0:1])
    half = dx_out.shape[0]
    dx_out[...] = full[pl.ds(pl.multiple_of(side[0] * half, half), half), :]
    sums_out[0:1] = jnp.sum(grad * normal, axis=0, keepdims=True)
    sums_out[1:2] = jnp.sum(grad, axis=0, keepdims=True)


SMEM = pl.BlockSpec(memory_space=pltpu.SMEM)
VMEM = pl.BlockSpec(memory_space=pltpu.VMEM)
ANY = pl.BlockSpec(memory_space=pl.ANY)
HBM = pl.BlockSpec(memory_space=pltpu.HBM)


def cost(microseconds):
    return pl.CostEstimate(flops=int(microseconds * 1.1e9), bytes_accessed=0, transcendentals=0)


class Arriving:
    def __init__(self, source, buffer, sem):
        self.copy = pltpu.make_async_copy(source, buffer, sem)
        self.copy.start()
        self.buffer, self.shape, self.waiting = buffer, buffer.shape, True

    def __getitem__(self, index):
        if self.waiting:
            self.copy.wait()
            self.waiting = False
        return self.buffer[index]


class Leaving:
    def __init__(self, buffer, target, sem):
        self.copy = pltpu.make_async_copy(buffer, target, sem)
        self.buffer, self.shape, self.dtype, self.sent = buffer, buffer.shape, buffer.dtype, False

    def __getitem__(self, index):
        return self.buffer[index]

    def __setitem__(self, index, value):
        self.buffer[index] = value

    def send(self):
        if not self.sent:
            self.copy.start()
            self.sent = True


def send(*results):
    for result in results:
        if isinstance(result, Leaving):
            result.send()


def streamed(body, counts, far_in, far_out, *refs):
    scalars, arrays, pieces, outs, grads, own = counts
    parts, start = [], 0
    for size in (scalars, arrays, pieces, outs, grads, own, len(far_in), len(far_out), 2):
        parts.append(list(refs[start : start + size]))
        start += size
    scalars, arrays, pieces, outs, grads, own, in_buffers, out_buffers, (in_sems, out_sems) = parts
    for place, index in enumerate(far_in):
        arrays[index] = Arriving(arrays[index], in_buffers[place], in_sems.at[place])
    for place, index in enumerate(far_out):
        outs[index] = Leaving(out_buffers[place], outs[index], out_sems.at[place])
    body(*scalars, *arrays, *pieces, *outs, *grads, *own)
    for index in far_in:
        if arrays[index].waiting:
            arrays[index].copy.wait()
    for index in far_out:
        outs[index].send()
    for index in far_out:
        outs[index].copy.wait()


COSTS = {"self_forward": 0.7, "pool_forward": 0.7, "cross_forward": 0.7, "feed_forward": 0.7, "cross_back": 0.7, "cross_weights": 0.5, "self_back": 0.7, "self_weights": 0.7, "input_back": 0.7, "adds": 0.8, "add_diagonal": 0.5, "pack_self": 0.7}


def call(body, name, scalars, arrays, pieces, outs, grads, scratch, microseconds, mib=20, gate=(), far=(), pin=()):
    arrays = [pltpu.with_memory_space_constraint(a, pltpu.HBM) if i in pin else a for i, a in enumerate(arrays)]
    if gate:
        arrays = list(tie(arrays, gate))
    shapes = [pltpu.HBM(*out[:2]) if len(out) > 2 else jax.ShapeDtypeStruct(*out) for out in outs]
    shapes += [pltpu.HBM(shape, dtype) for shape, dtype in grads]
    far = list(far)
    far_out = [index for index, out in enumerate(outs) if len(out) > 2]
    scratch = list(scratch)
    if far or far_out:
        counts = (len(scalars), len(arrays), len(pieces), len(outs), len(grads), len(scratch))
        body = functools.partial(streamed, body, counts, far, far_out)
        scratch += [pltpu.VMEM(arrays[index].shape, arrays[index].dtype) for index in far]
        scratch += [pltpu.VMEM(*outs[index][:2]) for index in far_out]
        scratch += [pltpu.SemaphoreType.DMA((max(len(some), 1),)) for some in (far, far_out)]
    return pl.pallas_call(
        body,
        name=name,
        out_shape=shapes,
        in_specs=[SMEM] * len(scalars)
        + [HBM if index in far else VMEM for index in range(len(arrays))]
        + [ANY] * len(pieces),
        out_specs=[HBM if index in far_out else VMEM for index in range(len(outs))] + [HBM] * len(grads),
        scratch_shapes=scratch,
        compiler_params=pltpu.CompilerParams(vmem_limit_bytes=mib * MIB),
        cost_estimate=cost(COSTS['adds' if name.startswith('add_') else name] * microseconds),
    )(*scalars, *arrays, *pieces)


def rope_tables(rows):
    half = HEAD_DIM // 2
    frequency = np.power(np.float32(10000.0), -np.arange(half, dtype=np.float32) / np.float32(half))
    angles = np.arange(rows, dtype=np.float32)[:, None] * frequency[None, :]
    cosine, sine = np.cos(angles), np.sin(angles)
    return (
        jnp.asarray(np.concatenate([cosine] * 4, axis=1), f32),
        jnp.asarray(np.concatenate([-sine, sine] * 2, axis=1), f32),
    )


def dma_sems(count, uses=1):
    blocks = BLOCKS if count > 1 else 1
    return pltpu.SemaphoreType.DMA((blocks * uses,))


def pack(*columns):
    return jnp.concatenate([column.astype(bf16) for column in columns], axis=1)


def pack_kernel(*refs):
    norms, (query, key, value, out_w, packed) = refs[:NORMS], refs[NORMS:]
    rows, width = query.shape
    lines = [norm[...] for norm in norms] + [jnp.zeros((LANES - NORMS, rows), f32)]
    packed[:, :LANES] = jnp.concatenate(lines, axis=0).T.astype(bf16)
    for place, ref in enumerate((query, key, value)):
        packed[:, LANES + place * width : LANES + (place + 1) * width] = ref[...].astype(bf16)
    packed[:, LANES + 3 * width :] = out_w[...].astype(bf16)


def pack_self(norms, query, key, value, out_w, fast):
    if not fast:
        lines = jnp.pad(jnp.stack(norms, axis=1), ((0, 0), (0, LANES - NORMS)))
        return pack(lines, query, key, value, out_w)
    lines = [norm.reshape(1, -1) for norm in norms]
    shape = (query.shape[0], LANES + 4 * query.shape[1])
    return call(pack_kernel, "pack_self", [], lines + [query, key, value, out_w], [], [(shape, bf16)], [], [], 2, mib=60)[0]


def on_device(count, inputs, neighbours, nbr_index, ln1_gain, ln1_bias, ln2_gain, ln2_bias, ln3_gain, ln3_bias,
              w_query, w_key, w_value, c_query, c_key, c_value, w_up, w_out, c_out, w_down, cotangent):
    width, hidden = w_query.shape[1], w_up.shape[1]
    shard_rows = w_query.shape[0]
    model = shard_rows * count
    rows = 2 * inputs.shape[0]
    norms = [ln1_gain, ln1_bias, ln2_gain, ln2_bias, ln3_gain, ln3_bias]

    stream = join_cores(inputs)
    cot = join_cores(cotangent)
    pool = join_cores(neighbours.reshape(-1, neighbours.shape[-1]))
    down_t = w_down.T
    part_hidden = hidden // 2
    cuts = [slice(0, part_hidden), slice(part_hidden, hidden)]
    self_w, cross_w, *ff_w, gate_self, gate_pool, gate_cross = gather_all(
        pack_self(norms, w_query, w_key, w_value, w_out.T, pieces_ok(count, shard_rows)),
        pack(c_query, c_out.T, c_key, c_value),
        pack(w_up[:, cuts[0]], down_t[:, cuts[0]]),
        pack(w_up[:, cuts[1]], down_t[:, cuts[1]]),
        count,
        (stream, cot, pool),
    )
    ff_w = ff_w[::-1]
    side = lax.axis_index("tensor").astype(jnp.int32).reshape(1)
    pieces = len(self_w)
    if pieces > 1:
        tables = jnp.asarray(block_tables(count))
        table, flat_table = (tables[i][lax.axis_index("dp")] for i in range(2))
        grad_rows = [shard_rows * blocks for blocks in (4, 4, 4, 2, 2)]
        flat_rows = [shard_rows * PLANES] * 4
    else:
        table = flat_table = jnp.zeros((1,), jnp.int32)
        grad_rows = flat_rows = [model]
    grad_count = len(grad_rows)

    def bind(body, *extra):
        return functools.partial(body, pieces, *extra)

    pool_rows = pool.shape[0]
    chosen = nbr_index.reshape(-1)
    cosine, sine = rope_tables(rows)
    pairs = width // LANES
    blocks = rows // GROUP
    tall, low = ((rows, model), f32), ((rows, model), bf16)
    slim = ((rows, width), bf16)
    rank8 = ((8, model), f32)
    half_tall, half_low = ((rows // 2, model), f32), ((rows // 2, model), bf16)

    def kept(out):
        return out + ("hbm",)


    part, h_one, queries, keys, values, attend, mixture, norm_rows, self_full = call(
        bind(self_forward), "self_forward", [table], [stream, cosine, sine], self_w,
        [low, kept(low), kept(slim), kept(slim), kept(slim), kept(((pairs, 2 * rows, rows), bf16)), kept(slim), rank8, kept(((model, LANES + 4 * width), bf16))], [],
        [dma_sems(pieces)], 8, mib=60, gate=gate_self, far=[0, 1, 2])
    got = swap_cores(part)
    ckeys, cvalues, cross_full = call(
        bind(pool_forward), "pool_forward", [table], [pool], cross_w,
        [kept(((pool_rows, width), bf16))] * 2 + [kept(((model, 2 * width), bf16))], [],
        [dma_sems(pieces)], 3, mib=60, gate=gate_pool, far=[0])
    part, after_self, h_two, cqueries, cattend, cmixture, cboth_full = call(
        bind(cross_forward), "cross_forward", [table, chosen], [stream, part, got, norm_rows, ckeys, cvalues], cross_w,
        [low, kept(tall), kept(low), kept(slim), kept(((blocks * pairs, 2 * GROUP, NBRS * NBR_LEN), bf16)), kept(slim), kept(((model, 2 * width), bf16))], [],
        [dma_sems(pieces)], 6, mib=60, gate=gate_cross, far=[0, 4, 5])
    got = swap_cores(part)
    slices = 2
    size = part_hidden // slices
    def ff_call(leading, ff_pieces, from_table, to_table, to_rows, arrays, outs, far, pin):
        wide_scratch = [] if leading else [pltpu.VMEM((rows, model), f32)] * 2
        results = call(
            functools.partial(feed_forward, len(ff_pieces), len(to_rows), slices, leading), "feed_forward",
            [from_table, to_table, side], arrays, ff_pieces, outs, [((count_of, 2 * part_hidden), bf16) for count_of in to_rows],
            [pltpu.VMEM((slices, model, size), bf16)] * 4 + wide_scratch + [dma_sems(pieces, 2 * slices)] * 2, 10,
            mib=34, far=far, pin=pin)
        return *results[:3], results[3:]

    after_cross, out, back, last_grads = ff_call(
        True, ff_w[0], flat_table, flat_table, flat_rows, [after_self, norm_rows, cot, part, got],
        [kept(tall)] * 3, [0, 2], [0])
    result, result_other, back, first_grads = ff_call(
        False, ff_w[1], table, table, grad_rows, [after_cross, norm_rows, cot, out, back], [half_tall, half_low, low], [0, 2, 3, 4], [0, 3, 4])
    ff_grads = [last_grads, first_grads]
    grad_part = back
    got = swap_cores(grad_part)
    ff_widths, ff_turned = [part_hidden] * 2, [False, False]
    one = FlatReduction(ff_grads[0], count, ff_widths, ff_turned)
    two = Reduction(ff_grads[1], count, ff_widths, ff_turned)
    one.near()
    two.diagonal()
    two.plane()
    one.far()
    acc = pltpu.VMEM((pool_rows, width), f32)
    grad_cross, low_cross, grad_part, dcq, dck, dcv, sums_three = call(
        cross_back, "cross_back", [chosen],
        [grad_part, got, norm_rows, after_cross, cot, cboth_full, cmixture, cattend, cvalues, ckeys, cqueries], [],
        [kept(tall), kept(low), low, kept(slim), kept(((pool_rows, width), bf16)), kept(((pool_rows, width), bf16)), rank8], [],
        [acc, acc], 8, mib=24, gate=(one.got_across,) if pieces > 1 else (), far=range(3, 11))
    got = swap_cores(grad_part)
    pool_part, pool_other, *cross_grads = call(
        functools.partial(cross_weights, grad_count), "cross_weights", [table, side],
        [h_two, dcq, pool, dck, dcv, low_cross, cmixture, cross_full], [],
        [((pool_rows // 2, model), bf16)] * 2, [((count_of, 4 * width), bf16) for count_of in grad_rows],
        [pltpu.VMEM((model, 4 * width), bf16), pltpu.VMEM((pool_rows, model), f32), dma_sems(pieces)],
        8, mib=24, gate=(one.across,) if pieces > 1 else (), far=range(8))
    grad_self, low_self, grad_part, dq, dk, dv, sums_two = call(
        self_back, "self_back", [],
        [grad_part, got, norm_rows, after_self, grad_cross, self_full, mixture, attend, values, keys, queries, cosine, sine], [],
        [kept(tall), kept(low), low, kept(slim), kept(slim), kept(slim), rank8], [],
        [], 7, mib=20, gate=tuple(two.sides) + (one.across,) if pieces > 1 else (), far=range(3, 13))
    got = swap_cores(grad_part)
    three = Reduction(cross_grads, count, [width] * 4, [False] * 4)
    three.diagonal()
    grad_input, sums_one = call(
        input_back, "input_back", [side], [grad_self, stream, norm_rows, grad_part, got], [], [half_tall, rank8], [],
        [pltpu.VMEM((rows, model), f32)], 2, mib=12, far=[0, 1])
    self_grads = call(
        functools.partial(self_weights, grad_count), "self_weights", [table],
        [sums_one, sums_two, sums_three, h_one, dq, dk, dv, low_self, mixture], [],
        [], [((count_of, 4 * width + LANES), bf16) for count_of in grad_rows],
        [pltpu.VMEM((model, 4 * width + LANES), bf16), dma_sems(pieces)], 4,
        mib=16, gate=(()) if pieces > 1 else (), far=range(3, 9))
    four = Reduction(self_grads, count, [width] * 4 + [8], [False] * 4 + [True])
    one.column((self_grads[-1],))
    one.diagonal()
    sent_one = one.ended
    two.near()
    four.diagonal(())
    one.plane()
    three.plane(sent_one)
    four.plane(two.ended + sent_one)
    two.far((), False)
    three.near()
    four.near((two.got_far,) if pieces > 1 else ())
    three.far()
    four.far(three.ended)
    one.join(two)
    d_cross, d_self = three.outs, four.outs
    if pieces > 1:
        d_up, d_down = one.joined
    else:
        d_up, d_down = (jnp.concatenate([two.outs[i], one.outs[i]], axis=1) for i in range(2))
    grad_pool = wide(pool_part) + wide(swap_cores(pool_other))
    mine = d_self[4]
    return (
        (result + wide(swap_cores(result_other))).astype(bf16),
        grad_input,
        grad_pool.reshape(neighbours.shape),
        mine[0],
        mine[1],
        mine[2],
        mine[3],
        mine[4],
        mine[5],
        *d_self[:3],
        *d_cross[:3],
        d_up,
        d_self[3].T,
        d_cross[3].T,
        d_down.T,
    )


def solution(mesh):
    both = P(("dp", "tensor"), None)
    pool = P(("dp", "tensor"), None, None)
    norm = P("dp")
    tall, flat = P("dp", "tensor"), P("tensor", "dp")
    return jax.shard_map(
        functools.partial(on_device, mesh.shape["dp"]),
        mesh=mesh,
        in_specs=(both, pool, P("dp", None)) + (norm,) * 6 + (tall,) * 7 + (flat,) * 3 + (both,),
        out_specs=(both, both, pool) + (norm,) * 6 + (tall,) * 7 + (flat,) * 3,
        check_vma=False,
    )
```

```python
import functools

import jax
import jax.numpy as jnp
import numpy as np
from jax import lax
from jax.experimental import pallas as pl
from jax.experimental.pallas import tpu as pltpu
from jax.sharding import PartitionSpec as P

HEAD_DIM = 64
GROUP = 64
NBR_LEN = 128
NBRS = 2
LANES = 128
NORMS = 6
NEG_FILL = -1e30
EPSILON = 1e-05
GELU_A = 0.7978845608028654
GELU_B = 0.044715
PLANES = 4
BLOCKS = 16
MIB = 2**20

bf16 = jnp.bfloat16
f32 = jnp.float32


def mm(left, right):
    return jnp.dot(left, right, preferred_element_type=f32)


def mm_nt(left, right):
    return lax.dot_general(left, right, (((1,), (1,)), ((), ())), preferred_element_type=f32)


def mm_tn(left, right):
    return lax.dot_general(left, right, (((0,), (0,)), ((), ())), preferred_element_type=f32)


def wide(array):
    return array.astype(f32)


def grid_perms(count):
    steps = {"x": 1, "y": 2, "near": 4, "far": 8}
    return {name: [(i, i ^ step) for i in range(count)] for name, step in steps.items()}


def block_tables(count):
    orders = [
        [4 * z + plane for plane in range(PLANES) for z in (0, 2, 1, 3)],
        [4 * z + plane for z in (0, 2, 1, 3) for plane in range(PLANES)],
    ]
    return np.array([[[device ^ step for step in order] for device in range(count)] for order in orders], np.int32)


def pieces_ok(count, rows):
    return count == BLOCKS and rows % 16 == 0


def tie(arrays, gate=()):
    arrays = tuple(arrays)
    if len(arrays) + len(gate) < 2:
        return arrays
    return lax.optimization_barrier(arrays + tuple(gate))[: len(arrays)]


def stack(*arrays):
    return jnp.concatenate(arrays, axis=0)


class Rounds:
    def __init__(self, count):
        self.perms = grid_perms(count)

    def go(self, gate, *sends):
        out = []
        for array, name in sends:
            (array,) = tie([array], gate)
            out.append(lax.ppermute(array, "dp", self.perms[name]))
        return out


def gather_all(a, b, c, d, count, early):
    if not pieces_ok(count, a.shape[0]):
        gathered = [(lax.all_gather(shard, "dp", axis=0, tiled=True),) for shard in (a, b, c, d)]
        return gathered + [(), (), ()]
    go = Rounds(count).go
    (a_far,) = go((), (a, "far"))
    d_x, d_y = go((a, early[0]), (d, "x"), (d, "y"))
    a1 = stack(a, a_far)
    r0 = (d_x, d_y)
    r1 = ax1, ay1, a2 = go((), (a1, "x"), (a1, "y"), (a1, "near"))
    (d_d,) = go((), (d_y, "x"))
    (b_far,) = go((a_far, d_y), (b, "far"))
    b1, column = stack(b, b_far), stack(d, d_x, d_y, d_d)
    r2 = bx1, by1, b2, c_far = go(r0 + (ay1,), (b1, "x"), (b1, "y"), (b1, "near"), (c, "far"))
    c1 = stack(c, c_far)
    r3 = ax2, ay2 = go(tuple(r1) + tuple(early), (a2, "x"), (a2, "y"))
    (column_far,) = go(tuple(r1) + (c_far,), (column, "far"))
    r4 = bx2, by2 = go(r2, (b2, "x"), (b2, "y"))
    (column_near,) = go(r4, (column, "near"))
    r5 = ad1, ad2 = go(r3, (ay1, "x"), (ax2, "y"))
    r6 = bd1, bd2, c2 = go(r4, (by1, "x"), (bx2, "y"), (c1, "near"))
    r7 = cx1, cy1 = go(r5, (c1, "x"), (c1, "y"))
    (column_both,) = go(r5, (column_far, "near"))
    r8 = cx2, cy2 = go(r6, (c2, "x"), (c2, "y"))
    cd1, cd2 = go(r7, (cy1, "x"), (cx2, "y"))
    return [
        (a1, a2, ax1, ax2, ay1, ay2, ad1, ad2),
        (b1, b2, bx1, bx2, by1, by2, bd1, bd2),
        (c1, c2, cx1, cx2, cy1, cy2, cd1, cd2),
        (column, column_far, column_near, column_both),
        tuple(r4),
        tuple(r7),
        (column_near,),
    ]


def add_half(own, got):
    return (wide(own) + wide(got)).astype(bf16)


def add_diagonal(x_in, y_in, from_x, from_y, x_out, y_out, x_buf, y_buf, sems):
    half = from_x.shape[0]
    loads = [
        pltpu.make_async_copy(x_in.at[pl.ds(half, half), :], x_buf, sems.at[0]),
        pltpu.make_async_copy(y_in.at[pl.ds(0, half), :], y_buf, sems.at[1]),
    ]
    for load in loads:
        load.start()
    finish(loads)
    x_buf[...] = add_half(x_buf[...], from_y[...])
    y_buf[...] = add_half(y_buf[...], from_x[...])
    stores = [
        pltpu.make_async_copy(x_buf, x_out.at[pl.ds(half, half), :], sems.at[2]),
        pltpu.make_async_copy(y_buf, y_out.at[pl.ds(0, half), :], sems.at[3]),
    ]
    for store in stores:
        store.start()
    finish(stores)


def add_plane(own, got_x, got_y, kept, other):
    half = kept.shape[0]
    total = wide(own[...]) + wide(got_x[...]) + wide(got_y[...])
    kept[...] = total[:half]
    other[...] = total[half:].astype(bf16)


def add_near(kept, got, mine, other):
    rows = mine.shape[0]
    total = kept[...] + wide(got[...])
    mine[...] = total[:rows]
    other[...] = total[rows:].astype(bf16)


def write_outs(turned, total, outs):
    start = 0
    for out, flip in zip(outs, turned):
        if flip:
            columns = max(out.shape[0], LANES)
            out[...] = total[:, start : start + columns].T[: out.shape[0]]
            start += columns
        else:
            out[...] = total[:, start : start + out.shape[1]]
            start += out.shape[1]


def add_far(turned, mine, got, *outs):
    write_outs(turned, mine[...] + wide(got[...]), outs)


class Reduction:
    def __init__(self, pieces, count, widths, turned):
        self.pieces, self.widths, self.turned = pieces, widths, turned
        self.perms = grid_perms(count)
        self.ended = ()
        self.outs = None
        if len(pieces) == 1:
            total = wide(lax.psum_scatter(pieces[0], "dp", scatter_dimension=0, tiled=True))
            self.outs, start = [], 0
            for width, flip in zip(widths, turned):
                part = total[:, start : start + width]
                self.outs.append(part.T if flip else part)
                start += max(width, LANES)

    def out_shapes(self, rows):
        return [((width, rows) if flip else (rows, width), f32) for width, flip in zip(self.widths, self.turned)]

    def move(self, arrays, names, gate):
        out = []
        for array, name in zip(arrays, names):
            (array,) = tie([array], gate)
            out.append(lax.ppermute(array, "dp", self.perms[name]))
        self.ended = tie(out)
        return self.ended

    def diagonal(self, gate=()):
        if self.outs is not None:
            return
        own, x_col, y_col, d_first, d_second = self.pieces
        half, columns = d_first.shape
        from_x, from_y = self.move([d_first, d_second], ["x", "y"], gate)
        buffer = pltpu.VMEM((half, columns), bf16)
        self.sides = pl.pallas_call(
            add_diagonal, name="add_diagonal", out_shape=[pltpu.HBM(x_col.shape, bf16)] * 2,
            in_specs=[HBM, HBM, VMEM, VMEM], out_specs=[HBM, HBM], input_output_aliases={0: 0, 1: 1},
            scratch_shapes=[buffer, buffer, pltpu.SemaphoreType.DMA((4,))],
            compiler_params=pltpu.CompilerParams(vmem_limit_bytes=8 * MIB), cost_estimate=cost(2 * COSTS['add_diagonal']),
        )(x_col, y_col, from_x, from_y)

    def plane(self, gate=()):
        if self.outs is not None:
            return
        half, columns = self.pieces[3].shape
        got_x, got_y = self.move(self.sides, ["x", "y"], gate)
        self.kept, self.other = call(
            add_plane, "add_plane", [], [self.pieces[0], got_x, got_y], [],
            [((half, columns), f32), ((half, columns), bf16)], [], [], 2, mib=10)

    def near(self, gate=()):
        if self.outs is not None:
            return
        half, columns = self.pieces[3].shape
        (got,) = self.move([self.other], ["near"], gate)
        self.mine, self.other = call(
            add_near, "add_near", [], [self.kept, got], [],
            [((half // 2, columns), f32), ((half // 2, columns), bf16)], [], [], 1, mib=8)

    def far(self, gate=(), last=True):
        if self.outs is not None:
            return
        (got,) = self.move([self.other], ["far"], gate)
        self.got_far = got
        if not last:
            return
        shapes = self.out_shapes(self.pieces[3].shape[0] // 2)
        self.outs = call(
            functools.partial(add_far, self.turned), "add_far", [], [self.mine, got], [], shapes, [], [], 1, mib=8)


def add_two(left, right, out):
    out[...] = add_half(left[...], right[...])


def add_column(own, got_near, got_far, mine, x_out, y_out, d_out):
    rows = mine.shape[0]
    total = wide(own[...]) + wide(got_near[...]) + wide(got_far[...])
    mine[...] = total[:rows]
    for place, out in enumerate((x_out, y_out, d_out)):
        out[...] = total[(place + 1) * rows : (place + 2) * rows].astype(bf16)


def add_sides(mine, got_x, got_y, first_mine, first_got, up, down):
    second = mine[...] + wide(got_x[...]) + wide(got_y[...])
    first = first_mine[...] + wide(first_got[...])
    half = up.shape[1] // 2
    for place, out in enumerate((up, down)):
        out[:, :half] = first[:, place * half : (place + 1) * half]
        out[:, half:] = second[:, place * half : (place + 1) * half]


class FlatReduction(Reduction):
    def near(self, gate=()):
        if self.outs is not None:
            return
        own, across, beside, corner = self.pieces
        (got_across,) = self.move([corner], ["near"], gate)
        self.got_across = got_across
        (self.got_own,) = self.move([beside], ["near"], gate)
        (self.across,) = call(add_two, "add_two", [], [across, got_across], [], [(across.shape, bf16)], [], [], 1, mib=8)

    def far(self, gate=()):
        if self.outs is not None:
            return
        (self.got,) = self.move([self.across], ["far"], gate)

    def column(self, gate=()):
        if self.outs is not None:
            return
        own, got = self.pieces[0], self.got
        self.rows = own.shape[0] // PLANES
        block = (self.rows, own.shape[1])
        self.mine, *self.sides = call(
            add_column, "add_column", [], [own, self.got_own, got], [], [(block, f32)] + [(block, bf16)] * 3, [], [], 2, mib=8, gate=gate)

    def diagonal(self, gate=()):
        if self.outs is not None:
            return
        (got,) = self.move([self.sides[2]], ["x"], gate)
        (self.y_side,) = call(add_two, "add_two", [], [self.sides[1], got], [], [(got.shape, bf16)], [], [], 1, mib=8)

    def plane(self, gate=()):
        if self.outs is not None:
            return
        got_x, got_y = self.move([self.sides[0], self.y_side], ["x", "y"], gate)
        self.got_sides = (got_x, got_y)

    def join(self, first):
        if self.outs is not None:
            return
        shape = (self.rows, 2 * self.widths[0])
        self.joined = call(
            add_sides, "add_sides", [], [self.mine, *self.got_sides, first.mine, first.got_far], [], [(shape, f32)] * 2, [], [], 1, mib=8)


def swap_cores(array):
    return lax.ppermute(array, "tensor", [(0, 1), (1, 0)])


def join_cores(array):
    other = swap_cores(array)
    low = lax.axis_index("tensor") == 0
    return jnp.concatenate(
        [jnp.where(low, array, other), jnp.where(low, other, array)], axis=0
    )


def fetch(table, pieces, target, sems, columns, sem_from=0):
    start, size = columns
    copies = []
    if len(pieces) == 1:
        copies.append(
            pltpu.make_async_copy(pieces[0].at[:, pl.ds(start, size)], target, sems.at[sem_from])
        )
    else:
        rows = target.shape[0] // table.shape[0]
        slot = 0
        for piece in pieces:
            for j in range(piece.shape[0] // rows):
                first = pl.multiple_of(table[slot] * rows, 16)
                copies.append(
                    pltpu.make_async_copy(
                        piece.at[pl.ds(j * rows, rows), pl.ds(start, size)],
                        target.at[pl.ds(first, rows), :],
                        sems.at[sem_from + slot],
                    )
                )
                slot += 1
    for copy in copies:
        copy.start()
    return copies


def put(table, source, pieces, sems, columns, sem_from=0):
    start, size = columns
    copies = []
    if len(pieces) == 1:
        copies.append(
            pltpu.make_async_copy(source, pieces[0].at[:, pl.ds(start, size)], sems.at[sem_from])
        )
    else:
        rows = source.shape[0] // table.shape[0]
        slot = 0
        for piece in pieces:
            for j in range(piece.shape[0] // rows):
                first = pl.multiple_of(table[slot] * rows, 16)
                copies.append(
                    pltpu.make_async_copy(
                        source.at[pl.ds(first, rows), :],
                        piece.at[pl.ds(j * rows, rows), pl.ds(start, size)],
                        sems.at[sem_from + slot],
                    )
                )
                slot += 1
    for copy in copies:
        copy.start()
    return copies


def finish(copies):
    for copy in copies:
        copy.wait()


def norm_parts(stream):
    center = stream - jnp.mean(stream, axis=-1, keepdims=True)
    spread = jnp.mean(center * center, axis=-1, keepdims=True)
    scale = lax.rsqrt(spread + EPSILON)
    return center * scale, scale


def norm_back(grad, normal, scale, gain):
    inner = grad * gain
    return scale * (
        inner
        - jnp.mean(inner, axis=-1, keepdims=True)
        - normal * jnp.mean(inner * normal, axis=-1, keepdims=True)
    )


def turn(pair, cosine, sine):
    lane = lax.broadcasted_iota(jnp.int32, pair.shape, 1)
    low_half = lane % HEAD_DIM < HEAD_DIM // 2
    partner = jnp.where(
        low_half,
        pltpu.roll(pair, LANES - HEAD_DIM // 2, 1),
        pltpu.roll(pair, HEAD_DIM // 2, 1),
    )
    return pair * cosine + partner * sine


def stack_heads(pair):
    lane = lax.broadcasted_iota(jnp.int32, pair.shape, 1)
    zero = jnp.zeros_like(pair)
    return jnp.concatenate(
        [jnp.where(lane < HEAD_DIM, pair, zero), jnp.where(lane < HEAD_DIM, zero, pair)], axis=0
    )


def merge_heads(stacked):
    rows = stacked.shape[0] // 2
    lane = lax.broadcasted_iota(jnp.int32, (rows, stacked.shape[1]), 1)
    return jnp.where(lane < HEAD_DIM, stacked[:rows], stacked[rows:])


def softmax_low(scores):
    raised = jnp.exp(scores - jnp.max(scores, axis=-1, keepdims=True))
    return (raised * (1.0 / jnp.sum(raised, axis=-1, keepdims=True))).astype(bf16)


def pairs_of(width):
    return [(pair, slice(pair * LANES, (pair + 1) * LANES)) for pair in range(width // LANES)]


SCALE = HEAD_DIM ** (-0.5)


def self_forward(count, table, x_ref, cos_ref, sin_ref, *refs):
    pieces, refs = refs[:count], refs[count:]
    part, h_out, q_out, k_out, v_out, p_out, o_out, norms_out, weights, sems = refs
    width = q_out.shape[1]
    copies = fetch(table, pieces, weights.buffer, sems, (0, weights.shape[1]))
    normal, _ = norm_parts(wide(x_ref[...]))
    finish(copies)
    send(weights)
    rows = wide(weights[:, :LANES]).T[:8]
    norms_out[...] = rows
    hidden = (normal * rows[0:1] + rows[1:2]).astype(bf16)
    h_out[...] = hidden
    send(h_out)
    mixed = mm(hidden, weights[:, LANES : LANES + 3 * width])
    cosine, sine = cos_ref[...], sin_ref[...]
    half = hidden.shape[0] // 2
    for pair, lanes in pairs_of(width):
        queries = turn(mixed[:, lanes], cosine, sine).astype(bf16)
        keys = turn(mixed[:, width + pair * LANES : width + (pair + 1) * LANES], cosine, sine).astype(bf16)
        values = mixed[:, 2 * width + pair * LANES : 2 * width + (pair + 1) * LANES].astype(bf16)
        q_out[:, lanes] = queries
        k_out[:, lanes] = keys
        v_out[:, lanes] = values
        for part_of in range(2):
            rows = slice(part_of * half, (part_of + 1) * half)
            seen = (part_of + 1) * half
            scores = mm_nt(stack_heads(queries[rows]), keys[:seen]) * SCALE
            query_pos = lax.broadcasted_iota(jnp.int32, scores.shape, 0) % half + part_of * half
            allowed = query_pos >= lax.broadcasted_iota(jnp.int32, scores.shape, 1)
            attend = softmax_low(jnp.where(allowed, scores, NEG_FILL))
            p_out[pair, 2 * part_of * half : 2 * (part_of + 1) * half, :seen] = attend
            o_out[rows, lanes] = merge_heads(mm(attend, values[:seen])).astype(bf16)
    send(q_out, k_out, v_out, p_out, o_out)
    part[...] = mm_nt(o_out[...], weights[:, LANES + 3 * width :]).astype(bf16)


def pool_forward(count, table, pool_ref, *refs):
    pieces, refs = refs[:count], refs[count:]
    k_out, v_out, weights, sems = refs
    width = k_out.shape[1]
    finish(fetch(table, pieces, weights.buffer, sems, (2 * width, 2 * width)))
    send(weights)
    mixed = mm(pool_ref[...], weights[...])
    k_out[...] = mixed[:, :width].astype(bf16)
    v_out[...] = mixed[:, width:].astype(bf16)


def chosen_rows(chosen, block, ref, lanes):
    return jnp.concatenate(
        [
            ref[pl.ds(pl.multiple_of(chosen[NBRS * block + j] * NBR_LEN, NBR_LEN), NBR_LEN), lanes]
            for j in range(NBRS)
        ],
        axis=0,
    )


def cross_forward(count, table, chosen, x_ref, own_ref, got_ref, norms, k_ref, v_ref, *refs):
    pieces, refs = refs[:count], refs[count:]
    part, x_out, h_out, q_out, p_out, o_out, both_w, sems = refs
    width = q_out.shape[1]
    copies = fetch(table, pieces, both_w.buffer, sems, (0, 2 * width))
    stream = wide(x_ref[...]) + (wide(own_ref[...]) + wide(got_ref[...]))
    x_out[...] = stream
    send(x_out)
    normal, _ = norm_parts(stream)
    hidden = (normal * norms[2:3] + norms[3:4]).astype(bf16)
    h_out[...] = hidden
    send(h_out)
    finish(copies)
    send(both_w)
    queries = mm(hidden, both_w[:, :width]).astype(bf16)
    q_out[...] = queries
    send(q_out)
    pair_count = width // LANES
    for block in range(queries.shape[0] // GROUP):
        rows = slice(block * GROUP, (block + 1) * GROUP)
        for pair, lanes in pairs_of(width):
            keys = chosen_rows(chosen, block, k_ref, lanes)
            values = chosen_rows(chosen, block, v_ref, lanes)
            attend = softmax_low(mm_nt(stack_heads(queries[rows, lanes]), keys) * SCALE)
            p_out[block * pair_count + pair] = attend
            o_out[rows, lanes] = merge_heads(mm(attend, values)).astype(bf16)
    send(p_out, o_out)
    part[...] = mm_nt(o_out[...], both_w[:, width:]).astype(bf16)


def feed_forward(count, grad_count, slices, leading, table, grad_table, side, x_ref, norms, g_ref, one_ref, two_ref, *refs):
    pieces, refs = refs[:count], refs[count:]
    results = refs[:3]
    grads, refs = refs[3 : 3 + grad_count], refs[3 + grad_count :]
    up_w, down_w, up_g, down_g, *full, sems, sems_out = refs
    total = up_w.shape[0] * up_w.shape[2]
    size = total // slices
    block_count = table.shape[0] if count > 1 else 1
    copies = []
    for turn_of in range(slices):
        copies.append(
            fetch(table, pieces, up_w.at[turn_of], sems, (turn_of * size, size), 2 * turn_of * block_count)
            + fetch(table, pieces, down_w.at[turn_of], sems, (total + turn_of * size, size), (2 * turn_of + 1) * block_count)
        )
    if leading:
        stream = wide(x_ref[...]) + (wide(one_ref[...]) + wide(two_ref[...]))
        results[0][...] = stream
        send(results[0])
    else:
        stream = x_ref[...]
    normal, _ = norm_parts(stream)
    hidden = (normal * norms[4:5] + norms[5:6]).astype(bf16)
    grad = g_ref[...]
    hidden_t, grad_t = hidden.T, grad.T
    kept = results[1:] if leading else full
    sent = []
    for turn_of in range(slices):
        finish(copies[turn_of])
        pre = mm(hidden, up_w[turn_of])
        grad_act = mm(grad, down_w[turn_of])
        square = pre * pre
        bend = jnp.tanh(GELU_A * (pre + GELU_B * square * pre))
        gate = 0.5 * (1.0 + bend)
        act = (pre * gate).astype(bf16)
        slope = gate + 0.5 * pre * (1.0 - bend * bend) * (GELU_A * (1.0 + 3.0 * GELU_B * square))
        grad_pre = (grad_act * slope).astype(bf16)
        more, less = mm_nt(act, down_w[turn_of]), mm_nt(grad_pre, up_w[turn_of])
        for keep, add, given in zip(kept, (more, less), (one_ref, two_ref)):
            base = keep[...] if turn_of else None if leading else given[...]
            keep[...] = add if base is None else base + add
        if turn_of == slices - 1:
            if leading:
                send(results[1], results[2])
            else:
                results[2][...] = full[1][...].astype(bf16)
                full[1][...] = full[0][...] + stream
                half = results[0].shape[0]
                results[0][...] = full[1][pl.ds(pl.multiple_of(side[0] * half, half), half), :]
                results[1][...] = full[0][pl.ds(pl.multiple_of((1 - side[0]) * half, half), half), :].astype(bf16)
        up_g[turn_of] = mm(hidden_t, grad_pre).astype(bf16)
        down_g[turn_of] = mm(grad_t, act).astype(bf16)
        sent += put(grad_table, up_g.at[turn_of], grads, sems_out, (turn_of * size, size), 2 * turn_of * block_count)
        sent += put(grad_table, down_g.at[turn_of], grads, sems_out, (total + turn_of * size, size), (2 * turn_of + 1) * block_count)
    finish(sent)


def attention_back(stacked_grad, outputs, attend, keys, values, stacked_queries):
    both = jnp.concatenate([outputs, outputs], axis=0)
    inner = jnp.sum(wide(stacked_grad) * wide(both), axis=-1, keepdims=True)
    grad_scores = (wide(attend) * (mm_nt(stacked_grad, values) - inner)).astype(bf16)
    grad_q = merge_heads(mm(grad_scores, keys)) * SCALE
    grad_k = mm_tn(grad_scores, stacked_queries) * SCALE
    grad_v = mm_tn(attend, stacked_grad)
    return grad_q, grad_k, grad_v


def cross_back(chosen, own_ref, got_ref, norms, x_ref, g_ref, both_w, o_ref, p_ref, v_ref, k_ref, q_ref, *refs):
    dx_out, low_out, dh_out, dq_out, dk_out, dv_out, sums_out, dk_acc, dv_acc = refs
    width = q_ref.shape[1]
    normal, scale = norm_parts(x_ref[...])
    grad = wide(own_ref[...]) + wide(got_ref[...])
    dx = wide(g_ref[...]) + norm_back(grad, normal, scale, norms[4:5])
    dx_out[...] = dx
    send(dx_out)
    sums_out[0:1] = jnp.sum(grad * normal, axis=0, keepdims=True)
    sums_out[1:2] = jnp.sum(grad, axis=0, keepdims=True)
    low = dx.astype(bf16)
    low_out[...] = low
    send(low_out)
    dk_acc[...] = jnp.zeros_like(dk_acc)
    dv_acc[...] = jnp.zeros_like(dv_acc)
    grad_mix = mm(low, both_w[:, width:]).astype(bf16)
    pair_count = width // LANES
    for block in range(low.shape[0] // GROUP):
        rows = slice(block * GROUP, (block + 1) * GROUP)
        for pair, lanes in pairs_of(width):
            keys = chosen_rows(chosen, block, k_ref, lanes)
            values = chosen_rows(chosen, block, v_ref, lanes)
            grad_q, grad_k, grad_v = attention_back(
                stack_heads(grad_mix[rows, lanes]),
                o_ref[rows, lanes],
                p_ref[block * pair_count + pair],
                keys,
                values,
                stack_heads(q_ref[rows, lanes]),
            )
            dq_out[rows, lanes] = grad_q.astype(bf16)
            for j in range(NBRS):
                place = pl.ds(pl.multiple_of(chosen[NBRS * block + j] * NBR_LEN, NBR_LEN), NBR_LEN)
                part = slice(j * NBR_LEN, (j + 1) * NBR_LEN)
                dk_acc[place, lanes] += grad_k[part]
                dv_acc[place, lanes] += grad_v[part]
    dk_out[...] = dk_acc[...].astype(bf16)
    dv_out[...] = dv_acc[...].astype(bf16)
    send(dq_out, dk_out, dv_out)
    dh_out[...] = mm_nt(dq_out[...], both_w[:, :width]).astype(bf16)


def cross_weights(grad_count, table, side, h_ref, dq_ref, pool_ref, dk_ref, dv_ref, low_ref, o_ref, weights, *refs):
    pool_out, pool_other = refs[:2]
    grads, refs = refs[2 : 2 + grad_count], refs[2 + grad_count :]
    made, full, sems_out = refs
    width = dq_ref.shape[1]
    block_count = table.shape[0] if grad_count > 1 else 1
    made[:, :width] = mm_tn(h_ref[...], dq_ref[...]).astype(bf16)
    pool_t = pool_ref[...].T
    made[:, width : 2 * width] = mm(pool_t, dk_ref[...]).astype(bf16)
    made[:, 2 * width : 3 * width] = mm(pool_t, dv_ref[...]).astype(bf16)
    made[:, 3 * width :] = mm_tn(low_ref[...], o_ref[...]).astype(bf16)
    sent = put(table, made, grads, sems_out, (0, 4 * width))
    full[...] = mm_nt(dk_ref[...], weights[:, :width]) + mm_nt(dv_ref[...], weights[:, width:])
    half = pool_out.shape[0]
    pool_out[...] = full[pl.ds(pl.multiple_of(side[0] * half, half), half), :].astype(bf16)
    pool_other[...] = full[pl.ds(pl.multiple_of((1 - side[0]) * half, half), half), :].astype(bf16)
    finish(sent)


def self_back(own_ref, got_ref, norms, x_ref, dx_ref, weights, o_ref, p_ref, v_ref, k_ref, q_ref, cos_ref, sin_ref, *refs):
    dx_out, low_out, dh_out, dq_out, dk_out, dv_out, sums_out = refs
    width = q_ref.shape[1]
    normal, scale = norm_parts(x_ref[...])
    grad = wide(own_ref[...]) + wide(got_ref[...])
    dx = dx_ref[...] + norm_back(grad, normal, scale, norms[2:3])
    dx_out[...] = dx
    send(dx_out)
    sums_out[0:1] = jnp.sum(grad * normal, axis=0, keepdims=True)
    sums_out[1:2] = jnp.sum(grad, axis=0, keepdims=True)
    low = dx.astype(bf16)
    low_out[...] = low
    send(low_out)
    grad_mix = mm(low, weights[:, LANES + 3 * width :]).astype(bf16)
    cosine, sine = cos_ref[...], -sin_ref[...]
    for pair, lanes in pairs_of(width):
        half = grad_mix.shape[0] // 2
        found = []
        for part_of in range(2):
            rows = slice(part_of * half, (part_of + 1) * half)
            seen = (part_of + 1) * half
            found.append(
                attention_back(
                    stack_heads(grad_mix[rows, lanes]),
                    o_ref[rows, lanes],
                    p_ref[pair, 2 * part_of * half : 2 * (part_of + 1) * half, :seen],
                    k_ref[:seen, lanes],
                    v_ref[:seen, lanes],
                    stack_heads(q_ref[rows, lanes]),
                )
            )
        grad_q = jnp.concatenate([found[0][0], found[1][0]], axis=0)
        grad_k, grad_v = (
            jnp.concatenate([found[0][i] + found[1][i][:half], found[1][i][half:]], axis=0) for i in (1, 2)
        )
        dq_out[:, lanes] = turn(grad_q, cosine, sine).astype(bf16)
        dk_out[:, lanes] = turn(grad_k, cosine, sine).astype(bf16)
        dv_out[:, lanes] = grad_v.astype(bf16)
    send(dq_out, dk_out, dv_out)
    dh_out[...] = (
        mm_nt(dq_out[...], weights[:, LANES : LANES + width])
        + mm_nt(dk_out[...], weights[:, LANES + width : LANES + 2 * width])
        + mm_nt(dv_out[...], weights[:, LANES + 2 * width : LANES + 3 * width])
    ).astype(bf16)


def self_weights(grad_count, table, one_ref, two_ref, three_ref, h_ref, dq_ref, dk_ref, dv_ref, low_ref, o_ref, *refs):
    grads, refs = refs[:grad_count], refs[grad_count:]
    made, sems_out = refs
    width = dq_ref.shape[1]
    sums = [one_ref[:2], two_ref[:2], three_ref[:2], jnp.zeros((LANES - NORMS, one_ref.shape[1]), f32)]
    made[:, 4 * width :] = jnp.concatenate(sums, axis=0).T.astype(bf16)
    hidden_t = h_ref[...].T
    for part, grad in enumerate((dq_ref, dk_ref, dv_ref)):
        made[:, part * width : (part + 1) * width] = mm(hidden_t, grad[...]).astype(bf16)
    made[:, 3 * width : 4 * width] = mm_tn(low_ref[...], o_ref[...]).astype(bf16)
    finish(put(table, made, grads, sems_out, (0, 4 * width + LANES)))


def input_back(side, dx_ref, x_ref, norms, own_ref, got_ref, dx_out, sums_out, full):
    normal, scale = norm_parts(wide(x_ref[...]))
    grad = wide(own_ref[...]) + wide(got_ref[...])
    full[...] = dx_ref[...] + norm_back(grad, normal, scale, norms[0:1])
    half = dx_out.shape[0]
    dx_out[...] = full[pl.ds(pl.multiple_of(side[0] * half, half), half), :]
    sums_out[0:1] = jnp.sum(grad * normal, axis=0, keepdims=True)
    sums_out[1:2] = jnp.sum(grad, axis=0, keepdims=True)


SMEM = pl.BlockSpec(memory_space=pltpu.SMEM)
VMEM = pl.BlockSpec(memory_space=pltpu.VMEM)
ANY = pl.BlockSpec(memory_space=pl.ANY)
HBM = pl.BlockSpec(memory_space=pltpu.HBM)


def cost(microseconds):
    return pl.CostEstimate(flops=int(microseconds * 1.1e9), bytes_accessed=0, transcendentals=0)


class Arriving:
    def __init__(self, source, buffer, sem):
        self.copy = pltpu.make_async_copy(source, buffer, sem)
        self.copy.start()
        self.buffer, self.shape, self.waiting = buffer, buffer.shape, True

    def __getitem__(self, index):
        if self.waiting:
            self.copy.wait()
            self.waiting = False
        return self.buffer[index]


class Leaving:
    def __init__(self, buffer, target, sem):
        self.copy = pltpu.make_async_copy(buffer, target, sem)
        self.buffer, self.shape, self.dtype, self.sent = buffer, buffer.shape, buffer.dtype, False

    def __getitem__(self, index):
        return self.buffer[index]

    def __setitem__(self, index, value):
        self.buffer[index] = value

    def send(self):
        if not self.sent:
            self.copy.start()
            self.sent = True


def send(*results):
    for result in results:
        if isinstance(result, Leaving):
            result.send()


def streamed(body, counts, far_in, far_out, *refs):
    scalars, arrays, pieces, outs, grads, own = counts
    parts, start = [], 0
    for size in (scalars, arrays, pieces, outs, grads, own, len(far_in), len(far_out), 2):
        parts.append(list(refs[start : start + size]))
        start += size
    scalars, arrays, pieces, outs, grads, own, in_buffers, out_buffers, (in_sems, out_sems) = parts
    for place, index in enumerate(far_in):
        arrays[index] = Arriving(arrays[index], in_buffers[place], in_sems.at[place])
    for place, index in enumerate(far_out):
        outs[index] = Leaving(out_buffers[place], outs[index], out_sems.at[place])
    body(*scalars, *arrays, *pieces, *outs, *grads, *own)
    for index in far_in:
        if arrays[index].waiting:
            arrays[index].copy.wait()
    for index in far_out:
        outs[index].send()
    for index in far_out:
        outs[index].copy.wait()


COSTS = {"self_forward": 0.65, "pool_forward": 0.7, "cross_forward": 0.7, "feed_forward": 0.6, "cross_back": 0.7, "cross_weights": 0.5, "self_back": 0.6, "self_weights": 0.7, "input_back": 0.7, "adds": 0.8, "add_diagonal": 0.5, "pack_self": 0.7}


def call(body, name, scalars, arrays, pieces, outs, grads, scratch, microseconds, mib=20, gate=(), far=(), pin=()):
    arrays = [pltpu.with_memory_space_constraint(a, pltpu.HBM) if i in pin else a for i, a in enumerate(arrays)]
    if gate:
        arrays = list(tie(arrays, gate))
    shapes = [pltpu.HBM(*out[:2]) if len(out) > 2 else jax.ShapeDtypeStruct(*out) for out in outs]
    shapes += [pltpu.HBM(shape, dtype) for shape, dtype in grads]
    far = list(far)
    far_out = [index for index, out in enumerate(outs) if len(out) > 2]
    scratch = list(scratch)
    if far or far_out:
        counts = (len(scalars), len(arrays), len(pieces), len(outs), len(grads), len(scratch))
        body = functools.partial(streamed, body, counts, far, far_out)
        scratch += [pltpu.VMEM(arrays[index].shape, arrays[index].dtype) for index in far]
        scratch += [pltpu.VMEM(*outs[index][:2]) for index in far_out]
        scratch += [pltpu.SemaphoreType.DMA((max(len(some), 1),)) for some in (far, far_out)]
    return pl.pallas_call(
        body,
        name=name,
        out_shape=shapes,
        in_specs=[SMEM] * len(scalars)
        + [HBM if index in far else VMEM for index in range(len(arrays))]
        + [ANY] * len(pieces),
        out_specs=[HBM if index in far_out else VMEM for index in range(len(outs))] + [HBM] * len(grads),
        scratch_shapes=scratch,
        compiler_params=pltpu.CompilerParams(vmem_limit_bytes=mib * MIB),
        cost_estimate=cost(COSTS['adds' if name.startswith('add_') else name] * microseconds),
    )(*scalars, *arrays, *pieces)


def rope_tables(rows):
    half = HEAD_DIM // 2
    frequency = np.power(np.float32(10000.0), -np.arange(half, dtype=np.float32) / np.float32(half))
    angles = np.arange(rows, dtype=np.float32)[:, None] * frequency[None, :]
    cosine, sine = np.cos(angles), np.sin(angles)
    return (
        jnp.asarray(np.concatenate([cosine] * 4, axis=1), f32),
        jnp.asarray(np.concatenate([-sine, sine] * 2, axis=1), f32),
    )


def dma_sems(count, uses=1):
    blocks = BLOCKS if count > 1 else 1
    return pltpu.SemaphoreType.DMA((blocks * uses,))


def pack(*columns):
    return jnp.concatenate([column.astype(bf16) for column in columns], axis=1)


def pack_kernel(*refs):
    norms, (query, key, value, out_w, packed) = refs[:NORMS], refs[NORMS:]
    rows, width = query.shape
    lines = [norm[...] for norm in norms] + [jnp.zeros((LANES - NORMS, rows), f32)]
    packed[:, :LANES] = jnp.concatenate(lines, axis=0).T.astype(bf16)
    for place, ref in enumerate((query, key, value)):
        packed[:, LANES + place * width : LANES + (place + 1) * width] = ref[...].astype(bf16)
    packed[:, LANES + 3 * width :] = out_w[...].astype(bf16)


def pack_self(norms, query, key, value, out_w, fast):
    if not fast:
        lines = jnp.pad(jnp.stack(norms, axis=1), ((0, 0), (0, LANES - NORMS)))
        return pack(lines, query, key, value, out_w)
    lines = [norm.reshape(1, -1) for norm in norms]
    shape = (query.shape[0], LANES + 4 * query.shape[1])
    return call(pack_kernel, "pack_self", [], lines + [query, key, value, out_w], [], [(shape, bf16)], [], [], 2, mib=60)[0]


def on_device(count, inputs, neighbours, nbr_index, ln1_gain, ln1_bias, ln2_gain, ln2_bias, ln3_gain, ln3_bias,
              w_query, w_key, w_value, c_query, c_key, c_value, w_up, w_out, c_out, w_down, cotangent):
    width, hidden = w_query.shape[1], w_up.shape[1]
    shard_rows = w_query.shape[0]
    model = shard_rows * count
    rows = 2 * inputs.shape[0]
    norms = [ln1_gain, ln1_bias, ln2_gain, ln2_bias, ln3_gain, ln3_bias]

    stream = join_cores(inputs)
    cot = join_cores(cotangent)
    pool = join_cores(neighbours.reshape(-1, neighbours.shape[-1]))
    down_t = w_down.T
    part_hidden = hidden // 2
    cuts = [slice(0, part_hidden), slice(part_hidden, hidden)]
    self_w, cross_w, *ff_w, gate_self, gate_pool, gate_cross = gather_all(
        pack_self(norms, w_query, w_key, w_value, w_out.T, pieces_ok(count, shard_rows)),
        pack(c_query, c_out.T, c_key, c_value),
        pack(w_up[:, cuts[0]], down_t[:, cuts[0]]),
        pack(w_up[:, cuts[1]], down_t[:, cuts[1]]),
        count,
        (stream, cot, pool),
    )
    ff_w = ff_w[::-1]
    side = lax.axis_index("tensor").astype(jnp.int32).reshape(1)
    pieces = len(self_w)
    if pieces > 1:
        tables = jnp.asarray(block_tables(count))
        table, flat_table = (tables[i][lax.axis_index("dp")] for i in range(2))
        grad_rows = [shard_rows * blocks for blocks in (4, 4, 4, 2, 2)]
        flat_rows = [shard_rows * PLANES] * 4
    else:
        table = flat_table = jnp.zeros((1,), jnp.int32)
        grad_rows = flat_rows = [model]
    grad_count = len(grad_rows)

    def bind(body, *extra):
        return functools.partial(body, pieces, *extra)

    pool_rows = pool.shape[0]
    chosen = nbr_index.reshape(-1)
    cosine, sine = rope_tables(rows)
    pairs = width // LANES
    blocks = rows // GROUP
    tall, low = ((rows, model), f32), ((rows, model), bf16)
    slim = ((rows, width), bf16)
    rank8 = ((8, model), f32)
    half_tall, half_low = ((rows // 2, model), f32), ((rows // 2, model), bf16)

    def kept(out):
        return out + ("hbm",)


    part, h_one, queries, keys, values, attend, mixture, norm_rows, self_full = call(
        bind(self_forward), "self_forward", [table], [stream, cosine, sine], self_w,
        [low, kept(low), kept(slim), kept(slim), kept(slim), kept(((pairs, 2 * rows, rows), bf16)), kept(slim), rank8, kept(((model, LANES + 4 * width), bf16))], [],
        [dma_sems(pieces)], 8, mib=60, gate=gate_self, far=[0, 1, 2])
    got = swap_cores(part)
    ckeys, cvalues, cross_full = call(
        bind(pool_forward), "pool_forward", [table], [pool], cross_w,
        [kept(((pool_rows, width), bf16))] * 2 + [kept(((model, 2 * width), bf16))], [],
        [dma_sems(pieces)], 3, mib=60, gate=gate_pool, far=[0])
    part, after_self, h_two, cqueries, cattend, cmixture, cboth_full = call(
        bind(cross_forward), "cross_forward", [table, chosen], [stream, part, got, norm_rows, ckeys, cvalues], cross_w,
        [low, kept(tall), kept(low), kept(slim), kept(((blocks * pairs, 2 * GROUP, NBRS * NBR_LEN), bf16)), kept(slim), kept(((model, 2 * width), bf16))], [],
        [dma_sems(pieces)], 6, mib=60, gate=gate_cross, far=[0, 4, 5])
    got = swap_cores(part)
    slices = 2
    size = part_hidden // slices
    def ff_call(leading, ff_pieces, from_table, to_table, to_rows, arrays, outs, far, pin):
        wide_scratch = [] if leading else [pltpu.VMEM((rows, model), f32)] * 2
        results = call(
            functools.partial(feed_forward, len(ff_pieces), len(to_rows), slices, leading), "feed_forward",
            [from_table, to_table, side], arrays, ff_pieces, outs, [((count_of, 2 * part_hidden), bf16) for count_of in to_rows],
            [pltpu.VMEM((slices, model, size), bf16)] * 4 + wide_scratch + [dma_sems(pieces, 2 * slices)] * 2, 10,
            mib=34, far=far, pin=pin)
        return *results[:3], results[3:]

    after_cross, out, back, last_grads = ff_call(
        True, ff_w[0], flat_table, flat_table, flat_rows, [after_self, norm_rows, cot, part, got],
        [kept(tall)] * 3, [0, 2], [0])
    result, result_other, back, first_grads = ff_call(
        False, ff_w[1], table, table, grad_rows, [after_cross, norm_rows, cot, out, back], [half_tall, half_low, low], [0, 2, 3, 4], [0, 3, 4])
    ff_grads = [last_grads, first_grads]
    grad_part = back
    got = swap_cores(grad_part)
    ff_widths, ff_turned = [part_hidden] * 2, [False, False]
    one = FlatReduction(ff_grads[0], count, ff_widths, ff_turned)
    two = Reduction(ff_grads[1], count, ff_widths, ff_turned)
    one.near()
    two.diagonal()
    two.plane()
    one.far()
    acc = pltpu.VMEM((pool_rows, width), f32)
    grad_cross, low_cross, grad_part, dcq, dck, dcv, sums_three = call(
        cross_back, "cross_back", [chosen],
        [grad_part, got, norm_rows, after_cross, cot, cboth_full, cmixture, cattend, cvalues, ckeys, cqueries], [],
        [kept(tall), kept(low), low, kept(slim), kept(((pool_rows, width), bf16)), kept(((pool_rows, width), bf16)), rank8], [],
        [acc, acc], 8, mib=24, gate=(one.got_across,) if pieces > 1 else (), far=range(3, 11))
    got = swap_cores(grad_part)
    pool_part, pool_other, *cross_grads = call(
        functools.partial(cross_weights, grad_count), "cross_weights", [table, side],
        [h_two, dcq, pool, dck, dcv, low_cross, cmixture, cross_full], [],
        [((pool_rows // 2, model), bf16)] * 2, [((count_of, 4 * width), bf16) for count_of in grad_rows],
        [pltpu.VMEM((model, 4 * width), bf16), pltpu.VMEM((pool_rows, model), f32), dma_sems(pieces)],
        8, mib=24, gate=(one.across,) if pieces > 1 else (), far=range(8))
    grad_self, low_self, grad_part, dq, dk, dv, sums_two = call(
        self_back, "self_back", [],
        [grad_part, got, norm_rows, after_self, grad_cross, self_full, mixture, attend, values, keys, queries, cosine, sine], [],
        [kept(tall), kept(low), low, kept(slim), kept(slim), kept(slim), rank8], [],
        [], 7, mib=20, gate=tuple(two.sides) + (one.across,) if pieces > 1 else (), far=range(3, 13))
    got = swap_cores(grad_part)
    three = Reduction(cross_grads, count, [width] * 4, [False] * 4)
    three.diagonal()
    grad_input, sums_one = call(
        input_back, "input_back", [side], [grad_self, stream, norm_rows, grad_part, got], [], [half_tall, rank8], [],
        [pltpu.VMEM((rows, model), f32)], 2, mib=12, far=[0, 1])
    self_grads = call(
        functools.partial(self_weights, grad_count), "self_weights", [table],
        [sums_one, sums_two, sums_three, h_one, dq, dk, dv, low_self, mixture], [],
        [], [((count_of, 4 * width + LANES), bf16) for count_of in grad_rows],
        [pltpu.VMEM((model, 4 * width + LANES), bf16), dma_sems(pieces)], 4,
        mib=16, gate=(()) if pieces > 1 else (), far=range(3, 9))
    four = Reduction(self_grads, count, [width] * 4 + [8], [False] * 4 + [True])
    one.column((self_grads[-1],))
    one.diagonal()
    sent_one = one.ended
    two.near()
    four.diagonal(())
    one.plane()
    three.plane(sent_one)
    four.plane(two.ended + sent_one)
    two.far((), False)
    three.near()
    four.near((two.got_far,) if pieces > 1 else ())
    three.far()
    four.far(three.ended)
    one.join(two)
    d_cross, d_self = three.outs, four.outs
    if pieces > 1:
        d_up, d_down = one.joined
    else:
        d_up, d_down = (jnp.concatenate([two.outs[i], one.outs[i]], axis=1) for i in range(2))
    grad_pool = wide(pool_part) + wide(swap_cores(pool_other))
    mine = d_self[4]
    return (
        (result + wide(swap_cores(result_other))).astype(bf16),
        grad_input,
        grad_pool.reshape(neighbours.shape),
        mine[0],
        mine[1],
        mine[2],
        mine[3],
        mine[4],
        mine[5],
        *d_self[:3],
        *d_cross[:3],
        d_up,
        d_self[3].T,
        d_cross[3].T,
        d_down.T,
    )


def solution(mesh):
    both = P(("dp", "tensor"), None)
    pool = P(("dp", "tensor"), None, None)
    norm = P("dp")
    tall, flat = P("dp", "tensor"), P("tensor", "dp")
    return jax.shard_map(
        functools.partial(on_device, mesh.shape["dp"]),
        mesh=mesh,
        in_specs=(both, pool, P("dp", None)) + (norm,) * 6 + (tall,) * 7 + (flat,) * 3 + (both,),
        out_specs=(both, both, pool) + (norm,) * 6 + (tall,) * 7 + (flat,) * 3,
        check_vma=False,
    )
```

```python
import functools

import jax
import jax.numpy as jnp
import numpy as np
from jax import lax
from jax.experimental import pallas as pl
from jax.experimental.pallas import tpu as pltpu
from jax.sharding import PartitionSpec as P

HEAD_DIM = 64
GROUP = 64
NBR_LEN = 128
NBRS = 2
LANES = 128
NORMS = 6
NEG_FILL = -1e30
EPSILON = 1e-05
GELU_A = 0.7978845608028654
GELU_B = 0.044715
PLANES = 4
BLOCKS = 16
MIB = 2**20

bf16 = jnp.bfloat16
f32 = jnp.float32


def mm(left, right):
    return jnp.dot(left, right, preferred_element_type=f32)


def mm_nt(left, right):
    return lax.dot_general(left, right, (((1,), (1,)), ((), ())), preferred_element_type=f32)


def mm_tn(left, right):
    return lax.dot_general(left, right, (((0,), (0,)), ((), ())), preferred_element_type=f32)


def wide(array):
    return array.astype(f32)


def grid_perms(count):
    steps = {"x": 1, "y": 2, "near": 4, "far": 8}
    return {name: [(i, i ^ step) for i in range(count)] for name, step in steps.items()}


def block_tables(count):
    orders = [
        [4 * z + plane for plane in range(PLANES) for z in (0, 2, 1, 3)],
        [4 * z + plane for z in (0, 2, 1, 3) for plane in range(PLANES)],
    ]
    return np.array([[[device ^ step for step in order] for device in range(count)] for order in orders], np.int32)


def pieces_ok(count, rows):
    return count == BLOCKS and rows % 16 == 0


def tie(arrays, gate=()):
    arrays = tuple(arrays)
    if len(arrays) + len(gate) < 2:
        return arrays
    return lax.optimization_barrier(arrays + tuple(gate))[: len(arrays)]


def stack(*arrays):
    return jnp.concatenate(arrays, axis=0)


class Rounds:
    def __init__(self, count):
        self.perms = grid_perms(count)

    def go(self, gate, *sends):
        out = []
        for array, name in sends:
            (array,) = tie([array], gate)
            out.append(lax.ppermute(array, "dp", self.perms[name]))
        return out


def gather_all(a, b, c, d, count, early):
    if not pieces_ok(count, a.shape[0]):
        gathered = [(lax.all_gather(shard, "dp", axis=0, tiled=True),) for shard in (a, b, c, d)]
        return gathered + [(), (), ()]
    go = Rounds(count).go
    (a_far,) = go((), (a, "far"))
    d_x, d_y = go((a, early[0]), (d, "x"), (d, "y"))
    a1 = stack(a, a_far)
    r0 = (d_x, d_y)
    r1 = ax1, ay1, a2 = go((), (a1, "x"), (a1, "y"), (a1, "near"))
    (d_d,) = go((), (d_y, "x"))
    (b_far,) = go((a_far, d_y), (b, "far"))
    b1, column = stack(b, b_far), stack(d, d_x, d_y, d_d)
    r2 = bx1, by1, b2, c_far = go(r0 + (ay1,), (b1, "x"), (b1, "y"), (b1, "near"), (c, "far"))
    c1 = stack(c, c_far)
    r3 = ax2, ay2 = go(tuple(r1) + tuple(early), (a2, "x"), (a2, "y"))
    (column_far,) = go(tuple(r1) + (c_far,), (column, "far"))
    r4 = bx2, by2 = go(r2, (b2, "x"), (b2, "y"))
    (column_near,) = go(r4, (column, "near"))
    r5 = ad1, ad2 = go(r3, (ay1, "x"), (ax2, "y"))
    r6 = bd1, bd2, c2 = go(r4, (by1, "x"), (bx2, "y"), (c1, "near"))
    r7 = cx1, cy1 = go(r5, (c1, "x"), (c1, "y"))
    (column_both,) = go(r5, (column_far, "near"))
    r8 = cx2, cy2 = go(r6, (c2, "x"), (c2, "y"))
    cd1, cd2 = go(r7, (cy1, "x"), (cx2, "y"))
    return [
        (a1, a2, ax1, ax2, ay1, ay2, ad1, ad2),
        (b1, b2, bx1, bx2, by1, by2, bd1, bd2),
        (c1, c2, cx1, cx2, cy1, cy2, cd1, cd2),
        (column, column_far, column_near, column_both),
        tuple(r4),
        tuple(r7),
        (column_near,),
    ]


def add_half(own, got):
    return (wide(own) + wide(got)).astype(bf16)


def add_diagonal(x_in, y_in, from_x, from_y, x_out, y_out, x_buf, y_buf, sems):
    half = from_x.shape[0]
    loads = [
        pltpu.make_async_copy(x_in.at[pl.ds(half, half), :], x_buf, sems.at[0]),
        pltpu.make_async_copy(y_in.at[pl.ds(0, half), :], y_buf, sems.at[1]),
    ]
    for load in loads:
        load.start()
    stores = [
        pltpu.make_async_copy(x_buf, x_out.at[pl.ds(half, half), :], sems.at[2]),
        pltpu.make_async_copy(y_buf, y_out.at[pl.ds(0, half), :], sems.at[3]),
    ]
    for load, store, buf, got in zip(loads, stores, (x_buf, y_buf), (from_y, from_x)):
        load.wait()
        buf[...] = add_half(buf[...], got[...])
        store.start()
    finish(stores)


def add_plane(own, got_x, got_y, kept, other):
    half = kept.shape[0]
    total = wide(own[...]) + wide(got_x[...]) + wide(got_y[...])
    kept[...] = total[:half]
    other[...] = total[half:].astype(bf16)


def add_near(kept, got, mine, other):
    rows = mine.shape[0]
    total = kept[...] + wide(got[...])
    mine[...] = total[:rows]
    other[...] = total[rows:].astype(bf16)


def write_outs(turned, total, outs):
    start = 0
    for out, flip in zip(outs, turned):
        if flip:
            columns = max(out.shape[0], LANES)
            out[...] = total[:, start : start + columns].T[: out.shape[0]]
            start += columns
        else:
            out[...] = total[:, start : start + out.shape[1]]
            start += out.shape[1]


def add_far(turned, mine, got, *outs):
    write_outs(turned, mine[...] + wide(got[...]), outs)


class Reduction:
    def __init__(self, pieces, count, widths, turned):
        self.pieces, self.widths, self.turned = pieces, widths, turned
        self.perms = grid_perms(count)
        self.ended = ()
        self.outs = None
        if len(pieces) == 1:
            total = wide(lax.psum_scatter(pieces[0], "dp", scatter_dimension=0, tiled=True))
            self.outs, start = [], 0
            for width, flip in zip(widths, turned):
                part = total[:, start : start + width]
                self.outs.append(part.T if flip else part)
                start += max(width, LANES)

    def out_shapes(self, rows):
        return [((width, rows) if flip else (rows, width), f32) for width, flip in zip(self.widths, self.turned)]

    def move(self, arrays, names, gate):
        out = []
        for array, name in zip(arrays, names):
            (array,) = tie([array], gate)
            out.append(lax.ppermute(array, "dp", self.perms[name]))
        self.ended = tie(out)
        return self.ended

    def diagonal(self, gate=()):
        if self.outs is not None:
            return
        own, x_col, y_col, d_first, d_second = self.pieces
        half, columns = d_first.shape
        from_x, from_y = self.move([d_first, d_second], ["x", "y"], gate)
        buffer = pltpu.VMEM((half, columns), bf16)
        self.sides = pl.pallas_call(
            add_diagonal, name="add_diagonal", out_shape=[pltpu.HBM(x_col.shape, bf16)] * 2,
            in_specs=[HBM, HBM, VMEM, VMEM], out_specs=[HBM, HBM], input_output_aliases={0: 0, 1: 1},
            scratch_shapes=[buffer, buffer, pltpu.SemaphoreType.DMA((4,))],
            compiler_params=pltpu.CompilerParams(vmem_limit_bytes=8 * MIB), cost_estimate=cost(2 * COSTS['add_diagonal']),
        )(x_col, y_col, from_x, from_y)

    def plane(self, gate=()):
        if self.outs is not None:
            return
        half, columns = self.pieces[3].shape
        got_x, got_y = self.move(self.sides, ["x", "y"], gate)
        self.kept, self.other = call(
            add_plane, "add_plane", [], [self.pieces[0], got_x, got_y], [],
            [((half, columns), f32), ((half, columns), bf16)], [], [], 2, mib=10)

    def near(self, gate=()):
        if self.outs is not None:
            return
        half, columns = self.pieces[3].shape
        (got,) = self.move([self.other], ["near"], gate)
        self.mine, self.other = call(
            add_near, "add_near", [], [self.kept, got], [],
            [((half // 2, columns), f32), ((half // 2, columns), bf16)], [], [], 1, mib=8)

    def far(self, gate=(), last=True):
        if self.outs is not None:
            return
        (got,) = self.move([self.other], ["far"], gate)
        self.got_far = got
        if not last:
            return
        shapes = self.out_shapes(self.pieces[3].shape[0] // 2)
        self.outs = call(
            functools.partial(add_far, self.turned), "add_far", [], [self.mine, got], [], shapes, [], [], 1, mib=8)


def add_two(left, right, out):
    out[...] = add_half(left[...], right[...])


def add_column(own, got_near, got_far, mine, x_out, y_out, d_out):
    rows = mine.shape[0]
    total = wide(own[...]) + wide(got_near[...]) + wide(got_far[...])
    mine[...] = total[:rows]
    for place, out in enumerate((x_out, y_out, d_out)):
        out[...] = total[(place + 1) * rows : (place + 2) * rows].astype(bf16)


def add_sides(mine, got_x, got_y, first_mine, first_got, up, down):
    second = mine[...] + wide(got_x[...]) + wide(got_y[...])
    first = first_mine[...] + wide(first_got[...])
    half = up.shape[1] // 2
    for place, out in enumerate((up, down)):
        out[:, :half] = first[:, place * half : (place + 1) * half]
        out[:, half:] = second[:, place * half : (place + 1) * half]


class FlatReduction(Reduction):
    def near(self, gate=()):
        if self.outs is not None:
            return
        own, across, beside, corner = self.pieces
        (got_across,) = self.move([corner], ["near"], gate)
        self.got_across = got_across
        (self.got_own,) = self.move([beside], ["near"], gate)
        (self.across,) = call(add_two, "add_two", [], [across, got_across], [], [(across.shape, bf16)], [], [], 1, mib=8)

    def far(self, gate=()):
        if self.outs is not None:
            return
        (self.got,) = self.move([self.across], ["far"], gate)

    def column(self, gate=()):
        if self.outs is not None:
            return
        own, got = self.pieces[0], self.got
        self.rows = own.shape[0] // PLANES
        block = (self.rows, own.shape[1])
        self.mine, *self.sides = call(
            add_column, "add_column", [], [own, self.got_own, got], [], [(block, f32)] + [(block, bf16)] * 3, [], [], 2, mib=8, gate=gate)

    def diagonal(self, gate=()):
        if self.outs is not None:
            return
        (got,) = self.move([self.sides[2]], ["x"], gate)
        (self.y_side,) = call(add_two, "add_two", [], [self.sides[1], got], [], [(got.shape, bf16)], [], [], 1, mib=8)

    def plane(self, gate=()):
        if self.outs is not None:
            return
        got_x, got_y = self.move([self.sides[0], self.y_side], ["x", "y"], gate)
        self.got_sides = (got_x, got_y)

    def join(self, first):
        if self.outs is not None:
            return
        shape = (self.rows, 2 * self.widths[0])
        self.joined = call(
            add_sides, "add_sides", [], [self.mine, *self.got_sides, first.mine, first.got_far], [], [(shape, f32)] * 2, [], [], 1, mib=8)


def swap_cores(array):
    return lax.ppermute(array, "tensor", [(0, 1), (1, 0)])


def join_cores(array):
    other = swap_cores(array)
    low = lax.axis_index("tensor") == 0
    return jnp.concatenate(
        [jnp.where(low, array, other), jnp.where(low, other, array)], axis=0
    )


def fetch(table, pieces, target, sems, columns, sem_from=0):
    start, size = columns
    copies = []
    if len(pieces) == 1:
        copies.append(
            pltpu.make_async_copy(pieces[0].at[:, pl.ds(start, size)], target, sems.at[sem_from])
        )
    else:
        rows = target.shape[0] // table.shape[0]
        slot = 0
        for piece in pieces:
            for j in range(piece.shape[0] // rows):
                first = pl.multiple_of(table[slot] * rows, 16)
                copies.append(
                    pltpu.make_async_copy(
                        piece.at[pl.ds(j * rows, rows), pl.ds(start, size)],
                        target.at[pl.ds(first, rows), :],
                        sems.at[sem_from + slot],
                    )
                )
                slot += 1
    for copy in copies:
        copy.start()
    return copies


def put(table, source, pieces, sems, columns, sem_from=0):
    start, size = columns
    copies = []
    if len(pieces) == 1:
        copies.append(
            pltpu.make_async_copy(source, pieces[0].at[:, pl.ds(start, size)], sems.at[sem_from])
        )
    else:
        rows = source.shape[0] // table.shape[0]
        slot = 0
        for piece in pieces:
            for j in range(piece.shape[0] // rows):
                first = pl.multiple_of(table[slot] * rows, 16)
                copies.append(
                    pltpu.make_async_copy(
                        source.at[pl.ds(first, rows), :],
                        piece.at[pl.ds(j * rows, rows), pl.ds(start, size)],
                        sems.at[sem_from + slot],
                    )
                )
                slot += 1
    for copy in copies:
        copy.start()
    return copies


def finish(copies):
    for copy in copies:
        copy.wait()


def norm_parts(stream):
    center = stream - jnp.mean(stream, axis=-1, keepdims=True)
    spread = jnp.mean(center * center, axis=-1, keepdims=True)
    scale = lax.rsqrt(spread + EPSILON)
    return center * scale, scale


def norm_back(grad, normal, scale, gain):
    inner = grad * gain
    return scale * (
        inner
        - jnp.mean(inner, axis=-1, keepdims=True)
        - normal * jnp.mean(inner * normal, axis=-1, keepdims=True)
    )


def turn(pair, cosine, sine):
    lane = lax.broadcasted_iota(jnp.int32, pair.shape, 1)
    low_half = lane % HEAD_DIM < HEAD_DIM // 2
    partner = jnp.where(
        low_half,
        pltpu.roll(pair, LANES - HEAD_DIM // 2, 1),
        pltpu.roll(pair, HEAD_DIM // 2, 1),
    )
    return pair * cosine + partner * sine


def stack_heads(pair):
    lane = lax.broadcasted_iota(jnp.int32, pair.shape, 1)
    zero = jnp.zeros_like(pair)
    return jnp.concatenate(
        [jnp.where(lane < HEAD_DIM, pair, zero), jnp.where(lane < HEAD_DIM, zero, pair)], axis=0
    )


def merge_heads(stacked):
    rows = stacked.shape[0] // 2
    lane = lax.broadcasted_iota(jnp.int32, (rows, stacked.shape[1]), 1)
    return jnp.where(lane < HEAD_DIM, stacked[:rows], stacked[rows:])


def softmax_low(scores):
    raised = jnp.exp(scores - jnp.max(scores, axis=-1, keepdims=True))
    return (raised * (1.0 / jnp.sum(raised, axis=-1, keepdims=True))).astype(bf16)


def pairs_of(width):
    return [(pair, slice(pair * LANES, (pair + 1) * LANES)) for pair in range(width // LANES)]


SCALE = HEAD_DIM ** (-0.5)


def self_forward(count, table, x_ref, cos_ref, sin_ref, *refs):
    pieces, refs = refs[:count], refs[count:]
    part, h_out, q_out, k_out, v_out, p_out, o_out, norms_out, weights, sems = refs
    width = q_out.shape[1]
    copies = fetch(table, pieces, weights.buffer, sems, (0, weights.shape[1]))
    normal, _ = norm_parts(wide(x_ref[...]))
    finish(copies)
    send(weights)
    rows = wide(weights[:, :LANES]).T[:8]
    norms_out[...] = rows
    hidden = (normal * rows[0:1] + rows[1:2]).astype(bf16)
    h_out[...] = hidden
    send(h_out)
    mixed = mm(hidden, weights[:, LANES : LANES + 3 * width])
    cosine, sine = cos_ref[...], sin_ref[...]
    half = hidden.shape[0] // 2
    for pair, lanes in pairs_of(width):
        queries = turn(mixed[:, lanes], cosine, sine).astype(bf16)
        keys = turn(mixed[:, width + pair * LANES : width + (pair + 1) * LANES], cosine, sine).astype(bf16)
        values = mixed[:, 2 * width + pair * LANES : 2 * width + (pair + 1) * LANES].astype(bf16)
        q_out[:, lanes] = queries
        k_out[:, lanes] = keys
        v_out[:, lanes] = values
        for part_of in range(2):
            rows = slice(part_of * half, (part_of + 1) * half)
            seen = (part_of + 1) * half
            scores = mm_nt(stack_heads(queries[rows]), keys[:seen]) * SCALE
            query_pos = lax.broadcasted_iota(jnp.int32, scores.shape, 0) % half + part_of * half
            allowed = query_pos >= lax.broadcasted_iota(jnp.int32, scores.shape, 1)
            attend = softmax_low(jnp.where(allowed, scores, NEG_FILL))
            p_out[pair, 2 * part_of * half : 2 * (part_of + 1) * half, :seen] = attend
            o_out[rows, lanes] = merge_heads(mm(attend, values[:seen])).astype(bf16)
    send(q_out, k_out, v_out, p_out, o_out)
    part[...] = mm_nt(o_out[...], weights[:, LANES + 3 * width :]).astype(bf16)


def pool_forward(count, table, pool_ref, *refs):
    pieces, refs = refs[:count], refs[count:]
    k_out, v_out, weights, sems = refs
    width = k_out.shape[1]
    finish(fetch(table, pieces, weights.buffer, sems, (2 * width, 2 * width)))
    send(weights)
    mixed = mm(pool_ref[...], weights[...])
    k_out[...] = mixed[:, :width].astype(bf16)
    v_out[...] = mixed[:, width:].astype(bf16)


def chosen_rows(chosen, block, ref, lanes):
    return jnp.concatenate(
        [
            ref[pl.ds(pl.multiple_of(chosen[NBRS * block + j] * NBR_LEN, NBR_LEN), NBR_LEN), lanes]
            for j in range(NBRS)
        ],
        axis=0,
    )


def cross_forward(count, table, chosen, x_ref, own_ref, got_ref, norms, k_ref, v_ref, *refs):
    pieces, refs = refs[:count], refs[count:]
    part, x_out, h_out, q_out, p_out, o_out, both_w, sems = refs
    width = q_out.shape[1]
    copies = fetch(table, pieces, both_w.buffer, sems, (0, 2 * width))
    stream = wide(x_ref[...]) + (wide(own_ref[...]) + wide(got_ref[...]))
    x_out[...] = stream
    send(x_out)
    normal, _ = norm_parts(stream)
    hidden = (normal * norms[2:3] + norms[3:4]).astype(bf16)
    h_out[...] = hidden
    send(h_out)
    finish(copies)
    send(both_w)
    queries = mm(hidden, both_w[:, :width]).astype(bf16)
    q_out[...] = queries
    send(q_out)
    pair_count = width // LANES
    for block in range(queries.shape[0] // GROUP):
        rows = slice(block * GROUP, (block + 1) * GROUP)
        for pair, lanes in pairs_of(width):
            keys = chosen_rows(chosen, block, k_ref, lanes)
            values = chosen_rows(chosen, block, v_ref, lanes)
            attend = softmax_low(mm_nt(stack_heads(queries[rows, lanes]), keys) * SCALE)
            p_out[block * pair_count + pair] = attend
            o_out[rows, lanes] = merge_heads(mm(attend, values)).astype(bf16)
    send(p_out, o_out)
    part[...] = mm_nt(o_out[...], both_w[:, width:]).astype(bf16)


def feed_forward(count, grad_count, slices, leading, table, grad_table, side, x_ref, norms, g_ref, one_ref, two_ref, *refs):
    pieces, refs = refs[:count], refs[count:]
    results = refs[:3]
    grads, refs = refs[3 : 3 + grad_count], refs[3 + grad_count :]
    up_w, down_w, up_g, down_g, *full, sems, sems_out = refs
    total = up_w.shape[0] * up_w.shape[2]
    size = total // slices
    block_count = table.shape[0] if count > 1 else 1
    copies = []
    for turn_of in range(slices):
        copies.append(
            fetch(table, pieces, up_w.at[turn_of], sems, (turn_of * size, size), 2 * turn_of * block_count)
            + fetch(table, pieces, down_w.at[turn_of], sems, (total + turn_of * size, size), (2 * turn_of + 1) * block_count)
        )
    if leading:
        stream = wide(x_ref[...]) + (wide(one_ref[...]) + wide(two_ref[...]))
        results[0][...] = stream
        send(results[0])
    else:
        stream = x_ref[...]
    normal, _ = norm_parts(stream)
    hidden = (normal * norms[4:5] + norms[5:6]).astype(bf16)
    grad = g_ref[...]
    hidden_t, grad_t = hidden.T, grad.T
    kept = results[1:] if leading else full
    sent = []
    for turn_of in range(slices):
        finish(copies[turn_of])
        pre = mm(hidden, up_w[turn_of])
        grad_act = mm(grad, down_w[turn_of])
        square = pre * pre
        bend = jnp.tanh(GELU_A * (pre + GELU_B * square * pre))
        gate = 0.5 * (1.0 + bend)
        act = (pre * gate).astype(bf16)
        slope = gate + 0.5 * pre * (1.0 - bend * bend) * (GELU_A * (1.0 + 3.0 * GELU_B * square))
        grad_pre = (grad_act * slope).astype(bf16)
        more, less = mm_nt(act, down_w[turn_of]), mm_nt(grad_pre, up_w[turn_of])
        for keep, add, given in zip(kept, (more, less), (one_ref, two_ref)):
            base = keep[...] if turn_of else None if leading else given[...]
            keep[...] = add if base is None else base + add
        if turn_of == slices - 1:
            if leading:
                send(results[1], results[2])
            else:
                results[2][...] = full[1][...].astype(bf16)
                full[1][...] = full[0][...] + stream
                half = results[0].shape[0]
                results[0][...] = full[1][pl.ds(pl.multiple_of(side[0] * half, half), half), :]
                results[1][...] = full[0][pl.ds(pl.multiple_of((1 - side[0]) * half, half), half), :].astype(bf16)
        up_g[turn_of] = mm(hidden_t, grad_pre).astype(bf16)
        down_g[turn_of] = mm(grad_t, act).astype(bf16)
        sent += put(grad_table, up_g.at[turn_of], grads, sems_out, (turn_of * size, size), 2 * turn_of * block_count)
        sent += put(grad_table, down_g.at[turn_of], grads, sems_out, (total + turn_of * size, size), (2 * turn_of + 1) * block_count)
    finish(sent)


def attention_back(stacked_grad, outputs, attend, keys, values, stacked_queries):
    both = jnp.concatenate([outputs, outputs], axis=0)
    inner = jnp.sum(wide(stacked_grad) * wide(both), axis=-1, keepdims=True)
    grad_scores = (wide(attend) * (mm_nt(stacked_grad, values) - inner)).astype(bf16)
    grad_q = merge_heads(mm(grad_scores, keys)) * SCALE
    grad_k = mm_tn(grad_scores, stacked_queries) * SCALE
    grad_v = mm_tn(attend, stacked_grad)
    return grad_q, grad_k, grad_v


def cross_back(chosen, own_ref, got_ref, norms, x_ref, g_ref, both_w, o_ref, p_ref, v_ref, k_ref, q_ref, *refs):
    dx_out, low_out, dh_out, dq_out, dk_out, dv_out, sums_out, dk_acc, dv_acc = refs
    width = q_ref.shape[1]
    normal, scale = norm_parts(x_ref[...])
    grad = wide(own_ref[...]) + wide(got_ref[...])
    dx = wide(g_ref[...]) + norm_back(grad, normal, scale, norms[4:5])
    dx_out[...] = dx
    send(dx_out)
    sums_out[0:1] = jnp.sum(grad * normal, axis=0, keepdims=True)
    sums_out[1:2] = jnp.sum(grad, axis=0, keepdims=True)
    low = dx.astype(bf16)
    low_out[...] = low
    send(low_out)
    dk_acc[...] = jnp.zeros_like(dk_acc)
    dv_acc[...] = jnp.zeros_like(dv_acc)
    grad_mix = mm(low, both_w[:, width:]).astype(bf16)
    pair_count = width // LANES
    for block in range(low.shape[0] // GROUP):
        rows = slice(block * GROUP, (block + 1) * GROUP)
        for pair, lanes in pairs_of(width):
            keys = chosen_rows(chosen, block, k_ref, lanes)
            values = chosen_rows(chosen, block, v_ref, lanes)
            grad_q, grad_k, grad_v = attention_back(
                stack_heads(grad_mix[rows, lanes]),
                o_ref[rows, lanes],
                p_ref[block * pair_count + pair],
                keys,
                values,
                stack_heads(q_ref[rows, lanes]),
            )
            dq_out[rows, lanes] = grad_q.astype(bf16)
            for j in range(NBRS):
                place = pl.ds(pl.multiple_of(chosen[NBRS * block + j] * NBR_LEN, NBR_LEN), NBR_LEN)
                part = slice(j * NBR_LEN, (j + 1) * NBR_LEN)
                dk_acc[place, lanes] += grad_k[part]
                dv_acc[place, lanes] += grad_v[part]
    dk_out[...] = dk_acc[...].astype(bf16)
    dv_out[...] = dv_acc[...].astype(bf16)
    send(dq_out, dk_out, dv_out)
    dh_out[...] = mm_nt(dq_out[...], both_w[:, :width]).astype(bf16)


def cross_weights(grad_count, table, side, h_ref, dq_ref, pool_ref, dk_ref, dv_ref, low_ref, o_ref, weights, *refs):
    pool_out, pool_other = refs[:2]
    grads, refs = refs[2 : 2 + grad_count], refs[2 + grad_count :]
    made, full, sems_out = refs
    width = dq_ref.shape[1]
    block_count = table.shape[0] if grad_count > 1 else 1
    made[:, :width] = mm_tn(h_ref[...], dq_ref[...]).astype(bf16)
    pool_t = pool_ref[...].T
    made[:, width : 2 * width] = mm(pool_t, dk_ref[...]).astype(bf16)
    made[:, 2 * width : 3 * width] = mm(pool_t, dv_ref[...]).astype(bf16)
    made[:, 3 * width :] = mm_tn(low_ref[...], o_ref[...]).astype(bf16)
    sent = put(table, made, grads, sems_out, (0, 4 * width))
    full[...] = mm_nt(dk_ref[...], weights[:, :width]) + mm_nt(dv_ref[...], weights[:, width:])
    half = pool_out.shape[0]
    pool_out[...] = full[pl.ds(pl.multiple_of(side[0] * half, half), half), :].astype(bf16)
    pool_other[...] = full[pl.ds(pl.multiple_of((1 - side[0]) * half, half), half), :].astype(bf16)
    finish(sent)


def self_back(own_ref, got_ref, norms, x_ref, dx_ref, weights, o_ref, p_ref, v_ref, k_ref, q_ref, cos_ref, sin_ref, *refs):
    dx_out, low_out, dh_out, dq_out, dk_out, dv_out, sums_out = refs
    width = q_ref.shape[1]
    normal, scale = norm_parts(x_ref[...])
    grad = wide(own_ref[...]) + wide(got_ref[...])
    dx = dx_ref[...] + norm_back(grad, normal, scale, norms[2:3])
    dx_out[...] = dx
    send(dx_out)
    sums_out[0:1] = jnp.sum(grad * normal, axis=0, keepdims=True)
    sums_out[1:2] = jnp.sum(grad, axis=0, keepdims=True)
    low = dx.astype(bf16)
    low_out[...] = low
    send(low_out)
    grad_mix = mm(low, weights[:, LANES + 3 * width :]).astype(bf16)
    cosine, sine = cos_ref[...], -sin_ref[...]
    for pair, lanes in pairs_of(width):
        half = grad_mix.shape[0] // 2
        found = []
        for part_of in range(2):
            rows = slice(part_of * half, (part_of + 1) * half)
            seen = (part_of + 1) * half
            found.append(
                attention_back(
                    stack_heads(grad_mix[rows, lanes]),
                    o_ref[rows, lanes],
                    p_ref[pair, 2 * part_of * half : 2 * (part_of + 1) * half, :seen],
                    k_ref[:seen, lanes],
                    v_ref[:seen, lanes],
                    stack_heads(q_ref[rows, lanes]),
                )
            )
        grad_q = jnp.concatenate([found[0][0], found[1][0]], axis=0)
        grad_k, grad_v = (
            jnp.concatenate([found[0][i] + found[1][i][:half], found[1][i][half:]], axis=0) for i in (1, 2)
        )
        dq_out[:, lanes] = turn(grad_q, cosine, sine).astype(bf16)
        dk_out[:, lanes] = turn(grad_k, cosine, sine).astype(bf16)
        dv_out[:, lanes] = grad_v.astype(bf16)
    send(dq_out, dk_out, dv_out)
    dh_out[...] = (
        mm_nt(dq_out[...], weights[:, LANES : LANES + width])
        + mm_nt(dk_out[...], weights[:, LANES + width : LANES + 2 * width])
        + mm_nt(dv_out[...], weights[:, LANES + 2 * width : LANES + 3 * width])
    ).astype(bf16)


def self_weights(grad_count, table, one_ref, two_ref, three_ref, h_ref, dq_ref, dk_ref, dv_ref, low_ref, o_ref, *refs):
    grads, refs = refs[:grad_count], refs[grad_count:]
    made, sems_out = refs
    width = dq_ref.shape[1]
    sums = [one_ref[:2], two_ref[:2], three_ref[:2], jnp.zeros((LANES - NORMS, one_ref.shape[1]), f32)]
    made[:, 4 * width :] = jnp.concatenate(sums, axis=0).T.astype(bf16)
    hidden_t = h_ref[...].T
    for part, grad in enumerate((dq_ref, dk_ref, dv_ref)):
        made[:, part * width : (part + 1) * width] = mm(hidden_t, grad[...]).astype(bf16)
    made[:, 3 * width : 4 * width] = mm_tn(low_ref[...], o_ref[...]).astype(bf16)
    finish(put(table, made, grads, sems_out, (0, 4 * width + LANES)))


def input_back(side, dx_ref, x_ref, norms, own_ref, got_ref, dx_out, sums_out, full):
    normal, scale = norm_parts(wide(x_ref[...]))
    grad = wide(own_ref[...]) + wide(got_ref[...])
    full[...] = dx_ref[...] + norm_back(grad, normal, scale, norms[0:1])
    half = dx_out.shape[0]
    dx_out[...] = full[pl.ds(pl.multiple_of(side[0] * half, half), half), :]
    sums_out[0:1] = jnp.sum(grad * normal, axis=0, keepdims=True)
    sums_out[1:2] = jnp.sum(grad, axis=0, keepdims=True)


SMEM = pl.BlockSpec(memory_space=pltpu.SMEM)
VMEM = pl.BlockSpec(memory_space=pltpu.VMEM)
ANY = pl.BlockSpec(memory_space=pl.ANY)
HBM = pl.BlockSpec(memory_space=pltpu.HBM)


def cost(microseconds):
    return pl.CostEstimate(flops=int(microseconds * 1.1e9), bytes_accessed=0, transcendentals=0)


class Arriving:
    def __init__(self, source, buffer, sem):
        self.copy = pltpu.make_async_copy(source, buffer, sem)
        self.copy.start()
        self.buffer, self.shape, self.waiting = buffer, buffer.shape, True

    def __getitem__(self, index):
        if self.waiting:
            self.copy.wait()
            self.waiting = False
        return self.buffer[index]


class Leaving:
    def __init__(self, buffer, target, sem):
        self.copy = pltpu.make_async_copy(buffer, target, sem)
        self.buffer, self.shape, self.dtype, self.sent = buffer, buffer.shape, buffer.dtype, False

    def __getitem__(self, index):
        return self.buffer[index]

    def __setitem__(self, index, value):
        self.buffer[index] = value

    def send(self):
        if not self.sent:
            self.copy.start()
            self.sent = True


def send(*results):
    for result in results:
        if isinstance(result, Leaving):
            result.send()


def streamed(body, counts, far_in, far_out, *refs):
    scalars, arrays, pieces, outs, grads, own = counts
    parts, start = [], 0
    for size in (scalars, arrays, pieces, outs, grads, own, len(far_in), len(far_out), 2):
        parts.append(list(refs[start : start + size]))
        start += size
    scalars, arrays, pieces, outs, grads, own, in_buffers, out_buffers, (in_sems, out_sems) = parts
    for place, index in enumerate(far_in):
        arrays[index] = Arriving(arrays[index], in_buffers[place], in_sems.at[place])
    for place, index in enumerate(far_out):
        outs[index] = Leaving(out_buffers[place], outs[index], out_sems.at[place])
    body(*scalars, *arrays, *pieces, *outs, *grads, *own)
    for index in far_in:
        if arrays[index].waiting:
            arrays[index].copy.wait()
    for index in far_out:
        outs[index].send()
    for index in far_out:
        outs[index].copy.wait()


COSTS = {"self_forward": 0.65, "pool_forward": 0.7, "cross_forward": 0.7, "feed_forward": 0.6, "cross_back": 0.7, "cross_weights": 0.5, "self_back": 0.6, "self_weights": 0.7, "input_back": 0.7, "adds": 0.8, "add_diagonal": 0.5, "pack_self": 0.7}


def call(body, name, scalars, arrays, pieces, outs, grads, scratch, microseconds, mib=20, gate=(), far=(), pin=()):
    arrays = [pltpu.with_memory_space_constraint(a, pltpu.HBM) if i in pin else a for i, a in enumerate(arrays)]
    if gate:
        arrays = list(tie(arrays, gate))
    shapes = [pltpu.HBM(*out[:2]) if len(out) > 2 else jax.ShapeDtypeStruct(*out) for out in outs]
    shapes += [pltpu.HBM(shape, dtype) for shape, dtype in grads]
    far = list(far)
    far_out = [index for index, out in enumerate(outs) if len(out) > 2]
    scratch = list(scratch)
    if far or far_out:
        counts = (len(scalars), len(arrays), len(pieces), len(outs), len(grads), len(scratch))
        body = functools.partial(streamed, body, counts, far, far_out)
        scratch += [pltpu.VMEM(arrays[index].shape, arrays[index].dtype) for index in far]
        scratch += [pltpu.VMEM(*outs[index][:2]) for index in far_out]
        scratch += [pltpu.SemaphoreType.DMA((max(len(some), 1),)) for some in (far, far_out)]
    return pl.pallas_call(
        body,
        name=name,
        out_shape=shapes,
        in_specs=[SMEM] * len(scalars)
        + [HBM if index in far else VMEM for index in range(len(arrays))]
        + [ANY] * len(pieces),
        out_specs=[HBM if index in far_out else VMEM for index in range(len(outs))] + [HBM] * len(grads),
        scratch_shapes=scratch,
        compiler_params=pltpu.CompilerParams(vmem_limit_bytes=mib * MIB),
        cost_estimate=cost(COSTS['adds' if name.startswith('add_') else name] * microseconds),
    )(*scalars, *arrays, *pieces)


def rope_tables(rows):
    half = HEAD_DIM // 2
    frequency = np.power(np.float32(10000.0), -np.arange(half, dtype=np.float32) / np.float32(half))
    angles = np.arange(rows, dtype=np.float32)[:, None] * frequency[None, :]
    cosine, sine = np.cos(angles), np.sin(angles)
    return (
        jnp.asarray(np.concatenate([cosine] * 4, axis=1), f32),
        jnp.asarray(np.concatenate([-sine, sine] * 2, axis=1), f32),
    )


def dma_sems(count, uses=1):
    blocks = BLOCKS if count > 1 else 1
    return pltpu.SemaphoreType.DMA((blocks * uses,))


def pack(*columns):
    return jnp.concatenate([column.astype(bf16) for column in columns], axis=1)


def pack_kernel(*refs):
    norms, (query, key, value, out_w, packed) = refs[:NORMS], refs[NORMS:]
    rows, width = query.shape
    lines = [norm[...] for norm in norms] + [jnp.zeros((LANES - NORMS, rows), f32)]
    packed[:, :LANES] = jnp.concatenate(lines, axis=0).T.astype(bf16)
    for place, ref in enumerate((query, key, value)):
        packed[:, LANES + place * width : LANES + (place + 1) * width] = ref[...].astype(bf16)
    packed[:, LANES + 3 * width :] = out_w[...].astype(bf16)


def pack_self(norms, query, key, value, out_w, fast):
    if not fast:
        lines = jnp.pad(jnp.stack(norms, axis=1), ((0, 0), (0, LANES - NORMS)))
        return pack(lines, query, key, value, out_w)
    lines = [norm.reshape(1, -1) for norm in norms]
    shape = (query.shape[0], LANES + 4 * query.shape[1])
    return call(pack_kernel, "pack_self", [], lines + [query, key, value, out_w], [], [(shape, bf16)], [], [], 2, mib=60)[0]


def on_device(count, inputs, neighbours, nbr_index, ln1_gain, ln1_bias, ln2_gain, ln2_bias, ln3_gain, ln3_bias,
              w_query, w_key, w_value, c_query, c_key, c_value, w_up, w_out, c_out, w_down, cotangent):
    width, hidden = w_query.shape[1], w_up.shape[1]
    shard_rows = w_query.shape[0]
    model = shard_rows * count
    rows = 2 * inputs.shape[0]
    norms = [ln1_gain, ln1_bias, ln2_gain, ln2_bias, ln3_gain, ln3_bias]

    stream = join_cores(inputs)
    cot = join_cores(cotangent)
    pool = join_cores(neighbours.reshape(-1, neighbours.shape[-1]))
    down_t = w_down.T
    part_hidden = hidden // 2
    cuts = [slice(0, part_hidden), slice(part_hidden, hidden)]
    self_w, cross_w, *ff_w, gate_self, gate_pool, gate_cross = gather_all(
        pack_self(norms, w_query, w_key, w_value, w_out.T, pieces_ok(count, shard_rows)),
        pack(c_query, c_out.T, c_key, c_value),
        pack(w_up[:, cuts[0]], down_t[:, cuts[0]]),
        pack(w_up[:, cuts[1]], down_t[:, cuts[1]]),
        count,
        (stream, cot, pool),
    )
    ff_w = ff_w[::-1]
    side = lax.axis_index("tensor").astype(jnp.int32).reshape(1)
    pieces = len(self_w)
    if pieces > 1:
        tables = jnp.asarray(block_tables(count))
        table, flat_table = (tables[i][lax.axis_index("dp")] for i in range(2))
        grad_rows = [shard_rows * blocks for blocks in (4, 4, 4, 2, 2)]
        flat_rows = [shard_rows * PLANES] * 4
    else:
        table = flat_table = jnp.zeros((1,), jnp.int32)
        grad_rows = flat_rows = [model]
    grad_count = len(grad_rows)

    def bind(body, *extra):
        return functools.partial(body, pieces, *extra)

    pool_rows = pool.shape[0]
    chosen = nbr_index.reshape(-1)
    cosine, sine = rope_tables(rows)
    pairs = width // LANES
    blocks = rows // GROUP
    tall, low = ((rows, model), f32), ((rows, model), bf16)
    slim = ((rows, width), bf16)
    rank8 = ((8, model), f32)
    half_tall, half_low = ((rows // 2, model), f32), ((rows // 2, model), bf16)

    def kept(out):
        return out + ("hbm",)


    part, h_one, queries, keys, values, attend, mixture, norm_rows, self_full = call(
        bind(self_forward), "self_forward", [table], [stream, cosine, sine], self_w,
        [low, kept(low), kept(slim), kept(slim), kept(slim), kept(((pairs, 2 * rows, rows), bf16)), kept(slim), rank8, kept(((model, LANES + 4 * width), bf16))], [],
        [dma_sems(pieces)], 8, mib=60, gate=gate_self, far=[0, 1, 2])
    got = swap_cores(part)
    ckeys, cvalues, cross_full = call(
        bind(pool_forward), "pool_forward", [table], [pool], cross_w,
        [kept(((pool_rows, width), bf16))] * 2 + [kept(((model, 2 * width), bf16))], [],
        [dma_sems(pieces)], 3, mib=60, gate=gate_pool, far=[0])
    part, after_self, h_two, cqueries, cattend, cmixture, cboth_full = call(
        bind(cross_forward), "cross_forward", [table, chosen], [stream, part, got, norm_rows, ckeys, cvalues], cross_w,
        [low, kept(tall), kept(low), kept(slim), kept(((blocks * pairs, 2 * GROUP, NBRS * NBR_LEN), bf16)), kept(slim), kept(((model, 2 * width), bf16))], [],
        [dma_sems(pieces)], 6, mib=60, gate=gate_cross, far=[0, 4, 5])
    got = swap_cores(part)
    slices = 2
    size = part_hidden // slices
    def ff_call(leading, ff_pieces, from_table, to_table, to_rows, arrays, outs, far, pin):
        wide_scratch = [] if leading else [pltpu.VMEM((rows, model), f32)] * 2
        results = call(
            functools.partial(feed_forward, len(ff_pieces), len(to_rows), slices, leading), "feed_forward",
            [from_table, to_table, side], arrays, ff_pieces, outs, [((count_of, 2 * part_hidden), bf16) for count_of in to_rows],
            [pltpu.VMEM((slices, model, size), bf16)] * 4 + wide_scratch + [dma_sems(pieces, 2 * slices)] * 2, 10,
            mib=34, far=far, pin=pin)
        return *results[:3], results[3:]

    after_cross, out, back, last_grads = ff_call(
        True, ff_w[0], flat_table, flat_table, flat_rows, [after_self, norm_rows, cot, part, got],
        [kept(tall)] * 3, [0, 2], [0])
    result, result_other, back, first_grads = ff_call(
        False, ff_w[1], table, table, grad_rows, [after_cross, norm_rows, cot, out, back], [half_tall, half_low, low], [0, 2, 3, 4], [0, 3, 4])
    ff_grads = [last_grads, first_grads]
    grad_part = back
    got = swap_cores(grad_part)
    ff_widths, ff_turned = [part_hidden] * 2, [False, False]
    one = FlatReduction(ff_grads[0], count, ff_widths, ff_turned)
    two = Reduction(ff_grads[1], count, ff_widths, ff_turned)
    one.near()
    two.diagonal()
    two.plane()
    one.far()
    acc = pltpu.VMEM((pool_rows, width), f32)
    grad_cross, low_cross, grad_part, dcq, dck, dcv, sums_three = call(
        cross_back, "cross_back", [chosen],
        [grad_part, got, norm_rows, after_cross, cot, cboth_full, cmixture, cattend, cvalues, ckeys, cqueries], [],
        [kept(tall), kept(low), low, kept(slim), kept(((pool_rows, width), bf16)), kept(((pool_rows, width), bf16)), rank8], [],
        [acc, acc], 8, mib=24, gate=(one.got_across,) if pieces > 1 else (), far=range(3, 11))
    got = swap_cores(grad_part)
    pool_part, pool_other, *cross_grads = call(
        functools.partial(cross_weights, grad_count), "cross_weights", [table, side],
        [h_two, dcq, pool, dck, dcv, low_cross, cmixture, cross_full], [],
        [((pool_rows // 2, model), bf16)] * 2, [((count_of, 4 * width), bf16) for count_of in grad_rows],
        [pltpu.VMEM((model, 4 * width), bf16), pltpu.VMEM((pool_rows, model), f32), dma_sems(pieces)],
        8, mib=24, gate=(one.across,) if pieces > 1 else (), far=range(8))
    grad_self, low_self, grad_part, dq, dk, dv, sums_two = call(
        self_back, "self_back", [],
        [grad_part, got, norm_rows, after_self, grad_cross, self_full, mixture, attend, values, keys, queries, cosine, sine], [],
        [kept(tall), kept(low), low, kept(slim), kept(slim), kept(slim), rank8], [],
        [], 7, mib=20, gate=tuple(two.sides) + (one.across,) if pieces > 1 else (), far=range(3, 13))
    got = swap_cores(grad_part)
    three = Reduction(cross_grads, count, [width] * 4, [False] * 4)
    three.diagonal()
    grad_input, sums_one = call(
        input_back, "input_back", [side], [grad_self, stream, norm_rows, grad_part, got], [], [half_tall, rank8], [],
        [pltpu.VMEM((rows, model), f32)], 2, mib=12, far=[0, 1])
    self_grads = call(
        functools.partial(self_weights, grad_count), "self_weights", [table],
        [sums_one, sums_two, sums_three, h_one, dq, dk, dv, low_self, mixture], [],
        [], [((count_of, 4 * width + LANES), bf16) for count_of in grad_rows],
        [pltpu.VMEM((model, 4 * width + LANES), bf16), dma_sems(pieces)], 4,
        mib=16, gate=(()) if pieces > 1 else (), far=range(3, 9))
    four = Reduction(self_grads, count, [width] * 4 + [8], [False] * 4 + [True])
    one.column((self_grads[-1],))
    one.diagonal()
    sent_one = one.ended
    two.near()
    four.diagonal(())
    one.plane()
    three.plane(sent_one)
    four.plane(two.ended + sent_one)
    two.far((), False)
    three.near()
    four.near((two.got_far,) if pieces > 1 else ())
    three.far()
    four.far(three.ended)
    one.join(two)
    d_cross, d_self = three.outs, four.outs
    if pieces > 1:
        d_up, d_down = one.joined
    else:
        d_up, d_down = (jnp.concatenate([two.outs[i], one.outs[i]], axis=1) for i in range(2))
    grad_pool = wide(pool_part) + wide(swap_cores(pool_other))
    mine = d_self[4]
    return (
        (result + wide(swap_cores(result_other))).astype(bf16),
        grad_input,
        grad_pool.reshape(neighbours.shape),
        mine[0],
        mine[1],
        mine[2],
        mine[3],
        mine[4],
        mine[5],
        *d_self[:3],
        *d_cross[:3],
        d_up,
        d_self[3].T,
        d_cross[3].T,
        d_down.T,
    )


def solution(mesh):
    both = P(("dp", "tensor"), None)
    pool = P(("dp", "tensor"), None, None)
    norm = P("dp")
    tall, flat = P("dp", "tensor"), P("tensor", "dp")
    return jax.shard_map(
        functools.partial(on_device, mesh.shape["dp"]),
        mesh=mesh,
        in_specs=(both, pool, P("dp", None)) + (norm,) * 6 + (tall,) * 7 + (flat,) * 3 + (both,),
        out_specs=(both, both, pool) + (norm,) * 6 + (tall,) * 7 + (flat,) * 3,
        check_vma=False,
    )
```
